32 devices in a mesh: rep: 8 (over z, x), shard: 4 (over y, core).
Axes of the slice: x: 2, y: 2, z: 4, core: 2. Of those that a mesh axis runs over, the one named last changes fastest.
Arguments:
- grads: bfloat16 [8, 12, 512, 512], P('rep', 'shard')
- owner_slot: int32 [12], replicated, may hold values from 0 to 11, as said below
- refresh: int32 [1], replicated, may hold values from 0 to 11
- left_stat: float32 [12, 512, 512], P('shard', 'rep'), as said below
- right_stat: float32 [12, 512, 512], P('shard', 'rep'), as said below
- left_root: bfloat16 [12, 512, 512], P('shard', 'rep'), as said below
- right_root: bfloat16 [12, 512, 512], P('shard'), as said below
Outputs:
- left_new: float32 [12, 512, 512], P('shard', 'rep')
- right_new: float32 [12, 512, 512], P('shard', 'rep')
- left_root_new: bfloat16 [12, 512, 512], P('shard', 'rep')
- right_root_new: bfloat16 [12, 512, 512], P('shard')
- direction: bfloat16 [12, 512, 512], P('shard')
The draws below stay inside these ranges and needn't reach their ends.
Inputs may be any that keep to these rules, and one draw needn't show every extreme that they name: A permutation: block b sits at position owner_slot[b] of owner order, which belongs to shard index owner_slot[b] // 3, with owner_slot[b] % 3 == b % 3; the 3 blocks s * 3 to s * 3 + 2 all go to different shard indices. `left_stat`: each block is symmetric positive definite. `right_stat`: each block is symmetric positive definite. `left_root`: each block is symmetric. `right_root`: each block is symmetric.
All inputs are finite; a program needn't handle non-finite values.
Results may differ from the reference program's by a relative error of at most 0.0004.
The reference program's roundings to bfloat16 on the way count: a program that leaves them out, or rounds other values in their place, can miss the bound.
Values may be sent and summed in bfloat16 or wider, within the bound.
A program may use at most 64 MiB of HBM per device.

```python
import jax
import jax.numpy as jnp
from jax import lax

BS = 512
BPS = 3
ITERS = 2
REFRESH = 1
NBLK = 12
N_REP = 8
N_SHARD = 4


def draw_grads(key, part):
    key_each = jax.random.fold_in(jax.random.fold_in(key, 3), 2)
    replica_keys = jax.random.split(key_each, N_REP)

    def one_replica(replica_key):
        return (jax.random.normal(replica_key, (NBLK, BS, BS)) * (1.0 / N_REP ** 0.5)).astype(jnp.bfloat16)
    return lax.map(one_replica, replica_keys)


def draw_owner_slot(key, part):
    key_outer, key_inner, key_shift = jax.random.split(jax.random.fold_in(key, 5), 3)
    outer_perm = jax.random.permutation(key_outer, N_SHARD)
    inner_perm = jax.random.permutation(key_inner, N_SHARD)
    shift_perm = jax.random.permutation(key_shift, N_SHARD)[:BPS]
    owners = outer_perm[(inner_perm[:, None] + shift_perm[None, :]) % N_SHARD]
    slot_ids = owners * BPS + jnp.arange(BPS, dtype=jnp.int32)[None, :]
    return slot_ids.reshape(-1).astype(jnp.int32)


def stat_blocks(key):
    key_base, key_scale = jax.random.split(key)
    factor_keys = jax.random.split(key_base, NBLK)
    identity = jnp.eye(BS, dtype=jnp.float32)

    def one_block(block_key):
        normal_part = jax.random.normal(block_key, (BS, BS))
        return jnp.dot(normal_part, normal_part.T) / BS + 0.5 * identity
    blocks = lax.map(one_block, factor_keys)
    row_scale = jnp.exp(jax.random.uniform(key_scale, (NBLK, BS, 1), minval=0.0, maxval=1.15))
    return blocks * row_scale * jnp.swapaxes(row_scale, 1, 2)


def root_blocks(key):
    key_diag, key_off = jax.random.split(key)
    diagonal_part = jnp.exp(jax.random.uniform(key_diag, (NBLK, BS), minval=-0.69, maxval=0.69))
    off_part = jax.random.normal(key_off, (NBLK, BS, BS)) * (0.7 / BS ** 0.5)
    symmetric = (off_part + jnp.swapaxes(off_part, 1, 2)) * 0.5
    return (symmetric + diagonal_part[:, :, None] * jnp.eye(BS, dtype=jnp.float32)).astype(jnp.bfloat16)


def draw_left_stat(key, part):
    return stat_blocks(jax.random.fold_in(key, 11))


def draw_right_stat(key, part):
    return stat_blocks(jax.random.fold_in(key, 13))


def draw_left_root(key, part):
    return root_blocks(jax.random.fold_in(key, 17))


def draw_right_root(key, part):
    return root_blocks(jax.random.fold_in(key, 19))


def setup_inputs(seed: int = 0) -> dict:
    key_of = jax.random.split(jax.random.key(seed), 8)
    grads = draw_grads(jax.random.fold_in(key_of[7], 71), 0)
    owner_slot = draw_owner_slot(jax.random.fold_in(key_of[7], 71), 0)
    refresh = jax.random.randint(key_of[2], (REFRESH,), 0, NBLK).astype(jnp.int32)
    left_stat = draw_left_stat(jax.random.fold_in(key_of[7], 71), 0)
    right_stat = draw_right_stat(jax.random.fold_in(key_of[7], 71), 0)
    left_root = draw_left_root(jax.random.fold_in(key_of[7], 71), 0)
    right_root = draw_right_root(jax.random.fold_in(key_of[7], 71), 0)
    return dict(grads=grads, owner_slot=owner_slot, refresh=refresh, left_stat=left_stat, right_stat=right_stat, left_root=left_root, right_root=right_root)


decay_rate = 0.95
epsilon_shift = 1e-06

def inverse_root(statistic):
    order = statistic.shape[0]
    identity = jnp.eye(order, dtype=jnp.float32)
    shifted = statistic + epsilon_shift * identity
    norm_scale = 2.5 / jnp.sqrt(jnp.sum(shifted * shifted))
    moment = norm_scale * shifted
    current = identity
    for number in range(ITERS):
        factor = (5.0 * identity - moment) * 0.25
        factor_low = factor.astype(jnp.bfloat16)
        if number == 0:
            current = jnp.sqrt(jnp.sqrt(norm_scale)) * factor
        else:
            current = jnp.dot(current.astype(jnp.bfloat16), factor_low, preferred_element_type=jnp.float32)
        if number + 1 < ITERS:
            square = jnp.dot(factor_low, factor_low, preferred_element_type=jnp.float32).astype(jnp.bfloat16)
            fourth = jnp.dot(square, square, preferred_element_type=jnp.float32).astype(jnp.bfloat16)
            moment = jnp.dot(fourth, moment.astype(jnp.bfloat16), preferred_element_type=jnp.float32)
    return current.astype(jnp.bfloat16)

def add_replica(running, piece):
    return (running + piece.astype(jnp.float32), None)

def reference(grads, owner_slot, refresh, left_stat, right_stat, left_root, right_root):
    summed, unused = lax.scan(add_replica, jnp.zeros((NBLK, BS, BS), jnp.float32), grads)
    gradient = summed.astype(jnp.bfloat16)
    owned_grad = jnp.zeros_like(gradient).at[owner_slot].set(gradient)
    owned_wide = owned_grad.astype(jnp.float32)
    highest = lax.Precision.HIGHEST
    left_new = decay_rate * left_stat + jnp.einsum('bij,bkj->bik', owned_wide, owned_wide, precision=highest) / BS
    right_new = decay_rate * right_stat + jnp.einsum('bji,bjk->bik', owned_wide, owned_wide, precision=highest) / BS
    fresh_slot = owner_slot[refresh[0]]
    fresh_left = inverse_root(left_new[fresh_slot])
    fresh_right = inverse_root(right_new[fresh_slot])
    left_root_new = left_root.at[fresh_slot].set(fresh_left)
    right_root_new = right_root.at[fresh_slot].set(fresh_right)
    half_step = jnp.einsum('bij,bjk->bik', left_root_new.astype(jnp.float32), owned_wide, precision=highest).astype(jnp.bfloat16)
    direction = jnp.einsum('bij,bjk->bik', half_step.astype(jnp.float32), right_root_new.astype(jnp.float32), precision=highest).astype(jnp.bfloat16)
    return (left_new, right_new, left_root_new, right_root_new, direction)
```

```python
import functools

import jax
import jax.numpy as jnp
from jax import lax
from jax.experimental import pallas as pl
from jax.experimental.pallas import tpu as pltpu
from jax.sharding import PartitionSpec as P

ITERS = 2


decay_rate = 0.95
epsilon_shift = 1e-06


def inverse_root(statistic):
    order = statistic.shape[0]
    identity = (
        lax.broadcasted_iota(jnp.int32, (order, order), 0)
        == lax.broadcasted_iota(jnp.int32, (order, order), 1)
    ).astype(jnp.float32)
    shifted = statistic + epsilon_shift * identity
    norm_scale = 2.5 / jnp.sqrt(jnp.sum(shifted * shifted))
    moment = norm_scale * shifted
    current = identity
    for number in range(ITERS):
        factor = (5.0 * identity - moment) * 0.25
        factor_low = factor.astype(jnp.bfloat16)
        if number == 0:
            current = jnp.sqrt(jnp.sqrt(norm_scale)) * factor
        else:
            current = jnp.dot(
                current.astype(jnp.bfloat16), factor_low, preferred_element_type=jnp.float32
            )
        if number + 1 < ITERS:
            square = jnp.dot(factor_low, factor_low, preferred_element_type=jnp.float32).astype(
                jnp.bfloat16
            )
            fourth = jnp.dot(square, square, preferred_element_type=jnp.float32).astype(
                jnp.bfloat16
            )
            moment = jnp.dot(
                fourth, moment.astype(jnp.bfloat16), preferred_element_type=jnp.float32
            )
    return current.astype(jnp.bfloat16)


def both_roots(fresh_whole):
    return (inverse_root(fresh_whole[0]), inverse_root(fresh_whole[1]))


def empty_roots(fresh_whole):
    blank = jnp.zeros(fresh_whole.shape[1:], jnp.bfloat16)
    return (blank, blank)


def body(grads, owner_slot, refresh, left_stat, right_stat, left_root, right_root):
    blocks = grads.shape[1]
    block_order = grads.shape[2]
    rep_count = lax.axis_size("rep")
    shards = lax.axis_size("shard")
    row_count = block_order // rep_count
    rep_index = lax.axis_index("rep")
    shard_index = lax.axis_index("shard")
    partial_value = grads[0].astype(jnp.float32)
    row_share = lax.psum_scatter(partial_value, "rep", scatter_dimension=1, tiled=True)
    row_share = row_share.astype(jnp.bfloat16)
    slot_table = owner_slot.reshape(shards, blocks)
    own_slots = lax.dynamic_index_in_dim(slot_table, shard_index, 0, keepdims=False)
    targets = own_slots // blocks
    selector = (targets[None, :] == jnp.arange(shards, dtype=jnp.int32)[:, None]).astype(
        jnp.bfloat16
    )
    outgoing = jnp.einsum(
        "ok,krc->orc", selector, row_share, preferred_element_type=jnp.float32
    ).astype(jnp.bfloat16)
    incoming = lax.all_to_all(outgoing, "shard", split_axis=0, concat_axis=0, tiled=True)
    wanted = shard_index * blocks + jnp.arange(blocks, dtype=jnp.int32)
    receiver = (jnp.transpose(slot_table) == wanted[:, None]).astype(jnp.bfloat16)
    owned_rows = jnp.einsum(
        "ks,src->krc", receiver, incoming, preferred_element_type=jnp.float32
    ).astype(jnp.bfloat16)
    gathered = lax.all_gather(owned_rows, "rep", axis=1, tiled=True)
    left_new = (
        decay_rate * left_stat
        + jnp.einsum("krc,kjc->krj", owned_rows, gathered, preferred_element_type=jnp.float32)
        / block_order
    )
    column_share = lax.dynamic_slice_in_dim(gathered, rep_index * row_count, row_count, 2)
    right_new = (
        decay_rate * right_stat
        + jnp.einsum("kic,kij->kcj", column_share, gathered, preferred_element_type=jnp.float32)
        / block_order
    )
    fresh_slot = owner_slot[refresh[0]]
    holder = fresh_slot // blocks
    slot_index = fresh_slot % blocks
    owns_fresh = holder == shard_index
    fresh_pair = jnp.stack(
        [
            lax.dynamic_index_in_dim(left_new, slot_index, 0, keepdims=False),
            lax.dynamic_index_in_dim(right_new, slot_index, 0, keepdims=False),
        ]
    )
    fresh_whole = lax.all_gather(fresh_pair, "rep", axis=1, tiled=True)
    fresh_left, fresh_right = lax.cond(owns_fresh, both_roots, empty_roots, fresh_whole)
    fresh_rows = lax.dynamic_slice_in_dim(fresh_left, rep_index * row_count, row_count, 0)
    left_updated = lax.dynamic_update_index_in_dim(left_root, fresh_rows, slot_index, 0)
    left_root_new = jnp.where(owns_fresh, left_updated, left_root)
    right_updated = lax.dynamic_update_index_in_dim(right_root, fresh_right, slot_index, 0)
    right_root_new = jnp.where(owns_fresh, right_updated, right_root)
    half_step = jnp.einsum(
        "kri,kic->krc", left_root_new, gathered, preferred_element_type=jnp.float32
    ).astype(jnp.bfloat16)
    preconditioned = jnp.einsum(
        "kri,kic->krc", half_step, right_root_new, preferred_element_type=jnp.float32
    ).astype(jnp.bfloat16)
    direction = lax.all_gather(preconditioned, "rep", axis=1, tiled=True)
    return (left_new, right_new, left_root_new, right_root_new, direction)


MESH = pl.DeviceIdType.MESH
LINE = 4


def dot(left, right, dims=(1, 0)):
    return lax.dot_general(
        left, right, (((dims[0],), (dims[1],)), ((), ())), preferred_element_type=jnp.float32
    )


def exchange_kernel(
    slots_ref,
    refresh_ref,
    grads_ref,
    left_ref,
    left_stat_ref,
    right_stat_ref,
    right_ref,
    left_new_ref,
    right_new_ref,
    direction_ref,
    fresh_rows_ref,
    fresh_right_ref,
    arrived,
    mine,
    left_stat,
    right_stat,
    right_full,
    left_full,
    grad_full,
    stat_ref,
    quarter_in,
    stat_full,
    across,
    partial_out,
    from_outer,
    from_inner,
    share,
    incoming,
    turned,
    moment,
    factor,
    current,
    square,
    left_out,
    right_out,
    direction_out,
    fresh_rows_out,
    load_sem,
    store_sem,
    across_send,
    across_recv,
    partial_send,
    outer_recv,
    inner_recv,
    swap_send,
    swap_recv,
    part_send,
    part_recv,
    stat_send,
    stat_recv,
    stat_side_send,
    stat_side_recv,
    spread_send,
    spread_recv,
    root_send,
    root_recv,
    root_side_send,
    root_side_recv,
    line_send,
    line_recv,
    side_send,
    side_recv,
):
    blocks, order = mine.shape[0], mine.shape[1]
    rows = order // (2 * LINE)
    group = 2 * rows
    shards = stat_ref.shape[0]
    last = blocks - 1
    me = lax.axis_index("rep")
    shard = lax.axis_index("shard")
    place = me // 2
    side = me % 2
    partner = (place * 2 + (1 - side), shard)
    flip = place // (LINE // 2)
    middle = (place == 1) | (place == 2)
    edge = jnp.logical_not(middle)

    def real(position):
        return position + flip * (LINE - 1 - 2 * position)

    def at(position):
        return (real(position) * 2 + side, shard)

    def span(index):
        return pl.ds(pl.multiple_of(index * rows, rows), rows)

    def pair_span(index):
        return pl.ds(pl.multiple_of(index * group, group), group)

    slot = slots_ref[refresh_ref[0]] % blocks
    keeper = slots_ref[refresh_ref[0]] // blocks
    owns = keeper == shard

    def local(block):
        return (slot + block) % blocks

    loads = [
        pltpu.make_async_copy(left_stat_ref, left_stat, load_sem.at[0]),
        pltpu.make_async_copy(right_stat_ref, right_stat, load_sem.at[1]),
        pltpu.make_async_copy(grads_ref.at[0], arrived, load_sem.at[2]),
        pltpu.make_async_copy(left_ref, left_full.at[:, span(me), :], load_sem.at[3]),
        pltpu.make_async_copy(right_ref, right_full, load_sem.at[4]),
    ]
    for copy in loads:
        copy.start()
    barrier = pltpu.get_barrier_semaphore()
    for step in range(1, LINE):
        pl.semaphore_signal(
            barrier,
            inc=1,
            device_id=((place + step) % LINE * 2 + side, shard),
            device_id_type=MESH,
        )
    pl.semaphore_signal(barrier, inc=1, device_id=partner, device_id_type=MESH)
    for step in range(1, shards):
        pl.semaphore_signal(
            barrier, inc=1, device_id=(me, (shard + step) % shards), device_id_type=MESH
        )
    loads[0].wait()
    loads[1].wait()
    part = rows // shards
    for index in range(shards):
        part_rows = pl.ds(index * part, part)
        stat_ref[index, 0] = left_stat[slot, part_rows, :].astype(jnp.bfloat16)
        stat_ref[index, 1] = right_stat[slot, part_rows, :].astype(jnp.bfloat16)
    loads[2].wait()
    for block in range(blocks):
        mine[block] = arrived[local(block)]
    loads[3].wait()
    pl.semaphore_wait(barrier, LINE - 1 + 1 + shards - 1)

    pending = {"all": [], "edge": [], "middle": []}

    def remote(src, dst, send_sem, recv_sem, device):
        return pltpu.make_async_remote_copy(
            src_ref=src,
            dst_ref=dst,
            send_sem=send_sem,
            recv_sem=recv_sem,
            device_id=device,
            device_id_type=MESH,
        )

    def send(kind, make):
        make().start()
        pending[kind].append(make)

    def arrive(dst, recv_sem):
        remote(dst, dst, recv_sem, recv_sem, partner).wait_recv()

    def both(on_edge, on_middle):
        pl.when(edge)(on_edge)
        pl.when(middle)(on_middle)

    def across_copy(block, target):
        return remote(
            mine.at[block, span(target * 2 + (1 - side)), :],
            across.at[block, target],
            across_send.at[block, target],
            across_recv.at[block, target],
            partner,
        )

    def send_across(kind, block, positions):
        for position in positions:
            send(kind, lambda p=position: across_copy(block, real(p)))

    def pair_sum(block, position):
        target = real(position)
        arrive(across.at[block, target], across_recv.at[block, target])
        own = mine[block, span(target * 2 + side), :].astype(jnp.float32)
        return own + across[block, target].astype(jnp.float32)

    def wait_outer(block, number):
        arrive(from_outer.at[block, number], outer_recv.at[block, number])
        return from_outer[block, number]

    def wait_inner(block, number):
        arrive(from_inner.at[block, number], inner_recv.at[block, number])
        return from_inner[block, number]

    def edge_far(block, position):
        number = position - 1
        partial_out[block, number] = pair_sum(block, position)
        send(
            "edge",
            lambda: remote(
                partial_out.at[block, number],
                from_outer.at[block, number],
                partial_send.at[block, number],
                outer_recv.at[block, number],
                at(1),
            ),
        )

    def middle_far(block, position):
        number = {3: 0, 2: 1, 0: 2}[position]
        if position == 0:
            earlier = wait_inner(block, 0)
            goal, landing = 0, 0
        else:
            earlier = wait_outer(block, position - 1)
            goal, landing = 2, number
        partial_out[block, number] = pair_sum(block, position) + earlier
        send(
            "middle",
            lambda: remote(
                partial_out.at[block, number],
                from_inner.at[block, landing],
                partial_send.at[block, number],
                inner_recv.at[block, landing],
                at(goal),
            ),
        )

    def swap(kind, block, total):
        share[block] = total.astype(jnp.bfloat16)
        for step in range(1, shards):
            send(
                kind,
                lambda step=step: remote(
                    share.at[block],
                    incoming.at[block, shard],
                    swap_send.at[block, step],
                    swap_recv.at[block, step],
                    (me, (shard + step) % shards),
                ),
            )
        incoming[block, shard] = share[block]

    def edge_own(block):
        swap("edge", block, pair_sum(block, 0) + wait_inner(block, 0))

    def middle_own(block):
        total = pair_sum(block, 1) + wait_inner(block, 1)
        swap("middle", block, total + wait_outer(block, 0))

    def side_copy(block, source):
        where = grad_full.at[block, span(source * 2 + side), :]
        return remote(
            where, where, side_send.at[block, source], side_recv.at[block, source], partner
        )

    def wait_side(block, source):
        arrive(
            grad_full.at[block, span(source * 2 + (1 - side)), :], side_recv.at[block, source]
        )

    def line_rows(block, source):
        if block < last:
            return grad_full.at[block, pair_span(source), :]
        return grad_full.at[block, span(source * 2 + side), :]

    def line_copy(block, source, way, goal):
        where = line_rows(block, source)
        return remote(
            where,
            where,
            line_send.at[block, source, way],
            line_recv.at[block, source],
            at(goal),
        )

    def take(kind, block):
        for step in range(1, shards):
            origin = (shard + shards - step) % shards
            arrive(incoming.at[block, origin], swap_recv.at[block, step])
        value = incoming[block, 0]
        wanted = shard * blocks + local(block)
        for origin in range(1, shards):
            held = slots_ref[origin * blocks + local(block)] == wanted
            value = jnp.where(held, incoming[block, origin], value)
        grad_full[block, span(me), :] = value
        if block == last:
            line_own(kind, block)
        send(kind, lambda: side_copy(block, place))

    def line_own(kind, block):
        if kind == "edge":
            send(kind, lambda: line_copy(block, real(0), 0, 1))
        else:
            send(kind, lambda: line_copy(block, real(1), 0, 0))
            send(kind, lambda: line_copy(block, real(1), 1, 2))

    def line_begin(kind, block):
        wait_side(block, place)
        line_own(kind, block)

    def line_next(kind, block, position):
        source = real(position)
        arrive(line_rows(block, source), line_recv.at[block, source])
        if kind == "middle":
            goal = 2 if position == 0 else 0
            send(kind, lambda: line_copy(block, real(position), 0, goal))
        if block == last:
            send(kind, lambda: side_copy(block, real(position)))

    pieces = {
        "edge": ((1, 1, 3), (2, 2, 2), (3, 3, 1)),
        "middle": ((0, 0, 1), (0, 3, 1), (2, 2, 2), (2, 0, 1), (3, 3, 1)),
    }

    def columns(first, count):
        return pl.ds(
            pl.multiple_of((first + flip * (LINE - 2 * first - count)) * group, group),
            count * group,
        )

    def root_piece(piece, which):
        position, first, count = piece
        return left_full.at[:, span(real(position) * 2 + which), columns(first, count)]

    def send_root(kind, number, piece, goal, landing):
        send(
            kind,
            lambda: remote(
                root_piece(piece, side),
                root_piece(piece, side),
                root_send.at[number],
                root_recv.at[landing],
                at(goal),
            ),
        )

    def wait_root(kind, number):
        arrive(root_piece(pieces[kind][number], side), root_recv.at[number])

    def edge_roots():
        send_root("edge", 0, (0, 0, 1), 1, 0)
        send_root("edge", 1, (0, 3, 1), 1, 1)

    def middle_roots():
        send_root("middle", 0, (1, 0, 2), 2, 2)
        send_root("middle", 1, (1, 1, 3), 0, 0)
        send_root("middle", 2, (1, 3, 1), 2, 3)

    def middle_roots_next():
        wait_root("middle", 0)
        send_root("middle", 3, (0, 0, 1), 2, 4)
        wait_root("middle", 2)
        send_root("middle", 4, (2, 2, 2), 0, 1)
        wait_root("middle", 4)
        send_root("middle", 5, (3, 3, 1), 0, 2)
        wait_root("middle", 1)
        wait_root("middle", 3)

    def edge_roots_next():
        for number in range(3):
            wait_root("edge", number)

    def root_side(kind, number):
        def make():
            if number == 0:
                where = left_full.at[:, span(me), :]
            else:
                where = root_piece(pieces[kind][number - 1], side)
            return remote(
                where, where, root_side_send.at[number], root_side_recv.at[number], partner
            )

        return make

    def wait_root_side(kind):
        arrive(left_full.at[:, span(place * 2 + 1 - side), :], root_side_recv.at[0])
        for number, piece in enumerate(pieces[kind]):
            arrive(root_piece(piece, 1 - side), root_side_recv.at[number + 1])

    def mirror(kind):
        tiles = [(1, 2), (1, 3), (2, 3)]
        if kind == "edge":
            tiles += [(0, 1), (0, 2), (0, 3)]
        else:
            tiles += [(1, 0), (2, 0), (0, 3)]
        for block in range(blocks):
            for row, column in tiles:
                value = left_full[block, pair_span(real(row)), columns(column, 1)]
                left_full[block, pair_span(real(column)), columns(row, 1)] = value.T

    def to_shards(step):
        peer = (shard + step) % shards
        return remote(
            stat_ref.at[peer],
            quarter_in.at[shard],
            part_send.at[step],
            part_recv.at[step],
            (me, peer),
        )

    def stat_rows(source, which, owner):
        return stat_full.at[:, source * 2 + which, owner]

    def send_quarters():
        for step in range(1, shards):
            origin = (shard + shards - step) % shards
            arrive(quarter_in.at[origin], part_recv.at[step])
        stat_full[:, me, shard] = quarter_in[keeper]
        for step in range(1, LINE):
            send(
                "all",
                lambda step=step: remote(
                    stat_rows(place, side, shard),
                    stat_rows(place, side, shard),
                    stat_send.at[step],
                    stat_recv.at[step],
                    ((place + step) % LINE * 2 + side, shard),
                ),
            )

    def stat_side(source):
        where = stat_rows(source, side, shard)
        return remote(
            where, where, stat_side_send.at[source], stat_side_recv.at[source], partner
        )

    def forward_quarters():
        send("all", lambda: stat_side(place))
        for step in range(1, LINE):
            source = (place + LINE - step) % LINE
            arrive(stat_rows(source, side, shard), stat_recv.at[step])
            send("all", lambda source=source: stat_side(source))

    other_row = (shard + 2) % shards
    other_core = shard + 1 - 2 * (shard % 2)

    def spread(number, owner, goal):
        where = stat_full.at[:, :, owner]
        return remote(
            where, where, spread_send.at[number], spread_recv.at[number], (me, goal)
        )

    def spread_quarters():
        for source in range(LINE):
            arrive(stat_rows(source, 1 - side, shard), stat_side_recv.at[source])
        send("all", lambda: spread(0, shard, other_row))
        send("all", lambda: spread(1, shard, other_core))

    def spread_next():
        arrive(stat_full.at[:, :, other_row], spread_recv.at[0])
        send("all", lambda: spread(2, other_row, other_core))

    def spread_end():
        arrive(stat_full.at[:, :, other_core], spread_recv.at[1])
        arrive(
            stat_full.at[:, :, (other_core + 2) % shards], spread_recv.at[2]
        )

    tile = pair_span(place)

    def new_statistics(block):
        grad = grad_full[block]
        own = grad_full[block, span(me), :]
        left_out[block] = decay_rate * left_stat[local(block)] + dot(own, grad, (1, 1)) / order
        turned_rows = grad_full[block, :, tile].T
        own_turned = jnp.where(side == 0, turned_rows[:rows], turned_rows[rows:])
        right_out[block] = decay_rate * right_stat[local(block)] + dot(own_turned, grad) / order
        stores.append((left_out.at[block], left_new_ref.at[block], 0, block))
        stores.append((right_out.at[block], right_new_ref.at[block], 1, block))
        for entry in stores[-2:]:
            store(*entry).start()

    stores = []

    def store(source, target, kind, block):
        return pltpu.make_async_copy(source, target, store_sem.at[kind, block])

    def renew_begin(which):
        identity = (
            lax.broadcasted_iota(jnp.int32, (order, order), 0)
            == lax.broadcasted_iota(jnp.int32, (order, order), 1)
        ).astype(jnp.float32)
        grad = grad_full[0]
        if which == 0:
            turned[...] = grad.T
            product = dot(grad, turned[...])
        else:
            product = dot(turned[...], grad)
        old = stat_full[which].reshape(order, order).astype(jnp.float32)
        shifted = decay_rate * old + product / order + epsilon_shift * identity
        scale = 2.5 / jnp.sqrt(jnp.sum(shifted * shifted))
        start = scale * shifted
        moment[which] = start.astype(jnp.bfloat16)
        step = (5.0 * identity - start) * 0.25
        factor[which] = step.astype(jnp.bfloat16)
        current[which] = (jnp.sqrt(jnp.sqrt(scale)) * step).astype(jnp.bfloat16)

    def renew_square():
        for which in range(2):
            square[which] = dot(factor[which], factor[which]).astype(jnp.bfloat16)

    def renew_fourth():
        for which in range(2):
            factor[which] = dot(square[which], square[which]).astype(jnp.bfloat16)

    def renew_factor():
        identity = (
            lax.broadcasted_iota(jnp.int32, (order, order), 0)
            == lax.broadcasted_iota(jnp.int32, (order, order), 1)
        ).astype(jnp.float32)
        for which in range(2):
            value = dot(factor[which], moment[which])
            square[which] = ((5.0 * identity - value) * 0.25).astype(jnp.bfloat16)

    def renew_end():
        for which in range(2):
            moment[which] = dot(current[which], square[which]).astype(jnp.bfloat16)
        fresh_rows_out[...] = moment[0, span(me), :]
        stores.append((fresh_rows_out, fresh_rows_ref, 2, 0))
        stores.append((moment.at[1], fresh_right_ref, 2, 1))
        for entry in stores[-2:]:
            store(*entry).start()

    def direct(block):
        root = left_full[local(block)]
        other = right_full[local(block)]
        if block == 0:
            root = jnp.where(owns, moment[0], root)
            other = jnp.where(owns, moment[1], other)
        half = dot(root, grad_full[block]).astype(jnp.bfloat16)
        direction_out[block] = dot(half, other).astype(jnp.bfloat16)
        stores.append((direction_out.at[block], direction_ref.at[block], 3, block))
        store(*stores[-1]).start()

    for step in range(1, shards):
        send("all", lambda step=step: to_shards(step))
    quarter_in[shard] = stat_ref[shard]

    def edge_start():
        for block in range(blocks):
            send_across("edge", block, (3, 2, 1, 0))
        edge_roots()

    def middle_start():
        for block in range(blocks):
            send_across("middle", block, (3, 2, 0, 1))
        middle_roots()

    both(edge_start, middle_start)
    send_quarters()

    def edge_first():
        for position in (3, 2, 1):
            edge_far(0, position)
        edge_roots_next()

    both(edge_first, middle_roots_next)
    forward_quarters()

    def edge_second():
        for position in (3, 2, 1):
            edge_far(1, position)
        edge_own(0)
        take("edge", 0)
        line_begin("edge", 0)
        for position in (3, 2, 1):
            edge_far(2, position)
        for number in range(2):
            send("edge", root_side("edge", number))

    def middle_second():
        middle_far(0, 3)
        middle_far(0, 2)
        middle_far(0, 0)
        middle_own(0)
        middle_far(1, 3)
        take("middle", 0)
        middle_far(1, 2)
        line_begin("middle", 0)
        middle_far(1, 0)
        for number in range(3):
            send("middle", root_side("middle", number))

    both(edge_second, middle_second)
    spread_quarters()

    def edge_third():
        edge_own(1)
        line_next("edge", 0, 1)
        line_next("edge", 0, 2)
        take("edge", 1)
        for number in range(2, 4):
            send("edge", root_side("edge", number))
        line_next("edge", 0, 3)

    def middle_third():
        middle_own(1)
        line_next("middle", 0, 2)
        line_next("middle", 0, 0)
        middle_far(2, 3)
        line_next("middle", 0, 3)
        take("middle", 1)
        for number in range(3, 6):
            send("middle", root_side("middle", number))
        middle_far(2, 2)

    both(edge_third, middle_third)
    spread_next()

    def edge_fourth():
        line_begin("edge", 1)

    def middle_fourth():
        line_begin("middle", 1)
        middle_far(2, 0)

    both(edge_fourth, middle_fourth)
    spread_end()
    renew_begin(0)

    def edge_fifth():
        edge_own(2)

    def middle_fifth():
        line_next("middle", 1, 2)
        line_next("middle", 1, 0)
        middle_own(2)

    both(edge_fifth, middle_fifth)
    renew_begin(1)

    def edge_sixth():
        take("edge", 2)

    def middle_sixth():
        line_next("middle", 1, 3)
        take("middle", 2)

    both(edge_sixth, middle_sixth)
    renew_square()

    def edge_seventh():
        line_next("edge", 2, 1)

    def middle_seventh():
        line_next("middle", 2, 2)
        line_next("middle", 2, 0)

    both(edge_seventh, middle_seventh)
    renew_fourth()

    def edge_eighth():
        line_next("edge", 2, 2)

    def middle_eighth():
        line_next("middle", 2, 3)

    both(edge_eighth, middle_eighth)
    renew_factor()

    def edge_ninth():
        line_next("edge", 2, 3)
        for position in (1, 2, 3):
            line_next("edge", 1, position)
        wait_root_side("edge")
        mirror("edge")

    def middle_ninth():
        wait_root_side("middle")
        mirror("middle")

    both(edge_ninth, middle_ninth)
    renew_end()
    loads[4].wait()
    new_statistics(0)
    direct(0)
    new_statistics(1)
    direct(1)
    for source in range(LINE):
        wait_side(last, source)
    direct(last)
    new_statistics(last)

    def finish(kind):
        for make in pending[kind]:
            make().wait_send()

    both(lambda: finish("edge"), lambda: finish("middle"))
    finish("all")
    for entry in stores:
        store(*entry).wait()


def exchange(owner_slot, refresh, grads, left_root, left_stat, right_stat, right_root, shards):
    blocks, order = grads.shape[1], grads.shape[2]
    reps = 2 * LINE
    rows = order // reps
    part = rows // shards
    low = jnp.bfloat16
    wide = jnp.float32
    smem = pl.BlockSpec(memory_space=pltpu.SMEM)
    hbm = pl.BlockSpec(memory_space=pl.ANY)
    dma = pltpu.SemaphoreType.DMA
    return pl.pallas_call(
        exchange_kernel,
        out_shape=(
            jax.ShapeDtypeStruct((blocks, rows, order), wide),
            jax.ShapeDtypeStruct((blocks, rows, order), wide),
            jax.ShapeDtypeStruct((blocks, order, order), low),
            jax.ShapeDtypeStruct((rows, order), low),
            jax.ShapeDtypeStruct((order, order), low),
        ),
        in_specs=[smem, smem] + [hbm] * 5,
        out_specs=(hbm,) * 5,
        scratch_shapes=[
            pltpu.VMEM((blocks, order, order), low),
            pltpu.VMEM((blocks, order, order), low),
            pltpu.VMEM((blocks, rows, order), wide),
            pltpu.VMEM((blocks, rows, order), wide),
            pltpu.VMEM((blocks, order, order), low),
            pltpu.VMEM((blocks, order, order), low),
            pltpu.VMEM((blocks, order, order), low),
            pltpu.VMEM((shards, 2, part, order), low),
            pltpu.VMEM((shards, 2, part, order), low),
            pltpu.VMEM((2, reps, shards, part, order), low),
            pltpu.VMEM((blocks, LINE, rows, order), low),
            pltpu.VMEM((blocks, 3, rows, order), wide),
            pltpu.VMEM((blocks, 3, rows, order), wide),
            pltpu.VMEM((blocks, 2, rows, order), wide),
            pltpu.VMEM((blocks, rows, order), low),
            pltpu.VMEM((blocks, shards, rows, order), low),
            pltpu.VMEM((order, order), low),
            pltpu.VMEM((2, order, order), low),
            pltpu.VMEM((2, order, order), low),
            pltpu.VMEM((2, order, order), low),
            pltpu.VMEM((2, order, order), low),
            pltpu.VMEM((blocks, rows, order), wide),
            pltpu.VMEM((blocks, rows, order), wide),
            pltpu.VMEM((blocks, order, order), low),
            pltpu.VMEM((rows, order), low),
            dma((5,)),
            dma((4, blocks)),
            dma((blocks, LINE)),
            dma((blocks, LINE)),
            dma((blocks, 3)),
            dma((blocks, 3)),
            dma((blocks, 2)),
            dma((blocks, shards)),
            dma((blocks, shards)),
            dma((shards,)),
            dma((shards,)),
            dma((LINE,)),
            dma((LINE,)),
            dma((LINE,)),
            dma((LINE,)),
            dma((3,)),
            dma((3,)),
            dma((6,)),
            dma((5,)),
            dma((6,)),
            dma((6,)),
            dma((blocks, LINE, 2)),
            dma((blocks, LINE)),
            dma((blocks, LINE)),
            dma((blocks, LINE)),
        ],
        compiler_params=pltpu.CompilerParams(
            collective_id=0, has_side_effects=True, vmem_limit_bytes=48 * 2**20
        ),
    )(owner_slot, refresh, grads, left_root, left_stat, right_stat, right_root)


def arrange_kernel(
    slots_ref,
    refresh_ref,
    left_in,
    right_in,
    direction_in,
    fresh_rows,
    fresh_right,
    left_root,
    right_root,
    left_new,
    right_new,
    left_root_new,
    right_root_new,
    direction,
    sems,
):
    blocks = left_in.shape[0]
    fresh_slot = slots_ref[refresh_ref[0]]
    slot = fresh_slot % blocks
    owns = fresh_slot // blocks == lax.axis_index("shard")
    copies = []

    def copy(source, target):
        copies.append(pltpu.make_async_copy(source, target, sems.at[len(copies)]))
        copies[-1].start()

    for block in range(blocks):
        where = (slot + block) % blocks
        copy(direction_in.at[block], direction.at[where])
        copy(left_in.at[block], left_new.at[where])
        copy(right_in.at[block], right_new.at[where])
        if block > 0:
            copy(right_root.at[where], right_root_new.at[where])
            copy(left_root.at[where], left_root_new.at[where])
    last = len(copies)

    @pl.when(owns)
    def _():
        pltpu.make_async_copy(fresh_right, right_root_new.at[slot], sems.at[last]).start()
        pltpu.make_async_copy(fresh_rows, left_root_new.at[slot], sems.at[last + 1]).start()

    @pl.when(jnp.logical_not(owns))
    def _():
        pltpu.make_async_copy(
            right_root.at[slot], right_root_new.at[slot], sems.at[last]
        ).start()
        pltpu.make_async_copy(
            left_root.at[slot], left_root_new.at[slot], sems.at[last + 1]
        ).start()

    pltpu.make_async_copy(fresh_right, right_root_new.at[slot], sems.at[last]).wait()
    pltpu.make_async_copy(fresh_rows, left_root_new.at[slot], sems.at[last + 1]).wait()
    for item in copies:
        item.wait()


def arrange(*operands):
    stat, root, right = operands[2], operands[7], operands[8]
    smem = pl.BlockSpec(memory_space=pltpu.SMEM)
    hbm = pl.BlockSpec(memory_space=pl.ANY)
    return pl.pallas_call(
        arrange_kernel,
        out_shape=(
            jax.ShapeDtypeStruct(stat.shape, stat.dtype),
            jax.ShapeDtypeStruct(stat.shape, stat.dtype),
            jax.ShapeDtypeStruct(root.shape, root.dtype),
            jax.ShapeDtypeStruct(right.shape, right.dtype),
            jax.ShapeDtypeStruct(right.shape, right.dtype),
        ),
        in_specs=[smem, smem] + [hbm] * 7,
        out_specs=(hbm,) * 5,
        scratch_shapes=[pltpu.SemaphoreType.DMA((5 * stat.shape[0],))],
    )(*operands)


def direct_body(grads, owner_slot, refresh, left_stat, right_stat, left_root, right_root):
    results = exchange(
        owner_slot,
        refresh,
        grads,
        left_root,
        left_stat,
        right_stat,
        right_root,
        lax.axis_size("shard"),
    )
    return arrange(owner_slot, refresh, *results, left_root, right_root)


def choose(mesh, *arrays):
    reps, shards = mesh.shape["rep"], mesh.shape["shard"]
    rows = arrays[0].shape[2] // reps
    direct = reps == 2 * LINE and shards == 4 and rows % (16 * shards) == 0
    return direct_body if direct else body


def solution(mesh):
    def run(*arrays):
        return mapped(mesh, choose(mesh, *arrays))(*arrays)

    return run


def mapped(mesh, body):
    return jax.shard_map(
        body,
        mesh=mesh,
        in_specs=(
            P("rep", "shard", None, None),
            P(),
            P(),
            P("shard", "rep", None),
            P("shard", "rep", None),
            P("shard", "rep", None),
            P("shard", None, None),
        ),
        out_specs=(
            P("shard", "rep", None),
            P("shard", "rep", None),
            P("shard", "rep", None),
            P("shard", None, None),
            P("shard", None, None),
        ),
        check_vma=False,
    )
```

```python
import functools

import jax
import jax.numpy as jnp
from jax import lax
from jax.experimental import pallas as pl
from jax.experimental.pallas import tpu as pltpu
from jax.sharding import PartitionSpec as P

ITERS = 2


decay_rate = 0.95
epsilon_shift = 1e-06


def inverse_root(statistic):
    order = statistic.shape[0]
    identity = (
        lax.broadcasted_iota(jnp.int32, (order, order), 0)
        == lax.broadcasted_iota(jnp.int32, (order, order), 1)
    ).astype(jnp.float32)
    shifted = statistic + epsilon_shift * identity
    norm_scale = 2.5 / jnp.sqrt(jnp.sum(shifted * shifted))
    moment = norm_scale * shifted
    current = identity
    for number in range(ITERS):
        factor = (5.0 * identity - moment) * 0.25
        factor_low = factor.astype(jnp.bfloat16)
        if number == 0:
            current = jnp.sqrt(jnp.sqrt(norm_scale)) * factor
        else:
            current = jnp.dot(
                current.astype(jnp.bfloat16), factor_low, preferred_element_type=jnp.float32
            )
        if number + 1 < ITERS:
            square = jnp.dot(factor_low, factor_low, preferred_element_type=jnp.float32).astype(
                jnp.bfloat16
            )
            fourth = jnp.dot(square, square, preferred_element_type=jnp.float32).astype(
                jnp.bfloat16
            )
            moment = jnp.dot(
                fourth, moment.astype(jnp.bfloat16), preferred_element_type=jnp.float32
            )
    return current.astype(jnp.bfloat16)


def both_roots(fresh_whole):
    return (inverse_root(fresh_whole[0]), inverse_root(fresh_whole[1]))


def empty_roots(fresh_whole):
    blank = jnp.zeros(fresh_whole.shape[1:], jnp.bfloat16)
    return (blank, blank)


def body(grads, owner_slot, refresh, left_stat, right_stat, left_root, right_root):
    blocks = grads.shape[1]
    block_order = grads.shape[2]
    rep_count = lax.axis_size("rep")
    shards = lax.axis_size("shard")
    row_count = block_order // rep_count
    rep_index = lax.axis_index("rep")
    shard_index = lax.axis_index("shard")
    partial_value = grads[0].astype(jnp.float32)
    row_share = lax.psum_scatter(partial_value, "rep", scatter_dimension=1, tiled=True)
    row_share = row_share.astype(jnp.bfloat16)
    slot_table = owner_slot.reshape(shards, blocks)
    own_slots = lax.dynamic_index_in_dim(slot_table, shard_index, 0, keepdims=False)
    targets = own_slots // blocks
    selector = (targets[None, :] == jnp.arange(shards, dtype=jnp.int32)[:, None]).astype(
        jnp.bfloat16
    )
    outgoing = jnp.einsum(
        "ok,krc->orc", selector, row_share, preferred_element_type=jnp.float32
    ).astype(jnp.bfloat16)
    incoming = lax.all_to_all(outgoing, "shard", split_axis=0, concat_axis=0, tiled=True)
    wanted = shard_index * blocks + jnp.arange(blocks, dtype=jnp.int32)
    receiver = (jnp.transpose(slot_table) == wanted[:, None]).astype(jnp.bfloat16)
    owned_rows = jnp.einsum(
        "ks,src->krc", receiver, incoming, preferred_element_type=jnp.float32
    ).astype(jnp.bfloat16)
    gathered = lax.all_gather(owned_rows, "rep", axis=1, tiled=True)
    left_new = (
        decay_rate * left_stat
        + jnp.einsum("krc,kjc->krj", owned_rows, gathered, preferred_element_type=jnp.float32)
        / block_order
    )
    column_share = lax.dynamic_slice_in_dim(gathered, rep_index * row_count, row_count, 2)
    right_new = (
        decay_rate * right_stat
        + jnp.einsum("kic,kij->kcj", column_share, gathered, preferred_element_type=jnp.float32)
        / block_order
    )
    fresh_slot = owner_slot[refresh[0]]
    holder = fresh_slot // blocks
    slot_index = fresh_slot % blocks
    owns_fresh = holder == shard_index
    fresh_pair = jnp.stack(
        [
            lax.dynamic_index_in_dim(left_new, slot_index, 0, keepdims=False),
            lax.dynamic_index_in_dim(right_new, slot_index, 0, keepdims=False),
        ]
    )
    fresh_whole = lax.all_gather(fresh_pair, "rep", axis=1, tiled=True)
    fresh_left, fresh_right = lax.cond(owns_fresh, both_roots, empty_roots, fresh_whole)
    fresh_rows = lax.dynamic_slice_in_dim(fresh_left, rep_index * row_count, row_count, 0)
    left_updated = lax.dynamic_update_index_in_dim(left_root, fresh_rows, slot_index, 0)
    left_root_new = jnp.where(owns_fresh, left_updated, left_root)
    right_updated = lax.dynamic_update_index_in_dim(right_root, fresh_right, slot_index, 0)
    right_root_new = jnp.where(owns_fresh, right_updated, right_root)
    half_step = jnp.einsum(
        "kri,kic->krc", left_root_new, gathered, preferred_element_type=jnp.float32
    ).astype(jnp.bfloat16)
    preconditioned = jnp.einsum(
        "kri,kic->krc", half_step, right_root_new, preferred_element_type=jnp.float32
    ).astype(jnp.bfloat16)
    direction = lax.all_gather(preconditioned, "rep", axis=1, tiled=True)
    return (left_new, right_new, left_root_new, right_root_new, direction)


MESH = pl.DeviceIdType.MESH
LINE = 4
PAIRED = ()


def dot(left, right, dims=(1, 0)):
    return lax.dot_general(
        left, right, (((dims[0],), (dims[1],)), ((), ())), preferred_element_type=jnp.float32
    )


def exchange_kernel(
    slots_in,
    refresh_ref,
    grads_ref,
    left_ref,
    left_stat_ref,
    right_stat_ref,
    right_ref,
    left_new_ref,
    right_new_ref,
    direction_ref,
    fresh_rows_ref,
    fresh_right_ref,
    slots_ref,
    arrived,
    mine,
    left_stat,
    right_stat,
    right_full,
    left_full,
    grad_full,
    stat_ref,
    quarter_in,
    stat_full,
    across,
    partial_out,
    from_outer,
    from_inner,
    share,
    incoming,
    turned,
    moment,
    factor,
    current,
    square,
    left_out,
    right_out,
    direction_out,
    fresh_rows_out,
    load_sem,
    store_sem,
    across_send,
    across_recv,
    partial_send,
    outer_recv,
    inner_recv,
    swap_send,
    swap_recv,
    part_send,
    part_recv,
    stat_send,
    stat_recv,
    stat_side_send,
    stat_side_recv,
    spread_send,
    spread_recv,
    root_send,
    root_recv,
    root_side_send,
    root_side_recv,
    line_send,
    line_recv,
    side_send,
    side_recv,
):
    blocks, order = mine.shape[0], mine.shape[1]
    rows = order // (2 * LINE)
    group = 2 * rows
    shards = stat_ref.shape[0]
    last = blocks - 1
    me = lax.axis_index("rep")
    shard = lax.axis_index("shard")
    place = me // 2
    side = me % 2
    other_row = (shard + 2) % shards
    other_core = shard + 1 - 2 * (shard % 2)
    partner = (place * 2 + (1 - side), shard)
    flip = place // (LINE // 2)
    middle = (place == 1) | (place == 2)
    edge = jnp.logical_not(middle)

    def real(position):
        return position + flip * (LINE - 1 - 2 * position)

    def at(position):
        return (real(position) * 2 + side, shard)

    def span(index):
        return pl.ds(pl.multiple_of(index * rows, rows), rows)

    def pair_span(index):
        return pl.ds(pl.multiple_of(index * group, group), group)

    loads = [
        pltpu.make_async_copy(left_stat_ref, left_stat, load_sem.at[0]),
        pltpu.make_async_copy(right_stat_ref, right_stat, load_sem.at[1]),
        pltpu.make_async_copy(grads_ref.at[0], arrived, load_sem.at[2]),
        pltpu.make_async_copy(left_ref, left_full.at[:, span(me), :], load_sem.at[3]),
        pltpu.make_async_copy(right_ref, right_full, load_sem.at[4]),
        pltpu.make_async_copy(slots_in, slots_ref, load_sem.at[5]),
    ]
    for index in (5, 0, 1, 2, 3, 4):
        loads[index].start()
    barrier = pltpu.get_barrier_semaphore()
    for step in range(1, LINE):
        pl.semaphore_signal(
            barrier,
            inc=1,
            device_id=((place + step) % LINE * 2 + side, shard),
            device_id_type=MESH,
        )
    pl.semaphore_signal(barrier, inc=1, device_id=partner, device_id_type=MESH)
    for step in range(1, shards):
        pl.semaphore_signal(
            barrier, inc=1, device_id=(me, (shard + step) % shards), device_id_type=MESH
        )
    loads[5].wait()
    slot = slots_ref[refresh_ref[0]] % blocks
    keeper = slots_ref[refresh_ref[0]] // blocks
    owns = keeper == shard

    def local(block):
        return (slot + block) % blocks

    loads[0].wait()
    loads[1].wait()
    part = rows // shards
    for index in range(shards):
        part_rows = pl.ds(index * part, part)
        stat_ref[index, 0] = left_stat[slot, part_rows, :].astype(jnp.bfloat16)
        stat_ref[index, 1] = right_stat[slot, part_rows, :].astype(jnp.bfloat16)
    loads[2].wait()
    for block in range(blocks):
        mine[block] = arrived[local(block)]
    loads[3].wait()
    pl.semaphore_wait(barrier, LINE - 1 + 1 + shards - 1)

    pending = {"all": [], "edge": [], "middle": []}

    def remote(src, dst, send_sem, recv_sem, device):
        return pltpu.make_async_remote_copy(
            src_ref=src,
            dst_ref=dst,
            send_sem=send_sem,
            recv_sem=recv_sem,
            device_id=device,
            device_id_type=MESH,
        )

    def send(kind, make):
        make().start()
        pending[kind].append(make)

    def arrive(dst, recv_sem):
        remote(dst, dst, recv_sem, recv_sem, partner).wait_recv()

    def both(on_edge, on_middle):
        pl.when(edge)(on_edge)
        pl.when(middle)(on_middle)

    def across_copy(block, target):
        return remote(
            mine.at[block, span(target * 2 + (1 - side)), :],
            across.at[block, target],
            across_send.at[block, target],
            across_recv.at[block, target],
            partner,
        )

    def send_across(kind, block, positions):
        for position in positions:
            send(kind, lambda p=position: across_copy(block, real(p)))

    def pair_sum(block, position):
        target = real(position)
        arrive(across.at[block, target], across_recv.at[block, target])
        own = mine[block, span(target * 2 + side), :].astype(jnp.float32)
        return own + across[block, target].astype(jnp.float32)

    def wait_outer(block, number):
        arrive(from_outer.at[block, number], outer_recv.at[block, number])
        return from_outer[block, number]

    def wait_inner(block, number):
        arrive(from_inner.at[block, number], inner_recv.at[block, number])
        return from_inner[block, number]

    def edge_far(block, position):
        number = position - 1
        partial_out[block, number] = pair_sum(block, position)
        send(
            "edge",
            lambda: remote(
                partial_out.at[block, number],
                from_outer.at[block, number],
                partial_send.at[block, number],
                outer_recv.at[block, number],
                at(1),
            ),
        )

    def middle_far(block, position):
        number = {3: 0, 2: 1, 0: 2}[position]
        if position == 0:
            earlier = wait_inner(block, 0)
            goal, landing = 0, 0
        else:
            earlier = wait_outer(block, position - 1)
            goal, landing = 2, number
        partial_out[block, number] = pair_sum(block, position) + earlier
        send(
            "middle",
            lambda: remote(
                partial_out.at[block, number],
                from_inner.at[block, landing],
                partial_send.at[block, number],
                inner_recv.at[block, landing],
                at(goal),
            ),
        )

    def swap_copy(block, number, source, owner, goal):
        return remote(
            source,
            incoming.at[block, owner],
            swap_send.at[block, number],
            swap_recv.at[block, number],
            (me, goal),
        )

    def swap(kind, block, total):
        share[block] = total.astype(jnp.bfloat16)
        send(kind, lambda: swap_copy(block, 0, share.at[block], shard, other_row))
        send(kind, lambda: swap_copy(block, 1, share.at[block], shard, other_core))
        incoming[block, shard] = share[block]

    def swap_next(kind, block):
        arrive(incoming.at[block, other_row], swap_recv.at[block, 0])
        send(
            kind,
            lambda: swap_copy(block, 2, incoming.at[block, other_row], other_row, other_core),
        )

    def edge_own(block):
        swap("edge", block, pair_sum(block, 0) + wait_inner(block, 0))

    def middle_own(block):
        total = pair_sum(block, 1) + wait_inner(block, 1)
        swap("middle", block, total + wait_outer(block, 0))

    def side_copy(block, source):
        where = grad_full.at[block, span(source * 2 + side), :]
        return remote(
            where, where, side_send.at[block, source], side_recv.at[block, source], partner
        )

    def wait_side(block, source):
        arrive(
            grad_full.at[block, span(source * 2 + (1 - side)), :], side_recv.at[block, source]
        )

    def line_rows(block, position):
        source = real(position)
        if block in PAIRED and position in (1, 2):
            return grad_full.at[block, pair_span(source), :]
        return grad_full.at[block, span(source * 2 + side), :]

    def line_copy(block, position, way, goal):
        where = line_rows(block, position)
        return remote(
            where,
            where,
            line_send.at[block, real(position), way],
            line_recv.at[block, real(position)],
            at(goal),
        )

    def wait_line(block, position):
        arrive(line_rows(block, position), line_recv.at[block, real(position)])

    def line_own(kind, block):
        if kind == "edge":
            send(kind, lambda: line_copy(block, 0, 0, 1))
        else:
            send(kind, lambda: line_copy(block, 1, 0, 0))
            send(kind, lambda: line_copy(block, 1, 1, 2))

    def take(kind, block):
        arrive(incoming.at[block, other_core], swap_recv.at[block, 1])
        arrive(incoming.at[block, (other_core + 2) % shards], swap_recv.at[block, 2])
        value = incoming[block, 0]
        wanted = shard * blocks + local(block)
        for origin in range(1, shards):
            held = slots_ref[origin * blocks + local(block)] == wanted
            value = jnp.where(held, incoming[block, origin], value)
        grad_full[block, span(me), :] = value
        if kind == "edge" or block not in PAIRED:
            line_own(kind, block)
        send(kind, lambda: side_copy(block, place))

    def line_begin(kind, block):
        wait_side(block, place)
        line_own(kind, block)

    def line_next(kind, block, position):
        wait_line(block, position)
        if kind == "middle":
            goal = 2 if position == 0 else 0
            send(kind, lambda: line_copy(block, position, 0, goal))
        if block not in PAIRED or position in (0, 3):
            send(kind, lambda: side_copy(block, real(position)))

    def gathered(kind, block):
        positions = [0, 1, 2, 3]
        if block in PAIRED:
            positions = [0, 3]
            if kind == "edge":
                wait_line(block, 1)
                wait_line(block, 2)
        for position in positions:
            wait_side(block, real(position))

    pieces = {
        "edge": ((1, 1, 3), (2, 2, 2), (3, 3, 1)),
        "middle": ((0, 0, 1), (0, 3, 1), (2, 2, 2), (2, 0, 1), (3, 3, 1)),
    }

    def columns(first, count):
        return pl.ds(
            pl.multiple_of((first + flip * (LINE - 2 * first - count)) * group, group),
            count * group,
        )

    def root_piece(piece, which):
        position, first, count = piece
        return left_full.at[:, span(real(position) * 2 + which), columns(first, count)]

    def send_root(kind, number, piece, goal, landing):
        send(
            kind,
            lambda: remote(
                root_piece(piece, side),
                root_piece(piece, side),
                root_send.at[number],
                root_recv.at[landing],
                at(goal),
            ),
        )

    def wait_root(kind, number):
        arrive(root_piece(pieces[kind][number], side), root_recv.at[number])

    def edge_roots():
        send_root("edge", 0, (0, 0, 1), 1, 0)
        send_root("edge", 1, (0, 3, 1), 1, 1)

    def middle_roots():
        send_root("middle", 0, (1, 0, 2), 2, 2)
        send_root("middle", 1, (1, 1, 3), 0, 0)
        send_root("middle", 2, (1, 3, 1), 2, 3)

    def middle_root(number):
        wait_root("middle", number)
        if number == 0:
            send_root("middle", 3, (0, 0, 1), 2, 4)
        if number == 2:
            send_root("middle", 4, (2, 2, 2), 0, 1)
        if number == 4:
            send_root("middle", 5, (3, 3, 1), 0, 2)
        if number == 1:
            wait_root("middle", 3)

    def edge_roots_next():
        for number in range(3):
            wait_root("edge", number)

    def root_side(kind, number):
        def make():
            if number == 0:
                where = left_full.at[:, span(me), :]
            else:
                where = root_piece(pieces[kind][number - 1], side)
            return remote(
                where, where, root_side_send.at[number], root_side_recv.at[number], partner
            )

        return make

    def wait_root_side(kind):
        arrive(left_full.at[:, span(place * 2 + 1 - side), :], root_side_recv.at[0])
        for number, piece in enumerate(pieces[kind]):
            arrive(root_piece(piece, 1 - side), root_side_recv.at[number + 1])

    def mirror(kind):
        tiles = [(1, 2), (1, 3), (2, 3)]
        if kind == "edge":
            tiles += [(0, 1), (0, 2), (0, 3)]
        else:
            tiles += [(1, 0), (2, 0), (0, 3)]
        for block in range(blocks):
            for row, column in tiles:
                value = left_full[block, pair_span(real(row)), columns(column, 1)]
                left_full[block, pair_span(real(column)), columns(row, 1)] = value.T

    def to_shards(step):
        peer = (shard + step) % shards
        return remote(
            stat_ref.at[peer],
            quarter_in.at[shard],
            part_send.at[step],
            part_recv.at[step],
            (me, peer),
        )

    def stat_side():
        where = stat_full.at[:, me, shard]
        return remote(where, where, stat_side_send.at[0], stat_side_recv.at[0], partner)

    def stat_rows(position):
        return stat_full.at[:, pl.ds(real(position) * 2, 2), shard]

    def stat_copy(position, way, goal):
        where = stat_rows(position)
        return remote(
            where,
            where,
            stat_send.at[real(position), way],
            stat_recv.at[real(position)],
            at(goal),
        )

    def wait_stat(position):
        arrive(stat_rows(position), stat_recv.at[real(position)])

    def send_quarters(kind):
        for step in range(1, shards):
            origin = (shard + shards - step) % shards
            arrive(quarter_in.at[origin], part_recv.at[step])
        stat_full[:, me, shard] = quarter_in[keeper]
        send(kind, stat_side)

    def stat_begin(kind):
        arrive(stat_full.at[:, place * 2 + (1 - side), shard], stat_side_recv.at[0])
        if kind == "edge":
            send(kind, lambda: stat_copy(0, 0, 1))
        else:
            send(kind, lambda: stat_copy(1, 0, 0))
            send(kind, lambda: stat_copy(1, 1, 2))

    def stat_next(position):
        wait_stat(position)
        goal = 2 if position == 0 else 0
        send("middle", lambda: stat_copy(position, 0, goal))

    def spread(number, owner, goal):
        where = stat_full.at[:, :, owner]
        return remote(
            where, where, spread_send.at[number], spread_recv.at[number], (me, goal)
        )

    def spread_quarters(kind):
        if kind == "edge":
            for position in (1, 2, 3):
                wait_stat(position)
        send(kind, lambda: spread(0, shard, other_row))
        send(kind, lambda: spread(1, shard, other_core))

    def spread_next(kind):
        arrive(stat_full.at[:, :, other_row], spread_recv.at[0])
        send(kind, lambda: spread(2, other_row, other_core))

    def spread_end():
        arrive(stat_full.at[:, :, other_core], spread_recv.at[1])
        arrive(
            stat_full.at[:, :, (other_core + 2) % shards], spread_recv.at[2]
        )

    tile = pair_span(place)

    def new_statistics(block):
        grad = grad_full[block]
        own = grad_full[block, span(me), :]
        left_out[block] = decay_rate * left_stat[local(block)] + dot(own, grad, (1, 1)) / order
        turned_rows = grad_full[block, :, tile].T
        own_turned = jnp.where(side == 0, turned_rows[:rows], turned_rows[rows:])
        right_out[block] = decay_rate * right_stat[local(block)] + dot(own_turned, grad) / order
        stores.append((left_out.at[block], left_new_ref.at[block], 0, block))
        stores.append((right_out.at[block], right_new_ref.at[block], 1, block))
        for entry in stores[-2:]:
            store(*entry).start()

    stores = []

    def store(source, target, kind, block):
        return pltpu.make_async_copy(source, target, store_sem.at[kind, block])

    def renew_begin(which):
        identity = (
            lax.broadcasted_iota(jnp.int32, (order, order), 0)
            == lax.broadcasted_iota(jnp.int32, (order, order), 1)
        ).astype(jnp.float32)
        grad = grad_full[0]
        if which == 0:
            turned[...] = grad.T
            product = dot(grad, turned[...])
        else:
            product = dot(turned[...], grad)
        old = stat_full[which].reshape(order, order).astype(jnp.float32)
        shifted = decay_rate * old + product / order + epsilon_shift * identity
        scale = 2.5 / jnp.sqrt(jnp.sum(shifted * shifted))
        start = scale * shifted
        moment[which] = start.astype(jnp.bfloat16)
        step = (5.0 * identity - start) * 0.25
        factor[which] = step.astype(jnp.bfloat16)
        current[which] = (jnp.sqrt(jnp.sqrt(scale)) * step).astype(jnp.bfloat16)

    def renew_square():
        for which in range(2):
            square[which] = dot(factor[which], factor[which]).astype(jnp.bfloat16)

    def renew_fourth():
        for which in range(2):
            factor[which] = dot(square[which], square[which]).astype(jnp.bfloat16)

    def renew_factor():
        identity = (
            lax.broadcasted_iota(jnp.int32, (order, order), 0)
            == lax.broadcasted_iota(jnp.int32, (order, order), 1)
        ).astype(jnp.float32)
        for which in range(2):
            value = dot(factor[which], moment[which])
            square[which] = ((5.0 * identity - value) * 0.25).astype(jnp.bfloat16)

    def renew_end():
        for which in range(2):
            moment[which] = dot(current[which], square[which]).astype(jnp.bfloat16)
        fresh_rows_out[...] = moment[0, span(me), :]
        stores.append((fresh_rows_out, fresh_rows_ref, 2, 0))
        stores.append((moment.at[1], fresh_right_ref, 2, 1))
        for entry in stores[-2:]:
            store(*entry).start()

    def direct(block):
        root = left_full[local(block)]
        other = right_full[local(block)]
        if block == 0:
            root = jnp.where(owns, moment[0], root)
            other = jnp.where(owns, moment[1], other)
        half = dot(root, grad_full[block]).astype(jnp.bfloat16)
        direction_out[block] = dot(half, other).astype(jnp.bfloat16)
        stores.append((direction_out.at[block], direction_ref.at[block], 3, block))
        store(*stores[-1]).start()

    for step in range(1, shards):
        send("all", lambda step=step: to_shards(step))
    quarter_in[shard] = stat_ref[shard]

    @pl.when(edge)
    def _():
        send_across("edge", 0, (3, 2, 1, 0))
        send_across("edge", 1, (3, 2, 1, 0))
        edge_roots()
        send("edge", root_side("edge", 0))
        send_quarters("edge")
        edge_far(0, 3)
        edge_far(0, 2)
        edge_far(0, 1)
        edge_roots_next()
        edge_far(1, 3)
        send_across("edge", 2, (3, 2, 1, 0))
        edge_far(1, 2)
        edge_far(1, 1)
        edge_own(0)
        send("edge", root_side("edge", 1))
        send("edge", root_side("edge", 2))
        stat_begin("edge")
        swap_next("edge", 0)
        edge_far(2, 3)
        take("edge", 0)
        edge_far(2, 2)
        edge_far(2, 1)
        line_next("edge", 0, 1)
        edge_own(1)
        line_next("edge", 0, 2)
        swap_next("edge", 1)
        spread_quarters("edge")
        take("edge", 1)
        send("edge", root_side("edge", 3))
        line_next("edge", 1, 1)
        edge_own(2)
        line_next("edge", 0, 3)
        spread_next("edge")
        wait_root_side("edge")
        mirror("edge")
        line_next("edge", 1, 2)
        swap_next("edge", 2)
        spread_end()
        take("edge", 2)
        gathered("edge", 0)

    @pl.when(middle)
    def _():
        send_across("middle", 0, (3, 2, 0, 1))
        middle_roots()
        send_quarters("middle")
        middle_root(0)
        middle_root(2)
        middle_root(1)
        middle_root(4)
        middle_far(0, 3)
        send_across("middle", 1, (3, 2, 0, 1))
        send("middle", root_side("middle", 0))
        send("middle", root_side("middle", 4))
        stat_begin("middle")
        middle_far(0, 2)
        middle_far(0, 0)
        stat_next(2)
        middle_own(0)
        middle_far(1, 3)
        send("middle", root_side("middle", 5))
        middle_far(1, 2)
        swap_next("middle", 0)
        take("middle", 0)
        send_across("middle", 2, (3, 2, 0, 1))
        send("middle", root_side("middle", 3))
        middle_far(1, 0)
        stat_next(0)
        middle_own(1)
        line_next("middle", 0, 2)
        middle_far(2, 3)
        stat_next(3)
        swap_next("middle", 1)
        spread_quarters("middle")
        line_next("middle", 0, 0)
        take("middle", 1)
        middle_far(2, 0)
        middle_far(2, 2)
        line_next("middle", 0, 3)
        line_next("middle", 1, 2)
        spread_next("middle")
        line_next("middle", 1, 0)
        spread_end()
        middle_own(2)
        send("middle", root_side("middle", 2))
        gathered("middle", 0)

    renew_begin(0)
    @pl.when(middle)
    def _():
        line_next("middle", 1, 3)

    renew_begin(1)
    @pl.when(edge)
    def _():
        line_next("edge", 1, 3)

    @pl.when(middle)
    def _():
        swap_next("middle", 2)

    renew_square()
    @pl.when(middle)
    def _():
        take("middle", 2)
        send("middle", root_side("middle", 1))

    renew_fourth()
    @pl.when(edge)
    def _():
        line_next("edge", 2, 1)

    @pl.when(middle)
    def _():
        line_next("middle", 2, 0)

    renew_factor()
    @pl.when(edge)
    def _():
        gathered("edge", 1)

    @pl.when(middle)
    def _():
        gathered("middle", 1)
        line_next("middle", 2, 2)
        line_next("middle", 2, 3)
        wait_root_side("middle")
        mirror("middle")

    loads[4].wait()
    direct(1)
    @pl.when(edge)
    def _():
        line_next("edge", 2, 2)

    new_statistics(0)
    renew_end()
    @pl.when(edge)
    def _():
        line_next("edge", 2, 3)

    direct(0)
    @pl.when(middle)
    def _():
        gathered("middle", 2)

    new_statistics(1)
    @pl.when(edge)
    def _():
        gathered("edge", 2)

    direct(2)
    new_statistics(2)
    def finish(kind):
        for make in pending[kind]:
            make().wait_send()

    both(lambda: finish("edge"), lambda: finish("middle"))
    finish("all")
    for entry in stores:
        store(*entry).wait()


def exchange(owner_slot, refresh, grads, left_root, left_stat, right_stat, right_root, shards):
    blocks, order = grads.shape[1], grads.shape[2]
    reps = 2 * LINE
    rows = order // reps
    part = rows // shards
    low = jnp.bfloat16
    wide = jnp.float32
    smem = pl.BlockSpec(memory_space=pltpu.SMEM)
    hbm = pl.BlockSpec(memory_space=pltpu.HBM)
    free = pl.BlockSpec(memory_space=pl.ANY)
    dma = pltpu.SemaphoreType.DMA
    return pl.pallas_call(
        exchange_kernel,
        out_shape=(
            jax.ShapeDtypeStruct((blocks, rows, order), wide),
            jax.ShapeDtypeStruct((blocks, rows, order), wide),
            jax.ShapeDtypeStruct((blocks, order, order), low),
            jax.ShapeDtypeStruct((rows, order), low),
            jax.ShapeDtypeStruct((order, order), low),
        ),
        in_specs=[hbm, smem] + [hbm] * 5,
        out_specs=(free,) * 5,
        scratch_shapes=[
            pltpu.SMEM(owner_slot.shape, owner_slot.dtype),
            pltpu.VMEM((blocks, order, order), low),
            pltpu.VMEM((blocks, order, order), low),
            pltpu.VMEM((blocks, rows, order), wide),
            pltpu.VMEM((blocks, rows, order), wide),
            pltpu.VMEM((blocks, order, order), low),
            pltpu.VMEM((blocks, order, order), low),
            pltpu.VMEM((blocks, order, order), low),
            pltpu.VMEM((shards, 2, part, order), low),
            pltpu.VMEM((shards, 2, part, order), low),
            pltpu.VMEM((2, reps, shards, part, order), low),
            pltpu.VMEM((blocks, LINE, rows, order), low),
            pltpu.VMEM((blocks, 3, rows, order), wide),
            pltpu.VMEM((blocks, 3, rows, order), wide),
            pltpu.VMEM((blocks, 2, rows, order), wide),
            pltpu.VMEM((blocks, rows, order), low),
            pltpu.VMEM((blocks, shards, rows, order), low),
            pltpu.VMEM((order, order), low),
            pltpu.VMEM((2, order, order), low),
            pltpu.VMEM((2, order, order), low),
            pltpu.VMEM((2, order, order), low),
            pltpu.VMEM((2, order, order), low),
            pltpu.VMEM((blocks, rows, order), wide),
            pltpu.VMEM((blocks, rows, order), wide),
            pltpu.VMEM((blocks, order, order), low),
            pltpu.VMEM((rows, order), low),
            dma((6,)),
            dma((4, blocks)),
            dma((blocks, LINE)),
            dma((blocks, LINE)),
            dma((blocks, 3)),
            dma((blocks, 3)),
            dma((blocks, 2)),
            dma((blocks, 3)),
            dma((blocks, 3)),
            dma((shards,)),
            dma((shards,)),
            dma((LINE, 2)),
            dma((LINE,)),
            dma((1,)),
            dma((1,)),
            dma((3,)),
            dma((3,)),
            dma((6,)),
            dma((5,)),
            dma((6,)),
            dma((6,)),
            dma((blocks, LINE, 2)),
            dma((blocks, LINE)),
            dma((blocks, LINE)),
            dma((blocks, LINE)),
        ],
        compiler_params=pltpu.CompilerParams(
            collective_id=0, has_side_effects=True, vmem_limit_bytes=48 * 2**20
        ),
    )(
        fixed(owner_slot),
        refresh,
        *map(fixed, (grads, left_root, left_stat, right_stat, right_root)),
    )


def fixed(array):
    return pltpu.with_memory_space_constraint(array, pltpu.HBM)


def arrange_kernel(
    slots_ref,
    refresh_ref,
    left_in,
    right_in,
    direction_in,
    fresh_rows,
    fresh_right,
    left_root,
    right_root,
    left_new,
    right_new,
    left_root_new,
    right_root_new,
    direction,
    sems,
):
    blocks = left_in.shape[0]
    fresh_slot = slots_ref[refresh_ref[0]]
    slot = fresh_slot % blocks
    owns = fresh_slot // blocks == lax.axis_index("shard")
    copies = []

    def copy(source, target):
        copies.append(pltpu.make_async_copy(source, target, sems.at[len(copies)]))
        copies[-1].start()

    for block in range(blocks):
        where = (slot + block) % blocks
        copy(direction_in.at[block], direction.at[where])
        copy(left_in.at[block], left_new.at[where])
        copy(right_in.at[block], right_new.at[where])
        if block > 0:
            copy(right_root.at[where], right_root_new.at[where])
            copy(left_root.at[where], left_root_new.at[where])
    last = len(copies)

    @pl.when(owns)
    def _():
        pltpu.make_async_copy(fresh_right, right_root_new.at[slot], sems.at[last]).start()
        pltpu.make_async_copy(fresh_rows, left_root_new.at[slot], sems.at[last + 1]).start()

    @pl.when(jnp.logical_not(owns))
    def _():
        pltpu.make_async_copy(
            right_root.at[slot], right_root_new.at[slot], sems.at[last]
        ).start()
        pltpu.make_async_copy(
            left_root.at[slot], left_root_new.at[slot], sems.at[last + 1]
        ).start()

    pltpu.make_async_copy(fresh_right, right_root_new.at[slot], sems.at[last]).wait()
    pltpu.make_async_copy(fresh_rows, left_root_new.at[slot], sems.at[last + 1]).wait()
    for item in copies:
        item.wait()


def arrange(*operands):
    stat, root, right = operands[2], operands[7], operands[8]
    smem = pl.BlockSpec(memory_space=pltpu.SMEM)
    hbm = pl.BlockSpec(memory_space=pl.ANY)
    return pl.pallas_call(
        arrange_kernel,
        out_shape=(
            jax.ShapeDtypeStruct(stat.shape, stat.dtype),
            jax.ShapeDtypeStruct(stat.shape, stat.dtype),
            jax.ShapeDtypeStruct(root.shape, root.dtype),
            jax.ShapeDtypeStruct(right.shape, right.dtype),
            jax.ShapeDtypeStruct(right.shape, right.dtype),
        ),
        in_specs=[smem, smem] + [hbm] * 7,
        out_specs=(hbm,) * 5,
        scratch_shapes=[pltpu.SemaphoreType.DMA((5 * stat.shape[0],))],
        compiler_params=pltpu.CompilerParams(vmem_limit_bytes=2**20),
    )(*operands)


def direct_body(grads, owner_slot, refresh, left_stat, right_stat, left_root, right_root):
    results = exchange(
        owner_slot,
        refresh,
        grads,
        left_root,
        left_stat,
        right_stat,
        right_root,
        lax.axis_size("shard"),
    )
    return arrange(owner_slot, refresh, *results, left_root, right_root)


def choose(mesh, *arrays):
    reps, shards = mesh.shape["rep"], mesh.shape["shard"]
    rows = arrays[0].shape[2] // reps
    direct = reps == 2 * LINE and shards == 4 and rows % (16 * shards) == 0
    return direct_body if direct else body


def solution(mesh):
    def run(*arrays):
        return mapped(mesh, choose(mesh, *arrays))(*arrays)

    return run


def mapped(mesh, body):
    return jax.shard_map(
        body,
        mesh=mesh,
        in_specs=(
            P("rep", "shard", None, None),
            P(),
            P(),
            P("shard", "rep", None),
            P("shard", "rep", None),
            P("shard", "rep", None),
            P("shard", None, None),
        ),
        out_specs=(
            P("shard", "rep", None),
            P("shard", "rep", None),
            P("shard", "rep", None),
            P("shard", None, None),
            P("shard", None, None),
        ),
        check_vma=False,
    )
```

```python
import functools

import jax
import jax.numpy as jnp
from jax import lax
from jax.experimental import pallas as pl
from jax.experimental.pallas import tpu as pltpu
from jax.sharding import PartitionSpec as P

ITERS = 2


decay_rate = 0.95
epsilon_shift = 1e-06


def inverse_root(statistic):
    order = statistic.shape[0]
    identity = (
        lax.broadcasted_iota(jnp.int32, (order, order), 0)
        == lax.broadcasted_iota(jnp.int32, (order, order), 1)
    ).astype(jnp.float32)
    shifted = statistic + epsilon_shift * identity
    norm_scale = 2.5 / jnp.sqrt(jnp.sum(shifted * shifted))
    moment = norm_scale * shifted
    current = identity
    for number in range(ITERS):
        factor = (5.0 * identity - moment) * 0.25
        factor_low = factor.astype(jnp.bfloat16)
        if number == 0:
            current = jnp.sqrt(jnp.sqrt(norm_scale)) * factor
        else:
            current = jnp.dot(
                current.astype(jnp.bfloat16), factor_low, preferred_element_type=jnp.float32
            )
        if number + 1 < ITERS:
            square = jnp.dot(factor_low, factor_low, preferred_element_type=jnp.float32).astype(
                jnp.bfloat16
            )
            fourth = jnp.dot(square, square, preferred_element_type=jnp.float32).astype(
                jnp.bfloat16
            )
            moment = jnp.dot(
                fourth, moment.astype(jnp.bfloat16), preferred_element_type=jnp.float32
            )
    return current.astype(jnp.bfloat16)


def both_roots(fresh_whole):
    return (inverse_root(fresh_whole[0]), inverse_root(fresh_whole[1]))


def empty_roots(fresh_whole):
    blank = jnp.zeros(fresh_whole.shape[1:], jnp.bfloat16)
    return (blank, blank)


def body(grads, owner_slot, refresh, left_stat, right_stat, left_root, right_root):
    blocks = grads.shape[1]
    block_order = grads.shape[2]
    rep_count = lax.axis_size("rep")
    shards = lax.axis_size("shard")
    row_count = block_order // rep_count
    rep_index = lax.axis_index("rep")
    shard_index = lax.axis_index("shard")
    partial_value = grads[0].astype(jnp.float32)
    row_share = lax.psum_scatter(partial_value, "rep", scatter_dimension=1, tiled=True)
    row_share = row_share.astype(jnp.bfloat16)
    slot_table = owner_slot.reshape(shards, blocks)
    own_slots = lax.dynamic_index_in_dim(slot_table, shard_index, 0, keepdims=False)
    targets = own_slots // blocks
    selector = (targets[None, :] == jnp.arange(shards, dtype=jnp.int32)[:, None]).astype(
        jnp.bfloat16
    )
    outgoing = jnp.einsum(
        "ok,krc->orc", selector, row_share, preferred_element_type=jnp.float32
    ).astype(jnp.bfloat16)
    incoming = lax.all_to_all(outgoing, "shard", split_axis=0, concat_axis=0, tiled=True)
    wanted = shard_index * blocks + jnp.arange(blocks, dtype=jnp.int32)
    receiver = (jnp.transpose(slot_table) == wanted[:, None]).astype(jnp.bfloat16)
    owned_rows = jnp.einsum(
        "ks,src->krc", receiver, incoming, preferred_element_type=jnp.float32
    ).astype(jnp.bfloat16)
    gathered = lax.all_gather(owned_rows, "rep", axis=1, tiled=True)
    left_new = (
        decay_rate * left_stat
        + jnp.einsum("krc,kjc->krj", owned_rows, gathered, preferred_element_type=jnp.float32)
        / block_order
    )
    column_share = lax.dynamic_slice_in_dim(gathered, rep_index * row_count, row_count, 2)
    right_new = (
        decay_rate * right_stat
        + jnp.einsum("kic,kij->kcj", column_share, gathered, preferred_element_type=jnp.float32)
        / block_order
    )
    fresh_slot = owner_slot[refresh[0]]
    holder = fresh_slot // blocks
    slot_index = fresh_slot % blocks
    owns_fresh = holder == shard_index
    fresh_pair = jnp.stack(
        [
            lax.dynamic_index_in_dim(left_new, slot_index, 0, keepdims=False),
            lax.dynamic_index_in_dim(right_new, slot_index, 0, keepdims=False),
        ]
    )
    fresh_whole = lax.all_gather(fresh_pair, "rep", axis=1, tiled=True)
    fresh_left, fresh_right = lax.cond(owns_fresh, both_roots, empty_roots, fresh_whole)
    fresh_rows = lax.dynamic_slice_in_dim(fresh_left, rep_index * row_count, row_count, 0)
    left_updated = lax.dynamic_update_index_in_dim(left_root, fresh_rows, slot_index, 0)
    left_root_new = jnp.where(owns_fresh, left_updated, left_root)
    right_updated = lax.dynamic_update_index_in_dim(right_root, fresh_right, slot_index, 0)
    right_root_new = jnp.where(owns_fresh, right_updated, right_root)
    half_step = jnp.einsum(
        "kri,kic->krc", left_root_new, gathered, preferred_element_type=jnp.float32
    ).astype(jnp.bfloat16)
    preconditioned = jnp.einsum(
        "kri,kic->krc", half_step, right_root_new, preferred_element_type=jnp.float32
    ).astype(jnp.bfloat16)
    direction = lax.all_gather(preconditioned, "rep", axis=1, tiled=True)
    return (left_new, right_new, left_root_new, right_root_new, direction)


MESH = pl.DeviceIdType.MESH
LINE = 4
CHUNKS = ((0, 0, 2), (0, 1, 2), (1, 0, 2), (1, 1, 2), (2, 0, 2), (2, 1, 2))
DIRECT = (2,)
PAIRED = ()


def dot(left, right, dims=(1, 0)):
    return lax.dot_general(
        left, right, (((dims[0],), (dims[1],)), ((), ())), preferred_element_type=jnp.float32
    )


def exchange_kernel(
    slots_in,
    refresh_ref,
    grads_ref,
    left_ref,
    left_stat_ref,
    right_stat_ref,
    right_ref,
    left_new_ref,
    right_new_ref,
    direction_ref,
    fresh_rows_ref,
    fresh_right_ref,
    slots_ref,
    arrived,
    mine,
    left_stat,
    right_stat,
    right_full,
    left_full,
    grad_full,
    stat_ref,
    quarter_in,
    stat_full,
    across,
    partial_out,
    from_outer,
    from_inner,
    share,
    incoming,
    turned,
    moment,
    factor,
    current,
    square,
    left_out,
    right_out,
    direction_out,
    fresh_rows_out,
    load_sem,
    store_sem,
    across_send,
    across_recv,
    partial_send,
    outer_recv,
    inner_recv,
    swap_send,
    swap_recv,
    part_send,
    part_recv,
    stat_send,
    stat_recv,
    stat_side_send,
    stat_side_recv,
    spread_send,
    spread_recv,
    root_send,
    root_recv,
    root_side_send,
    root_side_recv,
    line_send,
    line_recv,
    side_send,
    side_recv,
):
    blocks, order = mine.shape[0], mine.shape[1]
    rows = order // (2 * LINE)
    group = 2 * rows
    shards = stat_ref.shape[0]
    me = lax.axis_index("rep")
    shard = lax.axis_index("shard")
    place = me // 2
    side = me % 2
    other_row = (shard + 2) % shards
    other_core = shard + 1 - 2 * (shard % 2)
    partner = (place * 2 + (1 - side), shard)
    flip = place // (LINE // 2)
    middle = (place == 1) | (place == 2)
    edge = jnp.logical_not(middle)

    def real(position):
        return position + flip * (LINE - 1 - 2 * position)

    def at(position):
        return (real(position) * 2 + side, shard)

    def span(index):
        return pl.ds(pl.multiple_of(index * rows, rows), rows)

    def pair_span(index):
        return pl.ds(pl.multiple_of(index * group, group), group)

    loads = [
        pltpu.make_async_copy(left_stat_ref, left_stat, load_sem.at[0]),
        pltpu.make_async_copy(right_stat_ref, right_stat, load_sem.at[1]),
        pltpu.make_async_copy(grads_ref.at[0], arrived, load_sem.at[2]),
        pltpu.make_async_copy(left_ref, left_full.at[:, span(me), :], load_sem.at[3]),
        pltpu.make_async_copy(right_ref, right_full, load_sem.at[4]),
        pltpu.make_async_copy(slots_in, slots_ref, load_sem.at[5]),
    ]
    for index in (5, 2, 0, 1, 3, 4):
        loads[index].start()
    barrier = pltpu.get_barrier_semaphore()
    for step in range(1, LINE):
        pl.semaphore_signal(
            barrier,
            inc=1,
            device_id=((place + step) % LINE * 2 + side, shard),
            device_id_type=MESH,
        )
    pl.semaphore_signal(barrier, inc=1, device_id=partner, device_id_type=MESH)
    for step in range(1, shards):
        pl.semaphore_signal(
            barrier, inc=1, device_id=(me, (shard + step) % shards), device_id_type=MESH
        )
    loads[5].wait()
    slot = slots_ref[refresh_ref[0]] % blocks
    keeper = slots_ref[refresh_ref[0]] // blocks
    owns = keeper == shard

    def local(block):
        return (slot + block) % blocks

    loads[2].wait()
    mine[0] = arrived[local(0)]
    pl.semaphore_wait(barrier, LINE - 1 + 1 + shards - 1)

    pending = {"all": [], "edge": [], "middle": []}

    def remote(src, dst, send_sem, recv_sem, device):
        return pltpu.make_async_remote_copy(
            src_ref=src,
            dst_ref=dst,
            send_sem=send_sem,
            recv_sem=recv_sem,
            device_id=device,
            device_id_type=MESH,
        )

    def send(kind, make):
        make().start()
        pending[kind].append(make)

    def drain(kind):
        for make in pending[kind]:
            make().wait_send()
        pending[kind] = []

    def arrive(dst, recv_sem):
        remote(dst, dst, recv_sem, recv_sem, partner).wait_recv()

    def both(on_edge, on_middle):
        pl.when(edge)(on_edge)
        pl.when(middle)(on_middle)

    def cells(chunk):
        block, number, count = CHUNKS[chunk]
        size = rows // count
        return block, pl.ds(number * size, size)

    def span_of(chunk, index):
        block, number, count = CHUNKS[chunk]
        size = rows // count
        first = index * rows + number * size
        return block, pl.ds(pl.multiple_of(first, size), size)

    def across_copy(chunk, target):
        block, there = span_of(chunk, target * 2 + (1 - side))
        block, here = cells(chunk)
        return remote(
            mine.at[block, there, :],
            across.at[block, target, here],
            across_send.at[chunk, target],
            across_recv.at[chunk, target],
            partner,
        )

    def send_across(kind, chunk, positions):
        for position in positions:
            send(kind, lambda p=position: across_copy(chunk, real(p)))

    def pair_sum(chunk, position):
        target = real(position)
        block, here = cells(chunk)
        arrive(across.at[block, target, here], across_recv.at[chunk, target])
        own = mine[span_of(chunk, target * 2 + side)].astype(jnp.float32)
        return own + across[block, target, here].astype(jnp.float32)

    def wait_outer(chunk, number):
        block, here = cells(chunk)
        arrive(from_outer.at[block, number, here], outer_recv.at[chunk, number])
        return from_outer[block, number, here]

    def wait_inner(chunk, number):
        block, here = cells(chunk)
        arrive(from_inner.at[block, number, here], inner_recv.at[chunk, number])
        return from_inner[block, number, here]

    def edge_far(chunk, position):
        number = position - 1
        block, here = cells(chunk)
        partial_out[block, number, here] = pair_sum(chunk, position)
        send(
            "edge",
            lambda: remote(
                partial_out.at[block, number, here],
                from_outer.at[block, number, here],
                partial_send.at[chunk, number],
                outer_recv.at[chunk, number],
                at(1),
            ),
        )

    def middle_far(chunk, position):
        number = {3: 0, 2: 1, 0: 2}[position]
        block, here = cells(chunk)
        if position == 0:
            earlier = wait_inner(chunk, 0)
            goal, landing = 0, 0
        else:
            earlier = wait_outer(chunk, position - 1)
            goal, landing = 2, number
        partial_out[block, number, here] = pair_sum(chunk, position) + earlier
        send(
            "middle",
            lambda: remote(
                partial_out.at[block, number, here],
                from_inner.at[block, landing, here],
                partial_send.at[chunk, number],
                inner_recv.at[chunk, landing],
                at(goal),
            ),
        )

    def swap_rows(chunk, owner):
        block, here = cells(chunk)
        return incoming.at[block, owner, here]

    others = ((other_core + 2) % shards, other_row, other_core)

    def swap(kind, chunk, total):
        block, here = cells(chunk)
        value = total.astype(jnp.bfloat16)
        share[block, here] = value
        for number, goal in enumerate(others):
            send(
                kind,
                lambda n=number, g=goal: remote(
                    share.at[block, here],
                    swap_rows(chunk, shard),
                    swap_send.at[chunk, n],
                    swap_recv.at[chunk, n],
                    (me, g),
                ),
            )
        incoming[block, shard, here] = value

    def edge_own(chunk):
        swap("edge", chunk, pair_sum(chunk, 0) + wait_inner(chunk, 0))

    def middle_own(chunk):
        total = pair_sum(chunk, 1) + wait_inner(chunk, 1)
        swap("middle", chunk, total + wait_outer(chunk, 0))

    def share_rows(chunk, source, which):
        block, here = cells(chunk)
        return grad_full.at[block, source, which, here]

    def side_copy(chunk, source):
        where = share_rows(chunk, source, side)
        return remote(
            where, where, side_send.at[chunk, source], side_recv.at[chunk, source], partner
        )

    def wait_side(chunk, source):
        arrive(share_rows(chunk, source, 1 - side), side_recv.at[chunk, source])

    def line_rows(chunk, position):
        if CHUNKS[chunk][0] in PAIRED and position in (1, 2):
            return share_rows(chunk, real(position), slice(None))
        return share_rows(chunk, real(position), side)

    def line_copy(chunk, position, way, goal):
        where = line_rows(chunk, position)
        return remote(
            where,
            where,
            line_send.at[chunk, real(position), way],
            line_recv.at[chunk, real(position)],
            at(goal),
        )

    def take(kind, chunk):
        for number, origin in enumerate(others):
            arrive(swap_rows(chunk, origin), swap_recv.at[chunk, number])
        block, here = cells(chunk)
        value = incoming[block, 0, here]
        wanted = shard * blocks + local(block)
        for origin in range(1, shards):
            held = slots_ref[origin * blocks + local(block)] == wanted
            value = jnp.where(held, incoming[block, origin, here], value)
        grad_full[block, place, side, here] = value
        paired = block in PAIRED and kind == "middle"
        if not paired:
            line_begin(kind, chunk)
        send(kind, lambda: side_copy(chunk, place))
        if block in DIRECT:
            own, near, far = (0, 1, (2, 3)) if kind == "edge" else (1, 2, (3,))
            for way, goal in enumerate(far):
                send(kind, lambda w=way, g=goal: line_copy(chunk, own, near + w, g))

    def line_begin(kind, chunk):
        if CHUNKS[chunk][0] in PAIRED and kind == "middle":
            wait_side(chunk, place)
        if kind == "edge":
            send(kind, lambda: line_copy(chunk, 0, 0, 1))
        else:
            send(kind, lambda: line_copy(chunk, 1, 0, 0))
            send(kind, lambda: line_copy(chunk, 1, 1, 2))

    def wait_line(chunk, position):
        arrive(line_rows(chunk, position), line_recv.at[chunk, real(position)])

    def line_next(kind, chunk, position):
        block = CHUNKS[chunk][0]
        wait_line(chunk, position)
        if kind == "middle" and block not in DIRECT:
            goal = 2 if position == 0 else 0
            send(kind, lambda: line_copy(chunk, position, 0, goal))
        if block not in PAIRED or position in (0, 3):
            send(kind, lambda: side_copy(chunk, real(position)))

    def gathered(kind, block):
        if block == blocks - 1:
            for make in pending["all"]:
                make().wait_send()
            drain(kind)
        for chunk, entry in enumerate(CHUNKS):
            if entry[0] != block:
                continue
            paired = block in PAIRED
            if paired and kind == "edge":
                wait_line(chunk, 1)
                wait_line(chunk, 2)
            for position in (0, 3) if paired else range(LINE):
                wait_side(chunk, real(position))

    pieces = {
        "edge": ((1, 1, 3), (2, 2, 2), (3, 3, 1)),
        "middle": ((0, 0, 1), (0, 3, 1), (2, 2, 2), (2, 0, 1), (3, 3, 1)),
    }

    def columns(first, count):
        return pl.ds(
            pl.multiple_of((first + flip * (LINE - 2 * first - count)) * group, group),
            count * group,
        )

    def root_piece(piece, which):
        position, first, count = piece
        return left_full.at[:, span(real(position) * 2 + which), columns(first, count)]

    def send_root(kind, number, piece, goal, landing):
        send(
            kind,
            lambda: remote(
                root_piece(piece, side),
                root_piece(piece, side),
                root_send.at[number],
                root_recv.at[landing],
                at(goal),
            ),
        )

    def wait_root(kind, number):
        arrive(root_piece(pieces[kind][number], side), root_recv.at[number])

    def edge_roots():
        send_root("edge", 0, (0, 0, 1), 1, 0)
        send_root("edge", 1, (0, 3, 1), 1, 1)

    def middle_roots():
        send_root("middle", 0, (1, 0, 2), 2, 2)
        send_root("middle", 1, (1, 1, 3), 0, 0)
        send_root("middle", 2, (1, 3, 1), 2, 3)

    def middle_root(number):
        wait_root("middle", number)
        if number == 0:
            send_root("middle", 3, (0, 0, 1), 2, 4)
        if number == 2:
            send_root("middle", 4, (2, 2, 2), 0, 1)
        if number == 4:
            send_root("middle", 5, (3, 3, 1), 0, 2)
        if number == 1:
            wait_root("middle", 3)

    def edge_roots_next():
        for number in range(3):
            wait_root("edge", number)

    def root_side(kind, number):
        def make():
            if number == 0:
                where = left_full.at[:, span(me), :]
            else:
                where = root_piece(pieces[kind][number - 1], side)
            return remote(
                where, where, root_side_send.at[number], root_side_recv.at[number], partner
            )

        return make

    def wait_root_side(kind):
        arrive(left_full.at[:, span(place * 2 + 1 - side), :], root_side_recv.at[0])
        for number, piece in enumerate(pieces[kind]):
            arrive(root_piece(piece, 1 - side), root_side_recv.at[number + 1])

    def mirror(kind):
        tiles = [(1, 2), (1, 3), (2, 3)]
        if kind == "edge":
            tiles += [(0, 1), (0, 2), (0, 3)]
        else:
            tiles += [(1, 0), (2, 0), (0, 3)]
        for block in range(blocks):
            for row, column in tiles:
                value = left_full[block, pair_span(real(row)), columns(column, 1)]
                left_full[block, pair_span(real(column)), columns(row, 1)] = value.T

    def to_shards(step):
        peer = (shard + step) % shards
        return remote(
            stat_ref.at[peer],
            quarter_in.at[shard],
            part_send.at[step],
            part_recv.at[step],
            (me, peer),
        )

    def stat_side():
        where = stat_full.at[:, me, shard]
        return remote(where, where, stat_side_send.at[0], stat_side_recv.at[0], partner)

    def stat_rows(position):
        return stat_full.at[:, pl.ds(real(position) * 2, 2), shard]

    def stat_copy(position, way, goal):
        where = stat_rows(position)
        return remote(
            where,
            where,
            stat_send.at[real(position), way],
            stat_recv.at[real(position)],
            at(goal),
        )

    def wait_stat(position):
        arrive(stat_rows(position), stat_recv.at[real(position)])

    def send_quarters(kind):
        for step in range(1, shards):
            origin = (shard + shards - step) % shards
            arrive(quarter_in.at[origin], part_recv.at[step])
        stat_full[:, me, shard] = quarter_in[keeper]
        send(kind, stat_side)

    def stat_begin(kind):
        arrive(stat_full.at[:, place * 2 + (1 - side), shard], stat_side_recv.at[0])
        if kind == "edge":
            send(kind, lambda: stat_copy(0, 0, 1))
        else:
            send(kind, lambda: stat_copy(1, 0, 0))
            send(kind, lambda: stat_copy(1, 1, 2))

    def stat_next(position):
        wait_stat(position)
        goal = 2 if position == 0 else 0
        send("middle", lambda: stat_copy(position, 0, goal))

    def spread(number, owner, goal):
        where = stat_full.at[:, :, owner]
        return remote(
            where, where, spread_send.at[number], spread_recv.at[number], (me, goal)
        )

    def spread_quarters(kind):
        if kind == "edge":
            for position in (1, 2, 3):
                wait_stat(position)
        send(kind, lambda: spread(0, shard, other_row))
        send(kind, lambda: spread(1, shard, other_core))

    def spread_next(kind):
        arrive(stat_full.at[:, :, other_row], spread_recv.at[0])
        send(kind, lambda: spread(2, other_row, other_core))

    def spread_end():
        arrive(stat_full.at[:, :, other_core], spread_recv.at[1])
        arrive(
            stat_full.at[:, :, (other_core + 2) % shards], spread_recv.at[2]
        )

    tile = pair_span(place)

    def new_statistics(block):
        grad = grad_full[block].reshape(order, order)
        own = grad_full[block, place, side]
        left_out[block] = decay_rate * left_stat[local(block)] + dot(own, grad, (1, 1)) / order
        turned_rows = grad_full[block, :, :, :, tile].reshape(order, group).T
        own_turned = jnp.where(side == 0, turned_rows[:rows], turned_rows[rows:])
        right_out[block] = decay_rate * right_stat[local(block)] + dot(own_turned, grad) / order
        stores.append((left_out.at[block], left_new_ref.at[block], 0, block))
        stores.append((right_out.at[block], right_new_ref.at[block], 1, block))
        for entry in stores[-2:]:
            store(*entry).start()

    stores = []

    def store(source, target, kind, block):
        return pltpu.make_async_copy(source, target, store_sem.at[kind, block])

    def renew_begin(which):
        identity = (
            lax.broadcasted_iota(jnp.int32, (order, order), 0)
            == lax.broadcasted_iota(jnp.int32, (order, order), 1)
        ).astype(jnp.float32)
        grad = grad_full[0].reshape(order, order)
        if which == 0:
            turned[...] = grad.T
            product = dot(grad, turned[...])
        else:
            product = dot(turned[...], grad)
        old = stat_full[which].reshape(order, order).astype(jnp.float32)
        shifted = decay_rate * old + product / order + epsilon_shift * identity
        scale = 2.5 / jnp.sqrt(jnp.sum(shifted * shifted))
        start = scale * shifted
        moment[which] = start.astype(jnp.bfloat16)
        step = (5.0 * identity - start) * 0.25
        factor[which] = step.astype(jnp.bfloat16)
        current[which] = (jnp.sqrt(jnp.sqrt(scale)) * step).astype(jnp.bfloat16)

    def renew_square():
        for which in range(2):
            square[which] = dot(factor[which], factor[which]).astype(jnp.bfloat16)

    def renew_fourth():
        for which in range(2):
            factor[which] = dot(square[which], square[which]).astype(jnp.bfloat16)

    def renew_factor():
        identity = (
            lax.broadcasted_iota(jnp.int32, (order, order), 0)
            == lax.broadcasted_iota(jnp.int32, (order, order), 1)
        ).astype(jnp.float32)
        for which in range(2):
            value = dot(factor[which], moment[which])
            square[which] = ((5.0 * identity - value) * 0.25).astype(jnp.bfloat16)

    def renew_end():
        for which in range(2):
            moment[which] = dot(current[which], square[which]).astype(jnp.bfloat16)
        fresh_rows_out[...] = moment[0, span(me), :]
        stores.append((fresh_rows_out, fresh_rows_ref, 2, 0))
        stores.append((moment.at[1], fresh_right_ref, 2, 1))
        for entry in stores[-2:]:
            store(*entry).start()

    def direct(block):
        root = left_full[local(block)]
        other = right_full[local(block)]
        if block == 0:
            root = jnp.where(owns, moment[0], root)
            other = jnp.where(owns, moment[1], other)
        half = dot(root, grad_full[block].reshape(order, order)).astype(jnp.bfloat16)
        direction_out[block] = dot(half, other).astype(jnp.bfloat16)
        stores.append((direction_out.at[block], direction_ref.at[block], 3, block))
        store(*stores[-1]).start()

    @pl.when(edge)
    def _():
        send_across("edge", 0, (3, 2, 1, 0))
        send_across("edge", 1, (3, 2, 1, 0))

    @pl.when(middle)
    def _():
        send_across("middle", 0, (3, 2, 0, 1))
        send_across("middle", 1, (3, 2, 0, 1))
    for block in range(1, blocks):
        mine[block] = arrived[local(block)]
    loads[0].wait()
    loads[1].wait()
    part = rows // shards
    for index in range(shards):
        part_rows = pl.ds(index * part, part)
        stat_ref[index, 0] = left_stat[slot, part_rows, :].astype(jnp.bfloat16)
        stat_ref[index, 1] = right_stat[slot, part_rows, :].astype(jnp.bfloat16)
    for step in range(1, shards):
        send("all", lambda step=step: to_shards(step))
    quarter_in[shard] = stat_ref[shard]
    loads[3].wait()

    @pl.when(edge)
    def _():
        edge_roots()
        edge_far(0, 3)
        send_across("edge", 2, (3, 2, 1, 0))
        send_across("edge", 3, (3, 2, 1, 0))
        edge_far(0, 2)
        edge_far(0, 1)
        send_quarters("edge")
        edge_far(1, 3)
        edge_far(1, 2)
        edge_far(1, 1)
        edge_far(2, 3)
        send_across("edge", 4, (3, 2, 1, 0))
        send_across("edge", 5, (3, 2, 1, 0))
        edge_far(2, 2)
        edge_far(2, 1)
        edge_far(3, 3)
        edge_far(3, 2)
        edge_far(3, 1)
        stat_begin("edge")
        edge_far(4, 3)
        edge_roots_next()
        send("edge", root_side("edge", 1))
        send("edge", root_side("edge", 2))
        send("edge", root_side("edge", 3))
        edge_own(0)
        edge_far(5, 3)
        edge_own(1)
        take("edge", 0)
        line_next("edge", 0, 1)
        edge_own(2)
        take("edge", 1)
        edge_far(4, 2)
        edge_far(5, 2)
        line_next("edge", 0, 2)
        line_next("edge", 1, 1)
        send("edge", root_side("edge", 0))
        take("edge", 2)
        edge_own(3)
        edge_far(4, 1)
        edge_far(5, 1)
        line_next("edge", 1, 2)
        line_next("edge", 2, 1)
        spread_quarters("edge")
        take("edge", 3)
        edge_own(4)
        line_next("edge", 2, 2)
        wait_root_side("edge")
        mirror("edge")
        line_next("edge", 3, 1)
        edge_own(5)
        line_next("edge", 0, 3)
        line_next("edge", 1, 3)
        line_next("edge", 3, 2)
        spread_next("edge")
        gathered("edge", 0)
        line_next("edge", 2, 3)
        take("edge", 4)
        spread_end()
        line_next("edge", 4, 1)

    @pl.when(middle)
    def _():
        send_across("middle", 2, (3, 2, 0, 1))
        send_across("middle", 3, (3, 2, 0, 1))
        middle_roots()
        middle_root(0)
        send("middle", root_side("middle", 1))
        send_quarters("middle")
        middle_far(0, 3)
        send_across("middle", 4, (3, 2, 0, 1))
        send_across("middle", 5, (3, 2, 0, 1))
        middle_far(0, 2)
        middle_root(2)
        middle_root(1)
        middle_root(4)
        send("middle", root_side("middle", 4))
        middle_far(0, 0)
        middle_far(1, 3)
        middle_own(0)
        middle_far(1, 2)
        stat_begin("middle")
        middle_far(1, 0)
        middle_far(2, 3)
        take("middle", 0)
        middle_own(1)
        middle_far(2, 2)
        stat_next(2)
        middle_far(2, 0)
        middle_far(3, 3)
        line_next("middle", 0, 2)
        take("middle", 1)
        middle_far(3, 2)
        middle_own(2)
        send("middle", root_side("middle", 0))
        send("middle", root_side("middle", 2))
        send("middle", root_side("middle", 5))
        middle_far(3, 0)
        stat_next(0)
        line_next("middle", 1, 2)
        middle_far(4, 3)
        take("middle", 2)
        middle_own(3)
        middle_far(5, 3)
        stat_next(3)
        line_next("middle", 0, 0)
        spread_quarters("middle")
        line_next("middle", 1, 0)
        middle_far(4, 0)
        line_next("middle", 2, 2)
        middle_far(4, 2)
        take("middle", 3)
        middle_far(5, 0)
        middle_far(5, 2)
        line_next("middle", 0, 3)
        line_next("middle", 2, 0)
        line_next("middle", 1, 3)
        middle_own(4)
        line_next("middle", 3, 2)
        line_next("middle", 3, 0)
        middle_own(5)
        spread_next("middle")
        line_next("middle", 2, 3)
        gathered("middle", 0)
        send("middle", root_side("middle", 3))
        take("middle", 4)
        line_next("middle", 3, 3)
        spread_end()

    renew_begin(0)
    @pl.when(edge)
    def _():
        take("edge", 5)
        line_next("edge", 4, 2)
        line_next("edge", 3, 3)
        line_next("edge", 5, 1)

    @pl.when(middle)
    def _():
        take("middle", 5)

    renew_begin(1)
    @pl.when(edge)
    def _():
        line_next("edge", 5, 2)

    @pl.when(middle)
    def _():
        line_next("middle", 4, 2)

    renew_square()
    @pl.when(middle)
    def _():
        wait_root_side("middle")

    new_statistics(0)
    @pl.when(edge)
    def _():
        line_next("edge", 4, 3)

    @pl.when(middle)
    def _():
        line_next("middle", 5, 2)
        line_next("middle", 4, 0)
        gathered("middle", 1)

    renew_fourth()
    @pl.when(edge)
    def _():
        gathered("edge", 1)

    renew_factor()
    @pl.when(edge)
    def _():
        line_next("edge", 5, 3)

    @pl.when(middle)
    def _():
        line_next("middle", 4, 3)
        line_next("middle", 5, 0)

    renew_end()
    @pl.when(middle)
    def _():
        mirror("middle")
        line_next("middle", 5, 3)

    loads[4].wait()
    direct(0)
    direct(1)
    new_statistics(1)
    @pl.when(edge)
    def _():
        gathered("edge", 2)

    @pl.when(middle)
    def _():
        gathered("middle", 2)

    new_statistics(2)
    direct(2)
    both(lambda: drain("edge"), lambda: drain("middle"))
    for entry in stores:
        store(*entry).wait()


def exchange(owner_slot, refresh, grads, left_root, left_stat, right_stat, right_root, shards):
    blocks, order = grads.shape[1], grads.shape[2]
    reps = 2 * LINE
    rows = order // reps
    part = rows // shards
    chunks = len(CHUNKS)
    low = jnp.bfloat16
    wide = jnp.float32
    smem = pl.BlockSpec(memory_space=pltpu.SMEM)
    hbm = pl.BlockSpec(memory_space=pltpu.HBM)
    free = pl.BlockSpec(memory_space=pl.ANY)
    dma = pltpu.SemaphoreType.DMA
    return pl.pallas_call(
        exchange_kernel,
        out_shape=(
            jax.ShapeDtypeStruct((blocks, rows, order), wide),
            jax.ShapeDtypeStruct((blocks, rows, order), wide),
            jax.ShapeDtypeStruct((blocks, order, order), low),
            jax.ShapeDtypeStruct((rows, order), low),
            jax.ShapeDtypeStruct((order, order), low),
        ),
        in_specs=[hbm, smem] + [hbm] * 5,
        out_specs=(free,) * 5,
        scratch_shapes=[
            pltpu.SMEM(owner_slot.shape, owner_slot.dtype),
            pltpu.VMEM((blocks, order, order), low),
            pltpu.VMEM((blocks, order, order), low),
            pltpu.VMEM((blocks, rows, order), wide),
            pltpu.VMEM((blocks, rows, order), wide),
            pltpu.VMEM((blocks, order, order), low),
            pltpu.VMEM((blocks, order, order), low),
            pltpu.VMEM((blocks, LINE, 2, rows, order), low),
            pltpu.VMEM((shards, 2, part, order), low),
            pltpu.VMEM((shards, 2, part, order), low),
            pltpu.VMEM((2, reps, shards, part, order), low),
            pltpu.VMEM((blocks, LINE, rows, order), low),
            pltpu.VMEM((blocks, 3, rows, order), wide),
            pltpu.VMEM((blocks, 3, rows, order), wide),
            pltpu.VMEM((blocks, 2, rows, order), wide),
            pltpu.VMEM((blocks, rows, order), low),
            pltpu.VMEM((blocks, shards, rows, order), low),
            pltpu.VMEM((order, order), low),
            pltpu.VMEM((2, order, order), low),
            pltpu.VMEM((2, order, order), low),
            pltpu.VMEM((2, order, order), low),
            pltpu.VMEM((2, order, order), low),
            pltpu.VMEM((blocks, rows, order), wide),
            pltpu.VMEM((blocks, rows, order), wide),
            pltpu.VMEM((blocks, order, order), low),
            pltpu.VMEM((rows, order), low),
            dma((6,)),
            dma((4, blocks)),
            dma((chunks, LINE)),
            dma((chunks, LINE)),
            dma((chunks, 3)),
            dma((chunks, 3)),
            dma((chunks, 2)),
            dma((chunks, 3)),
            dma((chunks, 3)),
            dma((shards,)),
            dma((shards,)),
            dma((LINE, 2)),
            dma((LINE,)),
            dma((1,)),
            dma((1,)),
            dma((3,)),
            dma((3,)),
            dma((6,)),
            dma((5,)),
            dma((6,)),
            dma((6,)),
            dma((chunks, LINE, 3)),
            dma((chunks, LINE)),
            dma((chunks, LINE)),
            dma((chunks, LINE)),
        ],
        compiler_params=pltpu.CompilerParams(
            collective_id=0, has_side_effects=True, vmem_limit_bytes=48 * 2**20
        ),
    )(
        fixed(owner_slot),
        refresh,
        *map(fixed, (grads, left_root, left_stat, right_stat, right_root)),
    )


def fixed(array):
    return pltpu.with_memory_space_constraint(array, pltpu.HBM)


def arrange_kernel(
    slots_ref,
    refresh_ref,
    left_in,
    right_in,
    direction_in,
    fresh_rows,
    fresh_right,
    left_root,
    right_root,
    left_new,
    right_new,
    left_root_new,
    right_root_new,
    direction,
    sems,
):
    blocks = left_in.shape[0]
    fresh_slot = slots_ref[refresh_ref[0]]
    slot = fresh_slot % blocks
    owns = fresh_slot // blocks == lax.axis_index("shard")
    copies = []

    def copy(source, target):
        copies.append(pltpu.make_async_copy(source, target, sems.at[len(copies)]))
        copies[-1].start()

    for block in range(blocks):
        where = (slot + block) % blocks
        copy(direction_in.at[block], direction.at[where])
        copy(left_in.at[block], left_new.at[where])
        copy(right_in.at[block], right_new.at[where])
        if block > 0:
            copy(right_root.at[where], right_root_new.at[where])
            copy(left_root.at[where], left_root_new.at[where])
    last = len(copies)

    @pl.when(owns)
    def _():
        pltpu.make_async_copy(fresh_right, right_root_new.at[slot], sems.at[last]).start()
        pltpu.make_async_copy(fresh_rows, left_root_new.at[slot], sems.at[last + 1]).start()

    @pl.when(jnp.logical_not(owns))
    def _():
        pltpu.make_async_copy(
            right_root.at[slot], right_root_new.at[slot], sems.at[last]
        ).start()
        pltpu.make_async_copy(
            left_root.at[slot], left_root_new.at[slot], sems.at[last + 1]
        ).start()

    pltpu.make_async_copy(fresh_right, right_root_new.at[slot], sems.at[last]).wait()
    pltpu.make_async_copy(fresh_rows, left_root_new.at[slot], sems.at[last + 1]).wait()
    for item in copies:
        item.wait()


def arrange(*operands):
    stat, root, right = operands[2], operands[7], operands[8]
    smem = pl.BlockSpec(memory_space=pltpu.SMEM)
    hbm = pl.BlockSpec(memory_space=pl.ANY)
    return pl.pallas_call(
        arrange_kernel,
        out_shape=(
            jax.ShapeDtypeStruct(stat.shape, stat.dtype),
            jax.ShapeDtypeStruct(stat.shape, stat.dtype),
            jax.ShapeDtypeStruct(root.shape, root.dtype),
            jax.ShapeDtypeStruct(right.shape, right.dtype),
            jax.ShapeDtypeStruct(right.shape, right.dtype),
        ),
        in_specs=[smem, smem] + [hbm] * 7,
        out_specs=(hbm,) * 5,
        scratch_shapes=[pltpu.SemaphoreType.DMA((5 * stat.shape[0],))],
        compiler_params=pltpu.CompilerParams(vmem_limit_bytes=2**20),
    )(*operands)


def direct_body(grads, owner_slot, refresh, left_stat, right_stat, left_root, right_root):
    results = exchange(
        owner_slot,
        refresh,
        grads,
        left_root,
        left_stat,
        right_stat,
        right_root,
        lax.axis_size("shard"),
    )
    return arrange(owner_slot, refresh, *results, left_root, right_root)


def choose(mesh, *arrays):
    reps, shards = mesh.shape["rep"], mesh.shape["shard"]
    rows = arrays[0].shape[2] // reps
    blocks = arrays[0].shape[1] // shards
    finest = 16 * max(shards, *(entry[2] for entry in CHUNKS))
    direct = (reps, shards, blocks) == (2 * LINE, 4, 3) and rows % finest == 0
    return direct_body if direct else body


def solution(mesh):
    def run(*arrays):
        return mapped(mesh, choose(mesh, *arrays))(*arrays)

    return run


def mapped(mesh, body):
    return jax.shard_map(
        body,
        mesh=mesh,
        in_specs=(
            P("rep", "shard", None, None),
            P(),
            P(),
            P("shard", "rep", None),
            P("shard", "rep", None),
            P("shard", "rep", None),
            P("shard", None, None),
        ),
        out_specs=(
            P("shard", "rep", None),
            P("shard", "rep", None),
            P("shard", "rep", None),
            P("shard", None, None),
            P("shard", None, None),
        ),
        check_vma=False,
    )
```

```python
import functools

import jax
import jax.numpy as jnp
from jax import lax
from jax.experimental import pallas as pl
from jax.experimental.pallas import tpu as pltpu
from jax.sharding import PartitionSpec as P

ITERS = 2


decay_rate = 0.95
epsilon_shift = 1e-06


def inverse_root(statistic):
    order = statistic.shape[0]
    identity = (
        lax.broadcasted_iota(jnp.int32, (order, order), 0)
        == lax.broadcasted_iota(jnp.int32, (order, order), 1)
    ).astype(jnp.float32)
    shifted = statistic + epsilon_shift * identity
    norm_scale = 2.5 / jnp.sqrt(jnp.sum(shifted * shifted))
    moment = norm_scale * shifted
    current = identity
    for number in range(ITERS):
        factor = (5.0 * identity - moment) * 0.25
        factor_low = factor.astype(jnp.bfloat16)
        if number == 0:
            current = jnp.sqrt(jnp.sqrt(norm_scale)) * factor
        else:
            current = jnp.dot(
                current.astype(jnp.bfloat16), factor_low, preferred_element_type=jnp.float32
            )
        if number + 1 < ITERS:
            square = jnp.dot(factor_low, factor_low, preferred_element_type=jnp.float32).astype(
                jnp.bfloat16
            )
            fourth = jnp.dot(square, square, preferred_element_type=jnp.float32).astype(
                jnp.bfloat16
            )
            moment = jnp.dot(
                fourth, moment.astype(jnp.bfloat16), preferred_element_type=jnp.float32
            )
    return current.astype(jnp.bfloat16)


def both_roots(fresh_whole):
    return (inverse_root(fresh_whole[0]), inverse_root(fresh_whole[1]))


def empty_roots(fresh_whole):
    blank = jnp.zeros(fresh_whole.shape[1:], jnp.bfloat16)
    return (blank, blank)


def body(grads, owner_slot, refresh, left_stat, right_stat, left_root, right_root):
    blocks = grads.shape[1]
    block_order = grads.shape[2]
    rep_count = lax.axis_size("rep")
    shards = lax.axis_size("shard")
    row_count = block_order // rep_count
    rep_index = lax.axis_index("rep")
    shard_index = lax.axis_index("shard")
    partial_value = grads[0].astype(jnp.float32)
    row_share = lax.psum_scatter(partial_value, "rep", scatter_dimension=1, tiled=True)
    row_share = row_share.astype(jnp.bfloat16)
    slot_table = owner_slot.reshape(shards, blocks)
    own_slots = lax.dynamic_index_in_dim(slot_table, shard_index, 0, keepdims=False)
    targets = own_slots // blocks
    selector = (targets[None, :] == jnp.arange(shards, dtype=jnp.int32)[:, None]).astype(
        jnp.bfloat16
    )
    outgoing = jnp.einsum(
        "ok,krc->orc", selector, row_share, preferred_element_type=jnp.float32
    ).astype(jnp.bfloat16)
    incoming = lax.all_to_all(outgoing, "shard", split_axis=0, concat_axis=0, tiled=True)
    wanted = shard_index * blocks + jnp.arange(blocks, dtype=jnp.int32)
    receiver = (jnp.transpose(slot_table) == wanted[:, None]).astype(jnp.bfloat16)
    owned_rows = jnp.einsum(
        "ks,src->krc", receiver, incoming, preferred_element_type=jnp.float32
    ).astype(jnp.bfloat16)
    gathered = lax.all_gather(owned_rows, "rep", axis=1, tiled=True)
    left_new = (
        decay_rate * left_stat
        + jnp.einsum("krc,kjc->krj", owned_rows, gathered, preferred_element_type=jnp.float32)
        / block_order
    )
    column_share = lax.dynamic_slice_in_dim(gathered, rep_index * row_count, row_count, 2)
    right_new = (
        decay_rate * right_stat
        + jnp.einsum("kic,kij->kcj", column_share, gathered, preferred_element_type=jnp.float32)
        / block_order
    )
    fresh_slot = owner_slot[refresh[0]]
    holder = fresh_slot // blocks
    slot_index = fresh_slot % blocks
    owns_fresh = holder == shard_index
    fresh_pair = jnp.stack(
        [
            lax.dynamic_index_in_dim(left_new, slot_index, 0, keepdims=False),
            lax.dynamic_index_in_dim(right_new, slot_index, 0, keepdims=False),
        ]
    )
    fresh_whole = lax.all_gather(fresh_pair, "rep", axis=1, tiled=True)
    fresh_left, fresh_right = lax.cond(owns_fresh, both_roots, empty_roots, fresh_whole)
    fresh_rows = lax.dynamic_slice_in_dim(fresh_left, rep_index * row_count, row_count, 0)
    left_updated = lax.dynamic_update_index_in_dim(left_root, fresh_rows, slot_index, 0)
    left_root_new = jnp.where(owns_fresh, left_updated, left_root)
    right_updated = lax.dynamic_update_index_in_dim(right_root, fresh_right, slot_index, 0)
    right_root_new = jnp.where(owns_fresh, right_updated, right_root)
    half_step = jnp.einsum(
        "kri,kic->krc", left_root_new, gathered, preferred_element_type=jnp.float32
    ).astype(jnp.bfloat16)
    preconditioned = jnp.einsum(
        "kri,kic->krc", half_step, right_root_new, preferred_element_type=jnp.float32
    ).astype(jnp.bfloat16)
    direction = lax.all_gather(preconditioned, "rep", axis=1, tiled=True)
    return (left_new, right_new, left_root_new, right_root_new, direction)


MESH = pl.DeviceIdType.MESH
LINE = 4
CHUNKS = ((0, 0, 2, True), (0, 1, 2, True), (1, 0, 2, True), (1, 1, 2, False), (2, 0, 2, False), (2, 1, 2, False))
DIRECT = (2,)
PAIRED = ()


def dot(left, right, dims=(1, 0)):
    return lax.dot_general(
        left, right, (((dims[0],), (dims[1],)), ((), ())), preferred_element_type=jnp.float32
    )


def exchange_kernel(
    slots_in,
    refresh_ref,
    grads_ref,
    left_ref,
    left_stat_ref,
    right_stat_ref,
    right_ref,
    left_new_ref,
    right_new_ref,
    direction_ref,
    fresh_rows_ref,
    fresh_right_ref,
    slots_ref,
    arrived,
    mine,
    left_stat,
    right_stat,
    right_full,
    left_full,
    grad_full,
    stat_ref,
    quarter_in,
    stat_full,
    across,
    partial_out,
    from_outer,
    from_inner,
    share,
    incoming,
    turned,
    moment,
    factor,
    current,
    square,
    load_sem,
    across_send,
    across_recv,
    partial_send,
    outer_recv,
    inner_recv,
    swap_send,
    swap_recv,
    part_send,
    part_recv,
    stat_send,
    stat_recv,
    stat_side_send,
    stat_side_recv,
    spread_send,
    spread_recv,
    root_send,
    root_recv,
    root_side_send,
    root_side_recv,
    line_send,
    line_recv,
    side_send,
    side_recv,
):
    blocks, order = mine.shape[0], mine.shape[1]
    rows = order // (2 * LINE)
    group = 2 * rows
    shards = stat_ref.shape[0]
    me = lax.axis_index("rep")
    shard = lax.axis_index("shard")
    place = me // 2
    side = me % 2
    other_row = (shard + 2) % shards
    other_core = shard + 1 - 2 * (shard % 2)
    partner = (place * 2 + (1 - side), shard)
    flip = place // (LINE // 2)
    middle = (place == 1) | (place == 2)
    edge = jnp.logical_not(middle)

    def real(position):
        return position + flip * (LINE - 1 - 2 * position)

    def at(position):
        return (real(position) * 2 + side, shard)

    def span(index):
        return pl.ds(pl.multiple_of(index * rows, rows), rows)

    def pair_span(index):
        return pl.ds(pl.multiple_of(index * group, group), group)

    loads = [
        pltpu.make_async_copy(left_stat_ref, left_stat, load_sem.at[0]),
        pltpu.make_async_copy(right_stat_ref, right_stat, load_sem.at[1]),
        pltpu.make_async_copy(grads_ref.at[0], arrived, load_sem.at[2]),
        pltpu.make_async_copy(left_ref, left_full.at[:, span(me), :], load_sem.at[3]),
        pltpu.make_async_copy(right_ref, right_full, load_sem.at[4]),
        pltpu.make_async_copy(slots_in, slots_ref, load_sem.at[5]),
    ]
    barrier = pltpu.get_barrier_semaphore()
    for step in range(1, LINE):
        pl.semaphore_signal(
            barrier,
            inc=1,
            device_id=((place + step) % LINE * 2 + side, shard),
            device_id_type=MESH,
        )
    pl.semaphore_signal(barrier, inc=1, device_id=partner, device_id_type=MESH)
    for step in range(1, shards):
        pl.semaphore_signal(
            barrier, inc=1, device_id=(me, (shard + step) % shards), device_id_type=MESH
        )
    loads[5].start()
    loads[2].start()
    loads[5].wait()
    slot = slots_ref[refresh_ref[0]] % blocks
    keeper = slots_ref[refresh_ref[0]] // blocks
    owns = keeper == shard

    def local(block):
        return (slot + block) % blocks

    loads[2].wait()
    for index in (0, 1, 3):
        loads[index].start()
    mine[0] = arrived[local(0)]
    pl.semaphore_wait(barrier, LINE - 1 + 1 + shards - 1)

    pending = {"all": [], "edge": [], "middle": []}

    def remote(src, dst, send_sem, recv_sem, device):
        return pltpu.make_async_remote_copy(
            src_ref=src,
            dst_ref=dst,
            send_sem=send_sem,
            recv_sem=recv_sem,
            device_id=device,
            device_id_type=MESH,
        )

    def send(kind, make):
        make().start()
        pending[kind].append(make)

    def drain(kind):
        for make in pending[kind]:
            make().wait_send()
        pending[kind] = []

    def arrive(dst, recv_sem):
        remote(dst, dst, recv_sem, recv_sem, partner).wait_recv()

    def both(on_edge, on_middle):
        pl.when(edge)(on_edge)
        pl.when(middle)(on_middle)

    def cells(chunk):
        block, number, count, _ = CHUNKS[chunk]
        size = rows // count
        return block, pl.ds(number * size, size)

    def span_of(chunk, index):
        block, number, count, _ = CHUNKS[chunk]
        size = rows // count
        first = index * rows + number * size
        return block, pl.ds(pl.multiple_of(first, size), size)

    def across_copy(chunk, target):
        block, there = span_of(chunk, target * 2 + (1 - side))
        block, here = cells(chunk)
        return remote(
            mine.at[block, there, :],
            across.at[block, target, here],
            across_send.at[chunk, target],
            across_recv.at[chunk, target],
            partner,
        )

    def send_across(kind, chunk, positions):
        for position in positions:
            send(kind, lambda p=position: across_copy(chunk, real(p)))

    def pair_sum(chunk, position):
        target = real(position)
        block, here = cells(chunk)
        arrive(across.at[block, target, here], across_recv.at[chunk, target])
        own = mine[span_of(chunk, target * 2 + side)].astype(jnp.float32)
        return own + across[block, target, here].astype(jnp.float32)

    def wait_outer(chunk, number):
        block, here = cells(chunk)
        arrive(from_outer.at[block, number, here], outer_recv.at[chunk, number])
        return from_outer[block, number, here]

    def wait_inner(chunk, number):
        block, here = cells(chunk)
        arrive(from_inner.at[block, number, here], inner_recv.at[chunk, number])
        return from_inner[block, number, here]

    def edge_far(chunk, position):
        number = position - 1
        block, here = cells(chunk)
        partial_out[block, number, here] = pair_sum(chunk, position)
        send(
            "edge",
            lambda: remote(
                partial_out.at[block, number, here],
                from_outer.at[block, number, here],
                partial_send.at[chunk, number],
                outer_recv.at[chunk, number],
                at(1),
            ),
        )

    def middle_far(chunk, position):
        number = {3: 0, 2: 1, 0: 2, 1: 3}[position]
        block, here = cells(chunk)
        if position < 2:
            earlier = wait_inner(chunk, position)
            goal, landing = 0, position
        else:
            earlier = wait_outer(chunk, position - 1)
            goal, landing = 2, number
        partial_out[block, number, here] = pair_sum(chunk, position) + earlier
        send(
            "middle",
            lambda: remote(
                partial_out.at[block, number, here],
                from_inner.at[block, landing, here],
                partial_send.at[chunk, number],
                inner_recv.at[chunk, landing],
                at(goal),
            ),
        )

    def swap_rows(chunk, owner):
        block, here = cells(chunk)
        return incoming.at[block, owner, groups(chunk), here]

    def at_ends(chunk):
        return CHUNKS[chunk][3]

    def groups(chunk):
        return slice(None) if at_ends(chunk) else 0

    others = ((other_core + 2) % shards, other_row, other_core)

    def swap(kind, chunk, *totals):
        block, here = cells(chunk)
        for number, total in enumerate(totals):
            value = total.astype(jnp.bfloat16)
            share[block, number, here] = value
            incoming[block, shard, number, here] = value
        for number, goal in enumerate(others):
            send(
                kind,
                lambda n=number, g=goal: remote(
                    share.at[block, groups(chunk), here],
                    swap_rows(chunk, shard),
                    swap_send.at[chunk, n],
                    swap_recv.at[chunk, n],
                    (me, g),
                ),
            )

    def edge_own(chunk):
        positions = (0, 1) if at_ends(chunk) else (0,)
        swap("edge", chunk, *(pair_sum(chunk, p) + wait_inner(chunk, p) for p in positions))

    def middle_own(chunk):
        total = pair_sum(chunk, 1) + wait_inner(chunk, 1)
        swap("middle", chunk, total + wait_outer(chunk, 0))

    def share_rows(chunk, source, which):
        block, here = cells(chunk)
        if at_ends(chunk):
            half = LINE // 2
            return grad_full.at[block, pl.ds(source // half * half, half), which, here]
        return grad_full.at[block, source, which, here]

    def side_copy(chunk, source):
        where = share_rows(chunk, source, side)
        return remote(
            where, where, side_send.at[chunk, source], side_recv.at[chunk, source], partner
        )

    def wait_side(chunk, source):
        arrive(share_rows(chunk, source, 1 - side), side_recv.at[chunk, source])

    def line_rows(chunk, position):
        if CHUNKS[chunk][0] in PAIRED and position in (1, 2):
            return share_rows(chunk, real(position), slice(None))
        return share_rows(chunk, real(position), side)

    def line_copy(chunk, position, way, goal):
        where = line_rows(chunk, position)
        return remote(
            where,
            where,
            line_send.at[chunk, real(position), way],
            line_recv.at[chunk, real(position)],
            at(goal),
        )

    def take(kind, chunk):
        for number, origin in enumerate(others):
            arrive(swap_rows(chunk, origin), swap_recv.at[chunk, number])
        block, here = cells(chunk)
        wanted = shard * blocks + local(block)
        for number in range(2 if at_ends(chunk) else 1):
            value = incoming[block, 0, number, here]
            for origin in range(1, shards):
                held = slots_ref[origin * blocks + local(block)] == wanted
                value = jnp.where(held, incoming[block, origin, number, here], value)
            group_place = real(number) if at_ends(chunk) else place
            grad_full[block, group_place, side, here] = value
        paired = block in PAIRED and kind == "middle"
        if not paired:
            line_begin(kind, chunk)
        send(kind, lambda: side_copy(chunk, place))
        if block in DIRECT:
            own, near, far = (0, 1, (2, 3)) if kind == "edge" else (1, 2, (3,))
            for way, goal in enumerate(far):
                send(kind, lambda w=way, g=goal: line_copy(chunk, own, near + w, g))

    def line_begin(kind, chunk):
        if CHUNKS[chunk][0] in PAIRED and kind == "middle":
            wait_side(chunk, place)
        if kind == "edge":
            send(kind, lambda: line_copy(chunk, 0, 0, 1))
        else:
            send(kind, lambda: line_copy(chunk, 1, 0, 0))
            send(kind, lambda: line_copy(chunk, 1, 1, 2))

    def wait_line(chunk, position):
        arrive(line_rows(chunk, position), line_recv.at[chunk, real(position)])

    def line_next(kind, chunk, position):
        block = CHUNKS[chunk][0]
        wait_line(chunk, position)
        if kind == "middle" and block not in DIRECT:
            goal = 2 if position == 0 else 0
            send(kind, lambda: line_copy(chunk, position, 0, goal))
        if block not in PAIRED or position in (0, 3):
            send(kind, lambda: side_copy(chunk, real(position)))

    def gathered(kind, block):
        if block == blocks - 1:
            for make in pending["all"]:
                make().wait_send()
            drain(kind)
        for chunk, entry in enumerate(CHUNKS):
            if entry[0] != block:
                continue
            paired = block in PAIRED
            if paired and kind == "edge":
                wait_line(chunk, 1)
                wait_line(chunk, 2)
            for position in (0, 3) if paired or entry[3] else range(LINE):
                wait_side(chunk, real(position))

    pieces = {
        "edge": ((1, 1, 3), (2, 2, 2), (3, 3, 1)),
        "middle": ((0, 0, 1), (0, 3, 1), (2, 2, 2), (2, 0, 1), (3, 3, 1)),
    }

    def columns(first, count):
        return pl.ds(
            pl.multiple_of((first + flip * (LINE - 2 * first - count)) * group, group),
            count * group,
        )

    def root_piece(piece, which):
        position, first, count = piece
        return left_full.at[:, span(real(position) * 2 + which), columns(first, count)]

    def send_root(kind, number, piece, goal, landing):
        send(
            kind,
            lambda: remote(
                root_piece(piece, side),
                root_piece(piece, side),
                root_send.at[number],
                root_recv.at[landing],
                at(goal),
            ),
        )

    def wait_root(kind, number):
        arrive(root_piece(pieces[kind][number], side), root_recv.at[number])

    def edge_roots():
        send_root("edge", 0, (0, 0, 1), 1, 0)
        send_root("edge", 1, (0, 3, 1), 1, 1)

    def middle_roots():
        send_root("middle", 0, (1, 0, 2), 2, 2)
        send_root("middle", 1, (1, 1, 3), 0, 0)
        send_root("middle", 2, (1, 3, 1), 2, 3)

    def middle_root(number):
        wait_root("middle", number)
        if number == 0:
            send_root("middle", 3, (0, 0, 1), 2, 4)
        if number == 2:
            send_root("middle", 4, (2, 2, 2), 0, 1)
        if number == 4:
            send_root("middle", 5, (3, 3, 1), 0, 2)
        if number == 1:
            wait_root("middle", 3)

    def edge_roots_next():
        for number in range(3):
            wait_root("edge", number)

    def root_side(kind, number):
        def make():
            if number == 0:
                where = left_full.at[:, span(me), :]
            else:
                where = root_piece(pieces[kind][number - 1], side)
            return remote(
                where, where, root_side_send.at[number], root_side_recv.at[number], partner
            )

        return make

    def wait_root_side(kind):
        arrive(left_full.at[:, span(place * 2 + 1 - side), :], root_side_recv.at[0])
        for number, piece in enumerate(pieces[kind]):
            arrive(root_piece(piece, 1 - side), root_side_recv.at[number + 1])

    def mirror(kind):
        tiles = [(1, 2), (1, 3), (2, 3)]
        if kind == "edge":
            tiles += [(0, 1), (0, 2), (0, 3)]
        else:
            tiles += [(1, 0), (2, 0), (0, 3)]
        for block in range(blocks):
            for row, column in tiles:
                value = left_full[block, pair_span(real(row)), columns(column, 1)]
                left_full[block, pair_span(real(column)), columns(row, 1)] = value.T

    def to_shards(step):
        peer = (shard + step) % shards
        return remote(
            stat_ref.at[peer],
            quarter_in.at[shard],
            part_send.at[step],
            part_recv.at[step],
            (me, peer),
        )

    def stat_side():
        where = stat_full.at[:, me, shard]
        return remote(where, where, stat_side_send.at[0], stat_side_recv.at[0], partner)

    def stat_rows(position):
        return stat_full.at[:, pl.ds(real(position) * 2, 2), shard]

    def stat_copy(position, way, goal):
        where = stat_rows(position)
        return remote(
            where,
            where,
            stat_send.at[real(position), way],
            stat_recv.at[real(position)],
            at(goal),
        )

    def wait_stat(position):
        arrive(stat_rows(position), stat_recv.at[real(position)])

    def send_quarters(kind):
        for step in range(1, shards):
            origin = (shard + shards - step) % shards
            arrive(quarter_in.at[origin], part_recv.at[step])
        stat_full[:, me, shard] = quarter_in[keeper]
        send(kind, stat_side)

    def stat_begin(kind):
        arrive(stat_full.at[:, place * 2 + (1 - side), shard], stat_side_recv.at[0])
        if kind == "edge":
            send(kind, lambda: stat_copy(0, 0, 1))
        else:
            send(kind, lambda: stat_copy(1, 0, 0))
            send(kind, lambda: stat_copy(1, 1, 2))

    def stat_next(position):
        wait_stat(position)
        goal = 2 if position == 0 else 0
        send("middle", lambda: stat_copy(position, 0, goal))

    def spread(number, owner, goal):
        where = stat_full.at[:, :, owner]
        return remote(
            where, where, spread_send.at[number], spread_recv.at[number], (me, goal)
        )

    def spread_quarters(kind):
        if kind == "edge":
            for position in (1, 2, 3):
                wait_stat(position)
        send(kind, lambda: spread(0, shard, other_row))
        send(kind, lambda: spread(1, shard, other_core))

    def spread_next(kind):
        arrive(stat_full.at[:, :, other_row], spread_recv.at[0])
        send(kind, lambda: spread(2, other_row, other_core))

    def spread_end():
        arrive(stat_full.at[:, :, other_core], spread_recv.at[1])
        arrive(
            stat_full.at[:, :, (other_core + 2) % shards], spread_recv.at[2]
        )

    tile = pair_span(place)

    def new_statistics(block):
        grad = grad_full[block].reshape(order, order)
        own = grad_full[block, place, side]
        left_new_ref[block] = decay_rate * left_stat[local(block)] + dot(own, grad, (1, 1)) / order
        turned_rows = grad_full[block, :, :, :, tile].reshape(order, group).T
        own_turned = jnp.where(side == 0, turned_rows[:rows], turned_rows[rows:])
        right_new_ref[block] = decay_rate * right_stat[local(block)] + dot(own_turned, grad) / order

    def renew_begin(which):
        identity = (
            lax.broadcasted_iota(jnp.int32, (order, order), 0)
            == lax.broadcasted_iota(jnp.int32, (order, order), 1)
        ).astype(jnp.float32)
        grad = grad_full[0].reshape(order, order)
        if which == 0:
            turned[...] = grad.T
            product = dot(grad, turned[...])
        else:
            product = dot(turned[...], grad)
        old = stat_full[which].reshape(order, order).astype(jnp.float32)
        shifted = decay_rate * old + product / order + epsilon_shift * identity
        scale = 2.5 / jnp.sqrt(jnp.sum(shifted * shifted))
        start = scale * shifted
        moment[which] = start.astype(jnp.bfloat16)
        step = (5.0 * identity - start) * 0.25
        factor[which] = step.astype(jnp.bfloat16)
        current[which] = (jnp.sqrt(jnp.sqrt(scale)) * step).astype(jnp.bfloat16)

    def renew_square():
        for which in range(2):
            square[which] = dot(factor[which], factor[which]).astype(jnp.bfloat16)

    def renew_fourth():
        for which in range(2):
            factor[which] = dot(square[which], square[which]).astype(jnp.bfloat16)

    def renew_factor():
        identity = (
            lax.broadcasted_iota(jnp.int32, (order, order), 0)
            == lax.broadcasted_iota(jnp.int32, (order, order), 1)
        ).astype(jnp.float32)
        for which in range(2):
            value = dot(factor[which], moment[which])
            square[which] = ((5.0 * identity - value) * 0.25).astype(jnp.bfloat16)

    def renew_end():
        moment[0] = dot(current[0], square[0]).astype(jnp.bfloat16)
        fresh_right_ref[...] = dot(current[1], square[1]).astype(jnp.bfloat16)
        fresh_rows_ref[...] = moment[0, span(me), :]

    def direct(block):
        root = left_full[local(block)]
        other = right_full[local(block)]
        if block == 0:
            root = jnp.where(owns, moment[0], root)
            other = jnp.where(owns, fresh_right_ref[...], other)
        half = dot(root, grad_full[block].reshape(order, order)).astype(jnp.bfloat16)
        direction_ref[block] = dot(half, other).astype(jnp.bfloat16)

    @pl.when(edge)
    def _():
        send_across("edge", 0, (3, 2, 1, 0))
        send_across("edge", 1, (3, 2, 1, 0))

    @pl.when(middle)
    def _():
        send_across("middle", 0, (3, 2, 0, 1))
        send_across("middle", 1, (3, 2, 0, 1))
    for block in range(1, blocks):
        mine[block] = arrived[local(block)]
    loads[0].wait()
    loads[1].wait()
    part = rows // shards
    for index in range(shards):
        part_rows = pl.ds(index * part, part)
        stat_ref[index, 0] = left_stat[slot, part_rows, :].astype(jnp.bfloat16)
        stat_ref[index, 1] = right_stat[slot, part_rows, :].astype(jnp.bfloat16)
    for step in range(1, shards):
        send("all", lambda step=step: to_shards(step))
    quarter_in[shard] = stat_ref[shard]
    loads[3].wait()
    loads[4].start()

    @pl.when(edge)
    def _():
        edge_roots()
        edge_far(0, 3)
        send_across("edge", 2, (3, 2, 1, 0))
        send_across("edge", 3, (3, 2, 1, 0))
        edge_far(0, 2)
        send_quarters("edge")
        edge_far(1, 3)
        edge_far(1, 2)
        edge_far(2, 3)
        send_across("edge", 4, (3, 2, 1, 0))
        send_across("edge", 5, (3, 2, 1, 0))
        edge_far(2, 2)
        edge_far(3, 3)
        edge_far(3, 2)
        edge_far(3, 1)
        edge_roots_next()
        send("edge", root_side("edge", 1))
        stat_begin("edge")
        edge_far(4, 3)
        edge_far(4, 2)
        edge_own(0)
        edge_far(5, 3)
        edge_far(5, 2)
        edge_own(1)
        send("edge", root_side("edge", 0))
        take("edge", 0)
        edge_own(2)
        take("edge", 1)
        edge_own(3)
        edge_far(4, 1)
        edge_far(5, 1)
        spread_quarters("edge")
        send("edge", root_side("edge", 2))
        send("edge", root_side("edge", 3))
        edge_own(4)
        take("edge", 2)
        line_next("edge", 3, 1)
        take("edge", 3)
        edge_own(5)
        line_next("edge", 3, 2)
        wait_root_side("edge")
        mirror("edge")
        line_next("edge", 0, 3)
        spread_next("edge")
        line_next("edge", 1, 3)
        take("edge", 4)
        spread_end()
        line_next("edge", 4, 1)
        take("edge", 5)
        line_next("edge", 4, 2)
        line_next("edge", 5, 1)
        gathered("edge", 0)

    @pl.when(middle)
    def _():
        send_across("middle", 2, (3, 2, 0, 1))
        send_across("middle", 3, (3, 2, 0, 1))
        middle_roots()
        middle_root(0)
        send("middle", root_side("middle", 1))
        send_quarters("middle")
        middle_far(0, 3)
        middle_root(2)
        send("middle", root_side("middle", 0))
        middle_root(1)
        middle_far(0, 2)
        send("middle", root_side("middle", 4))
        middle_root(4)
        middle_far(1, 3)
        middle_far(0, 0)
        middle_far(1, 2)
        middle_far(0, 1)
        middle_far(2, 3)
        middle_far(1, 0)
        middle_far(2, 2)
        stat_begin("middle")
        middle_far(1, 1)
        send_across("middle", 4, (3, 2, 0, 1))
        send_across("middle", 5, (3, 2, 0, 1))
        middle_far(3, 3)
        middle_far(3, 2)
        middle_far(2, 0)
        middle_far(2, 1)
        send("middle", root_side("middle", 5))
        stat_next(2)
        stat_next(0)
        middle_far(3, 0)
        middle_far(4, 3)
        middle_own(3)
        middle_far(4, 2)
        stat_next(3)
        spread_quarters("middle")
        middle_far(5, 3)
        middle_far(4, 0)
        middle_far(5, 2)
        take("middle", 3)
        send("middle", root_side("middle", 2))
        line_next("middle", 0, 0)
        send("middle", root_side("middle", 3))
        middle_far(5, 0)
        line_next("middle", 1, 0)
        line_next("middle", 3, 2)
        middle_own(4)
        line_next("middle", 0, 3)
        spread_next("middle")
        middle_own(5)
        line_next("middle", 1, 3)
        line_next("middle", 2, 0)
        wait_root_side("middle")
        spread_end()
        line_next("middle", 3, 0)
        take("middle", 4)
        mirror("middle")
        take("middle", 5)
        line_next("middle", 2, 3)
        line_next("middle", 3, 3)
        line_next("middle", 4, 2)
        gathered("middle", 0)

    renew_begin(0)
    @pl.when(edge)
    def _():
        line_next("edge", 5, 2)

    renew_begin(1)
    @pl.when(edge)
    def _():
        line_next("edge", 2, 3)

    @pl.when(middle)
    def _():
        line_next("middle", 5, 2)
        line_next("middle", 4, 0)

    renew_square()
    renew_fourth()
    @pl.when(edge)
    def _():
        line_next("edge", 3, 3)
        line_next("edge", 4, 3)

    @pl.when(middle)
    def _():
        line_next("middle", 4, 3)
        line_next("middle", 5, 0)

    renew_factor()
    @pl.when(edge)
    def _():
        line_next("edge", 5, 3)

    @pl.when(middle)
    def _():
        line_next("middle", 5, 3)

    renew_end()
    @pl.when(middle)
    def _():
        gathered("middle", 1)

    loads[4].wait()
    direct(0)
    @pl.when(edge)
    def _():
        gathered("edge", 1)

    new_statistics(1)
    new_statistics(0)
    @pl.when(edge)
    def _():
        gathered("edge", 2)

    direct(1)
    @pl.when(middle)
    def _():
        gathered("middle", 2)

    new_statistics(2)
    direct(2)
    both(lambda: drain("edge"), lambda: drain("middle"))


def exchange(owner_slot, refresh, grads, left_root, left_stat, right_stat, right_root, shards):
    blocks, order = grads.shape[1], grads.shape[2]
    reps = 2 * LINE
    rows = order // reps
    part = rows // shards
    chunks = len(CHUNKS)
    low = jnp.bfloat16
    wide = jnp.float32
    smem = pl.BlockSpec(memory_space=pltpu.SMEM)
    hbm = pl.BlockSpec(memory_space=pltpu.HBM)
    dma = pltpu.SemaphoreType.DMA
    return pl.pallas_call(
        exchange_kernel,
        out_shape=(
            jax.ShapeDtypeStruct((blocks, rows, order), wide),
            jax.ShapeDtypeStruct((blocks, rows, order), wide),
            jax.ShapeDtypeStruct((blocks, order, order), low),
            jax.ShapeDtypeStruct((rows, order), low),
            jax.ShapeDtypeStruct((order, order), low),
        ),
        in_specs=[hbm, smem] + [hbm] * 5,
        out_specs=(pl.BlockSpec(memory_space=pltpu.VMEM),) * 5,
        scratch_shapes=[
            pltpu.SMEM(owner_slot.shape, owner_slot.dtype),
            pltpu.VMEM((blocks, order, order), low),
            pltpu.VMEM((blocks, order, order), low),
            pltpu.VMEM((blocks, rows, order), wide),
            pltpu.VMEM((blocks, rows, order), wide),
            pltpu.VMEM((blocks, order, order), low),
            pltpu.VMEM((blocks, order, order), low),
            pltpu.VMEM((blocks, LINE, 2, rows, order), low),
            pltpu.VMEM((shards, 2, part, order), low),
            pltpu.VMEM((shards, 2, part, order), low),
            pltpu.VMEM((2, reps, shards, part, order), low),
            pltpu.VMEM((blocks, LINE, rows, order), low),
            pltpu.VMEM((blocks, LINE, rows, order), wide),
            pltpu.VMEM((blocks, 3, rows, order), wide),
            pltpu.VMEM((blocks, 2, rows, order), wide),
            pltpu.VMEM((blocks, 2, rows, order), low),
            pltpu.VMEM((blocks, shards, 2, rows, order), low),
            pltpu.VMEM((order, order), low),
            pltpu.VMEM((2, order, order), low),
            pltpu.VMEM((2, order, order), low),
            pltpu.VMEM((2, order, order), low),
            pltpu.VMEM((2, order, order), low),
            dma((6,)),
            dma((chunks, LINE)),
            dma((chunks, LINE)),
            dma((chunks, LINE)),
            dma((chunks, 3)),
            dma((chunks, 2)),
            dma((chunks, 3)),
            dma((chunks, 3)),
            dma((shards,)),
            dma((shards,)),
            dma((LINE, 2)),
            dma((LINE,)),
            dma((1,)),
            dma((1,)),
            dma((3,)),
            dma((3,)),
            dma((6,)),
            dma((5,)),
            dma((6,)),
            dma((6,)),
            dma((chunks, LINE, 3)),
            dma((chunks, LINE)),
            dma((chunks, LINE)),
            dma((chunks, LINE)),
        ],
        compiler_params=pltpu.CompilerParams(
            collective_id=0, has_side_effects=True, vmem_limit_bytes=48 * 2**20
        ),
    )(
        fixed(owner_slot),
        refresh,
        *map(fixed, (grads, left_root, left_stat, right_stat, right_root)),
    )


def fixed(array):
    return pltpu.with_memory_space_constraint(array, pltpu.HBM)


def arrange_kernel(
    slots_ref,
    refresh_ref,
    left_in,
    right_in,
    direction_in,
    fresh_rows,
    fresh_right,
    left_root,
    right_root,
    left_new,
    right_new,
    left_root_new,
    right_root_new,
    direction,
    sems,
):
    blocks = left_in.shape[0]
    fresh_slot = slots_ref[refresh_ref[0]]
    slot = fresh_slot % blocks
    owns = fresh_slot // blocks == lax.axis_index("shard")
    copies = []

    def copy(source, target):
        copies.append(pltpu.make_async_copy(source, target, sems.at[len(copies)]))
        copies[-1].start()

    for block in range(blocks):
        where = (slot + block) % blocks
        copy(direction_in.at[block], direction.at[where])
        copy(left_in.at[block], left_new.at[where])
        copy(right_in.at[block], right_new.at[where])
        if block > 0:
            copy(right_root.at[where], right_root_new.at[where])
            copy(left_root.at[where], left_root_new.at[where])
    last = len(copies)

    @pl.when(owns)
    def _():
        pltpu.make_async_copy(fresh_right, right_root_new.at[slot], sems.at[last]).start()
        pltpu.make_async_copy(fresh_rows, left_root_new.at[slot], sems.at[last + 1]).start()

    @pl.when(jnp.logical_not(owns))
    def _():
        pltpu.make_async_copy(
            right_root.at[slot], right_root_new.at[slot], sems.at[last]
        ).start()
        pltpu.make_async_copy(
            left_root.at[slot], left_root_new.at[slot], sems.at[last + 1]
        ).start()

    pltpu.make_async_copy(fresh_right, right_root_new.at[slot], sems.at[last]).wait()
    pltpu.make_async_copy(fresh_rows, left_root_new.at[slot], sems.at[last + 1]).wait()
    for item in copies:
        item.wait()


def arrange(*operands):
    stat, root, right = operands[2], operands[7], operands[8]
    smem = pl.BlockSpec(memory_space=pltpu.SMEM)
    hbm = pl.BlockSpec(memory_space=pl.ANY)
    return pl.pallas_call(
        arrange_kernel,
        out_shape=(
            jax.ShapeDtypeStruct(stat.shape, stat.dtype),
            jax.ShapeDtypeStruct(stat.shape, stat.dtype),
            jax.ShapeDtypeStruct(root.shape, root.dtype),
            jax.ShapeDtypeStruct(right.shape, right.dtype),
            jax.ShapeDtypeStruct(right.shape, right.dtype),
        ),
        in_specs=[smem, smem] + [hbm] * 7,
        out_specs=(hbm,) * 5,
        scratch_shapes=[pltpu.SemaphoreType.DMA((5 * stat.shape[0],))],
        compiler_params=pltpu.CompilerParams(vmem_limit_bytes=2**20),
    )(*operands)


def direct_body(grads, owner_slot, refresh, left_stat, right_stat, left_root, right_root):
    results = exchange(
        owner_slot,
        refresh,
        grads,
        left_root,
        left_stat,
        right_stat,
        right_root,
        lax.axis_size("shard"),
    )
    return arrange(owner_slot, refresh, *results, left_root, right_root)


def choose(mesh, *arrays):
    reps, shards = mesh.shape["rep"], mesh.shape["shard"]
    rows = arrays[0].shape[2] // reps
    blocks = arrays[0].shape[1] // shards
    finest = 16 * max(shards, *(entry[2] for entry in CHUNKS))
    direct = (reps, shards, blocks) == (2 * LINE, 4, 3) and rows % finest == 0
    return direct_body if direct else body


def solution(mesh):
    def run(*arrays):
        return mapped(mesh, choose(mesh, *arrays))(*arrays)

    return run


def mapped(mesh, body):
    return jax.shard_map(
        body,
        mesh=mesh,
        in_specs=(
            P("rep", "shard", None, None),
            P(),
            P(),
            P("shard", "rep", None),
            P("shard", "rep", None),
            P("shard", "rep", None),
            P("shard", None, None),
        ),
        out_specs=(
            P("shard", "rep", None),
            P("shard", "rep", None),
            P("shard", "rep", None),
            P("shard", None, None),
            P("shard", None, None),
        ),
        check_vma=False,
    )
```

```python
import functools

import jax
import jax.numpy as jnp
from jax import lax
from jax.experimental import pallas as pl
from jax.experimental.pallas import tpu as pltpu
from jax.sharding import PartitionSpec as P

ITERS = 2


decay_rate = 0.95
epsilon_shift = 1e-06


def inverse_root(statistic):
    order = statistic.shape[0]
    identity = (
        lax.broadcasted_iota(jnp.int32, (order, order), 0)
        == lax.broadcasted_iota(jnp.int32, (order, order), 1)
    ).astype(jnp.float32)
    shifted = statistic + epsilon_shift * identity
    norm_scale = 2.5 / jnp.sqrt(jnp.sum(shifted * shifted))
    moment = norm_scale * shifted
    current = identity
    for number in range(ITERS):
        factor = (5.0 * identity - moment) * 0.25
        factor_low = factor.astype(jnp.bfloat16)
        if number == 0:
            current = jnp.sqrt(jnp.sqrt(norm_scale)) * factor
        else:
            current = jnp.dot(
                current.astype(jnp.bfloat16), factor_low, preferred_element_type=jnp.float32
            )
        if number + 1 < ITERS:
            square = jnp.dot(factor_low, factor_low, preferred_element_type=jnp.float32).astype(
                jnp.bfloat16
            )
            fourth = jnp.dot(square, square, preferred_element_type=jnp.float32).astype(
                jnp.bfloat16
            )
            moment = jnp.dot(
                fourth, moment.astype(jnp.bfloat16), preferred_element_type=jnp.float32
            )
    return current.astype(jnp.bfloat16)


def both_roots(fresh_whole):
    return (inverse_root(fresh_whole[0]), inverse_root(fresh_whole[1]))


def empty_roots(fresh_whole):
    blank = jnp.zeros(fresh_whole.shape[1:], jnp.bfloat16)
    return (blank, blank)


def body(grads, owner_slot, refresh, left_stat, right_stat, left_root, right_root):
    blocks = grads.shape[1]
    block_order = grads.shape[2]
    rep_count = lax.axis_size("rep")
    shards = lax.axis_size("shard")
    row_count = block_order // rep_count
    rep_index = lax.axis_index("rep")
    shard_index = lax.axis_index("shard")
    partial_value = grads[0].astype(jnp.float32)
    row_share = lax.psum_scatter(partial_value, "rep", scatter_dimension=1, tiled=True)
    row_share = row_share.astype(jnp.bfloat16)
    slot_table = owner_slot.reshape(shards, blocks)
    own_slots = lax.dynamic_index_in_dim(slot_table, shard_index, 0, keepdims=False)
    targets = own_slots // blocks
    selector = (targets[None, :] == jnp.arange(shards, dtype=jnp.int32)[:, None]).astype(
        jnp.bfloat16
    )
    outgoing = jnp.einsum(
        "ok,krc->orc", selector, row_share, preferred_element_type=jnp.float32
    ).astype(jnp.bfloat16)
    incoming = lax.all_to_all(outgoing, "shard", split_axis=0, concat_axis=0, tiled=True)
    wanted = shard_index * blocks + jnp.arange(blocks, dtype=jnp.int32)
    receiver = (jnp.transpose(slot_table) == wanted[:, None]).astype(jnp.bfloat16)
    owned_rows = jnp.einsum(
        "ks,src->krc", receiver, incoming, preferred_element_type=jnp.float32
    ).astype(jnp.bfloat16)
    gathered = lax.all_gather(owned_rows, "rep", axis=1, tiled=True)
    left_new = (
        decay_rate * left_stat
        + jnp.einsum("krc,kjc->krj", owned_rows, gathered, preferred_element_type=jnp.float32)
        / block_order
    )
    column_share = lax.dynamic_slice_in_dim(gathered, rep_index * row_count, row_count, 2)
    right_new = (
        decay_rate * right_stat
        + jnp.einsum("kic,kij->kcj", column_share, gathered, preferred_element_type=jnp.float32)
        / block_order
    )
    fresh_slot = owner_slot[refresh[0]]
    holder = fresh_slot // blocks
    slot_index = fresh_slot % blocks
    owns_fresh = holder == shard_index
    fresh_pair = jnp.stack(
        [
            lax.dynamic_index_in_dim(left_new, slot_index, 0, keepdims=False),
            lax.dynamic_index_in_dim(right_new, slot_index, 0, keepdims=False),
        ]
    )
    fresh_whole = lax.all_gather(fresh_pair, "rep", axis=1, tiled=True)
    fresh_left, fresh_right = lax.cond(owns_fresh, both_roots, empty_roots, fresh_whole)
    fresh_rows = lax.dynamic_slice_in_dim(fresh_left, rep_index * row_count, row_count, 0)
    left_updated = lax.dynamic_update_index_in_dim(left_root, fresh_rows, slot_index, 0)
    left_root_new = jnp.where(owns_fresh, left_updated, left_root)
    right_updated = lax.dynamic_update_index_in_dim(right_root, fresh_right, slot_index, 0)
    right_root_new = jnp.where(owns_fresh, right_updated, right_root)
    half_step = jnp.einsum(
        "kri,kic->krc", left_root_new, gathered, preferred_element_type=jnp.float32
    ).astype(jnp.bfloat16)
    preconditioned = jnp.einsum(
        "kri,kic->krc", half_step, right_root_new, preferred_element_type=jnp.float32
    ).astype(jnp.bfloat16)
    direction = lax.all_gather(preconditioned, "rep", axis=1, tiled=True)
    return (left_new, right_new, left_root_new, right_root_new, direction)


MESH = pl.DeviceIdType.MESH
LINE = 4
CHUNKS = ((0, 0, 2, True), (0, 1, 2, False), (1, 0, 2, True), (1, 1, 2, False), (2, 0, 2, False), (2, 1, 2, False))
DIRECT = (2,)
PAIRED = ()


def dot(left, right, dims=(1, 0)):
    return lax.dot_general(
        left, right, (((dims[0],), (dims[1],)), ((), ())), preferred_element_type=jnp.float32
    )


def exchange_kernel(
    slots_in,
    refresh_ref,
    grads_ref,
    left_ref,
    left_stat_ref,
    right_stat_ref,
    right_ref,
    left_new_ref,
    right_new_ref,
    direction_ref,
    fresh_rows_ref,
    fresh_right_ref,
    slots_ref,
    arrived,
    mine,
    left_stat,
    right_stat,
    right_full,
    left_full,
    grad_full,
    stat_ref,
    quarter_in,
    stat_full,
    across,
    partial_out,
    from_outer,
    from_inner,
    share,
    incoming,
    turned,
    moment,
    factor,
    current,
    square,
    load_sem,
    across_send,
    across_recv,
    partial_send,
    outer_recv,
    inner_recv,
    swap_send,
    swap_recv,
    part_send,
    part_recv,
    stat_send,
    stat_recv,
    stat_side_send,
    stat_side_recv,
    spread_send,
    spread_recv,
    root_send,
    root_recv,
    root_side_send,
    root_side_recv,
    line_send,
    line_recv,
    side_send,
    side_recv,
):
    blocks, order = mine.shape[0], mine.shape[1]
    rows = order // (2 * LINE)
    group = 2 * rows
    shards = stat_ref.shape[0]
    me = lax.axis_index("rep")
    shard = lax.axis_index("shard")
    place = me // 2
    side = me % 2
    other_row = (shard + 2) % shards
    other_core = shard + 1 - 2 * (shard % 2)
    partner = (place * 2 + (1 - side), shard)
    flip = place // (LINE // 2)
    middle = (place == 1) | (place == 2)
    edge = jnp.logical_not(middle)

    def real(position):
        return position + flip * (LINE - 1 - 2 * position)

    def at(position):
        return (real(position) * 2 + side, shard)

    def span(index):
        return pl.ds(pl.multiple_of(index * rows, rows), rows)

    def pair_span(index):
        return pl.ds(pl.multiple_of(index * group, group), group)

    loads = [
        pltpu.make_async_copy(left_stat_ref, left_stat, load_sem.at[0]),
        pltpu.make_async_copy(right_stat_ref, right_stat, load_sem.at[1]),
        pltpu.make_async_copy(grads_ref.at[0], arrived, load_sem.at[2]),
        pltpu.make_async_copy(left_ref, left_full.at[:, span(me), :], load_sem.at[3]),
        pltpu.make_async_copy(right_ref, right_full, load_sem.at[4]),
        pltpu.make_async_copy(slots_in, slots_ref, load_sem.at[5]),
    ]
    barrier = pltpu.get_barrier_semaphore()
    for step in range(1, LINE):
        pl.semaphore_signal(
            barrier,
            inc=1,
            device_id=((place + step) % LINE * 2 + side, shard),
            device_id_type=MESH,
        )
    pl.semaphore_signal(barrier, inc=1, device_id=partner, device_id_type=MESH)
    for step in range(1, shards):
        pl.semaphore_signal(
            barrier, inc=1, device_id=(me, (shard + step) % shards), device_id_type=MESH
        )
    loads[5].start()
    loads[2].start()
    loads[5].wait()
    slot = slots_ref[refresh_ref[0]] % blocks
    keeper = slots_ref[refresh_ref[0]] // blocks
    owns = keeper == shard

    def local(block):
        return (slot + block) % blocks

    loads[2].wait()
    for index in (0, 1, 3):
        loads[index].start()
    mine[0] = arrived[local(0)]
    pl.semaphore_wait(barrier, LINE - 1 + 1 + shards - 1)

    pending = {"all": [], "edge": [], "middle": []}

    def remote(src, dst, send_sem, recv_sem, device):
        return pltpu.make_async_remote_copy(
            src_ref=src,
            dst_ref=dst,
            send_sem=send_sem,
            recv_sem=recv_sem,
            device_id=device,
            device_id_type=MESH,
        )

    def send(kind, make):
        make().start()
        pending[kind].append(make)

    def drain(kind):
        for make in pending[kind]:
            make().wait_send()
        pending[kind] = []

    def arrive(dst, recv_sem):
        remote(dst, dst, recv_sem, recv_sem, partner).wait_recv()

    def both(on_edge, on_middle):
        pl.when(edge)(on_edge)
        pl.when(middle)(on_middle)

    def cells(chunk):
        block, number, count, _ = CHUNKS[chunk]
        size = rows // count
        return block, pl.ds(number * size, size)

    def span_of(chunk, index):
        block, number, count, _ = CHUNKS[chunk]
        size = rows // count
        first = index * rows + number * size
        return block, pl.ds(pl.multiple_of(first, size), size)

    def across_copy(chunk, target):
        block, there = span_of(chunk, target * 2 + (1 - side))
        block, here = cells(chunk)
        return remote(
            mine.at[block, there, :],
            across.at[block, target, here],
            across_send.at[chunk, target],
            across_recv.at[chunk, target],
            partner,
        )

    def send_across(kind, chunk, positions):
        for position in positions:
            send(kind, lambda p=position: across_copy(chunk, real(p)))

    def pair_sum(chunk, position):
        target = real(position)
        block, here = cells(chunk)
        arrive(across.at[block, target, here], across_recv.at[chunk, target])
        own = mine[span_of(chunk, target * 2 + side)].astype(jnp.float32)
        return own + across[block, target, here].astype(jnp.float32)

    def wait_outer(chunk, number):
        block, here = cells(chunk)
        arrive(from_outer.at[block, number, here], outer_recv.at[chunk, number])
        return from_outer[block, number, here]

    def wait_inner(chunk, number):
        block, here = cells(chunk)
        arrive(from_inner.at[block, number, here], inner_recv.at[chunk, number])
        return from_inner[block, number, here]

    def edge_far(chunk, position):
        number = position - 1
        block, here = cells(chunk)
        partial_out[block, number, here] = pair_sum(chunk, position)
        send(
            "edge",
            lambda: remote(
                partial_out.at[block, number, here],
                from_outer.at[block, number, here],
                partial_send.at[chunk, number],
                outer_recv.at[chunk, number],
                at(1),
            ),
        )

    def middle_far(chunk, position):
        number = {3: 0, 2: 1, 0: 2, 1: 3}[position]
        block, here = cells(chunk)
        if position < 2:
            earlier = wait_inner(chunk, position)
            goal, landing = 0, position
        else:
            earlier = wait_outer(chunk, position - 1)
            goal, landing = 2, number
        partial_out[block, number, here] = pair_sum(chunk, position) + earlier
        send(
            "middle",
            lambda: remote(
                partial_out.at[block, number, here],
                from_inner.at[block, landing, here],
                partial_send.at[chunk, number],
                inner_recv.at[chunk, landing],
                at(goal),
            ),
        )

    def swap_rows(chunk, owner):
        block, here = cells(chunk)
        return incoming.at[block, owner, groups(chunk), here]

    def at_ends(chunk):
        return CHUNKS[chunk][3]

    def groups(chunk):
        return slice(None) if at_ends(chunk) else 0

    others = ((other_core + 2) % shards, other_row, other_core)

    def swap(kind, chunk, *totals):
        block, here = cells(chunk)
        for number, total in enumerate(totals):
            value = total.astype(jnp.bfloat16)
            share[block, number, here] = value
            incoming[block, shard, number, here] = value
        for number, goal in enumerate(others):
            send(
                kind,
                lambda n=number, g=goal: remote(
                    share.at[block, groups(chunk), here],
                    swap_rows(chunk, shard),
                    swap_send.at[chunk, n],
                    swap_recv.at[chunk, n],
                    (me, g),
                ),
            )

    def edge_own(chunk):
        positions = (0, 1) if at_ends(chunk) else (0,)
        swap("edge", chunk, *(pair_sum(chunk, p) + wait_inner(chunk, p) for p in positions))

    def middle_own(chunk):
        total = pair_sum(chunk, 1) + wait_inner(chunk, 1)
        swap("middle", chunk, total + wait_outer(chunk, 0))

    def share_rows(chunk, source, which):
        block, here = cells(chunk)
        if at_ends(chunk):
            half = LINE // 2
            return grad_full.at[block, pl.ds(source // half * half, half), which, here]
        return grad_full.at[block, source, which, here]

    def side_copy(chunk, source):
        where = share_rows(chunk, source, side)
        return remote(
            where, where, side_send.at[chunk, source], side_recv.at[chunk, source], partner
        )

    def wait_side(chunk, source):
        arrive(share_rows(chunk, source, 1 - side), side_recv.at[chunk, source])

    def line_rows(chunk, position):
        if CHUNKS[chunk][0] in PAIRED and position in (1, 2):
            return share_rows(chunk, real(position), slice(None))
        return share_rows(chunk, real(position), side)

    def line_copy(chunk, position, way, goal):
        where = line_rows(chunk, position)
        return remote(
            where,
            where,
            line_send.at[chunk, real(position), way],
            line_recv.at[chunk, real(position)],
            at(goal),
        )

    def take(kind, chunk):
        for number, origin in enumerate(others):
            arrive(swap_rows(chunk, origin), swap_recv.at[chunk, number])
        block, here = cells(chunk)
        wanted = shard * blocks + local(block)
        for number in range(2 if at_ends(chunk) else 1):
            value = incoming[block, 0, number, here]
            for origin in range(1, shards):
                held = slots_ref[origin * blocks + local(block)] == wanted
                value = jnp.where(held, incoming[block, origin, number, here], value)
            group_place = real(number) if at_ends(chunk) else place
            grad_full[block, group_place, side, here] = value
        paired = block in PAIRED and kind == "middle"
        if not paired:
            line_begin(kind, chunk)
        send(kind, lambda: side_copy(chunk, place))
        if block in DIRECT:
            own, near, far = (0, 1, (2, 3)) if kind == "edge" else (1, 2, (3,))
            for way, goal in enumerate(far):
                send(kind, lambda w=way, g=goal: line_copy(chunk, own, near + w, g))

    def line_begin(kind, chunk):
        if CHUNKS[chunk][0] in PAIRED and kind == "middle":
            wait_side(chunk, place)
        if kind == "edge":
            send(kind, lambda: line_copy(chunk, 0, 0, 1))
        else:
            send(kind, lambda: line_copy(chunk, 1, 0, 0))
            send(kind, lambda: line_copy(chunk, 1, 1, 2))

    def wait_line(chunk, position):
        arrive(line_rows(chunk, position), line_recv.at[chunk, real(position)])

    def line_next(kind, chunk, position):
        block = CHUNKS[chunk][0]
        wait_line(chunk, position)
        if kind == "middle" and block not in DIRECT:
            goal = 2 if position == 0 else 0
            send(kind, lambda: line_copy(chunk, position, 0, goal))
        if block not in PAIRED or position in (0, 3):
            send(kind, lambda: side_copy(chunk, real(position)))

    def gathered(kind, block):
        if block == blocks - 1:
            for make in pending["all"]:
                make().wait_send()
            drain(kind)
        for chunk, entry in enumerate(CHUNKS):
            if entry[0] != block:
                continue
            paired = block in PAIRED
            if paired and kind == "edge":
                wait_line(chunk, 1)
                wait_line(chunk, 2)
            for position in (0, 3) if paired or entry[3] else range(LINE):
                wait_side(chunk, real(position))

    pieces = {
        "edge": ((1, 1, 3), (2, 2, 2), (3, 3, 1)),
        "middle": ((0, 0, 1), (0, 3, 1), (2, 2, 2), (2, 0, 1), (3, 3, 1)),
    }

    def columns(first, count):
        return pl.ds(
            pl.multiple_of((first + flip * (LINE - 2 * first - count)) * group, group),
            count * group,
        )

    def root_piece(piece, which):
        position, first, count = piece
        return left_full.at[:, span(real(position) * 2 + which), columns(first, count)]

    def send_root(kind, number, piece, goal, landing):
        send(
            kind,
            lambda: remote(
                root_piece(piece, side),
                root_piece(piece, side),
                root_send.at[number],
                root_recv.at[landing],
                at(goal),
            ),
        )

    def wait_root(kind, number):
        arrive(root_piece(pieces[kind][number], side), root_recv.at[number])

    def edge_roots():
        send_root("edge", 0, (0, 0, 1), 1, 0)
        send_root("edge", 1, (0, 3, 1), 1, 1)

    def middle_roots():
        send_root("middle", 0, (1, 0, 2), 2, 2)
        send_root("middle", 1, (1, 1, 3), 0, 0)
        send_root("middle", 2, (1, 3, 1), 2, 3)

    def middle_root(number):
        wait_root("middle", number)
        if number == 0:
            send_root("middle", 3, (0, 0, 1), 2, 4)
        if number == 2:
            send_root("middle", 4, (2, 2, 2), 0, 1)
        if number == 4:
            send_root("middle", 5, (3, 3, 1), 0, 2)
        if number == 1:
            wait_root("middle", 3)

    def edge_roots_next():
        for number in range(3):
            wait_root("edge", number)

    def root_side(kind, number):
        def make():
            if number == 0:
                where = left_full.at[:, span(me), :]
            else:
                where = root_piece(pieces[kind][number - 1], side)
            return remote(
                where, where, root_side_send.at[number], root_side_recv.at[number], partner
            )

        return make

    def wait_root_side(kind):
        arrive(left_full.at[:, span(place * 2 + 1 - side), :], root_side_recv.at[0])
        for number, piece in enumerate(pieces[kind]):
            arrive(root_piece(piece, 1 - side), root_side_recv.at[number + 1])

    def mirror(kind):
        tiles = [(1, 2), (1, 3), (2, 3)]
        if kind == "edge":
            tiles += [(0, 1), (0, 2), (0, 3)]
        else:
            tiles += [(1, 0), (2, 0), (0, 3)]
        for block in range(blocks):
            for row, column in tiles:
                value = left_full[block, pair_span(real(row)), columns(column, 1)]
                left_full[block, pair_span(real(column)), columns(row, 1)] = value.T

    def to_shards(step):
        peer = (shard + step) % shards
        return remote(
            stat_ref.at[peer],
            quarter_in.at[shard],
            part_send.at[step],
            part_recv.at[step],
            (me, peer),
        )

    def stat_side():
        where = stat_full.at[:, me, shard]
        return remote(where, where, stat_side_send.at[0], stat_side_recv.at[0], partner)

    def stat_rows(position):
        return stat_full.at[:, pl.ds(real(position) * 2, 2), shard]

    def stat_copy(position, way, goal):
        where = stat_rows(position)
        return remote(
            where,
            where,
            stat_send.at[real(position), way],
            stat_recv.at[real(position)],
            at(goal),
        )

    def wait_stat(position):
        arrive(stat_rows(position), stat_recv.at[real(position)])

    def send_quarters(kind):
        for step in range(1, shards):
            origin = (shard + shards - step) % shards
            arrive(quarter_in.at[origin], part_recv.at[step])
        stat_full[:, me, shard] = quarter_in[keeper]
        send(kind, stat_side)

    def stat_begin(kind):
        arrive(stat_full.at[:, place * 2 + (1 - side), shard], stat_side_recv.at[0])
        if kind == "edge":
            send(kind, lambda: stat_copy(0, 0, 1))
        else:
            send(kind, lambda: stat_copy(1, 0, 0))
            send(kind, lambda: stat_copy(1, 1, 2))

    def stat_next(position):
        wait_stat(position)
        goal = 2 if position == 0 else 0
        send("middle", lambda: stat_copy(position, 0, goal))

    def spread(number, owner, goal):
        where = stat_full.at[:, :, owner]
        return remote(
            where, where, spread_send.at[number], spread_recv.at[number], (me, goal)
        )

    def spread_quarters(kind):
        if kind == "edge":
            for position in (1, 2, 3):
                wait_stat(position)
        send(kind, lambda: spread(0, shard, other_row))
        send(kind, lambda: spread(1, shard, other_core))

    def spread_next(kind):
        arrive(stat_full.at[:, :, other_row], spread_recv.at[0])
        send(kind, lambda: spread(2, other_row, other_core))

    def spread_end():
        arrive(stat_full.at[:, :, other_core], spread_recv.at[1])
        arrive(
            stat_full.at[:, :, (other_core + 2) % shards], spread_recv.at[2]
        )

    tile = pair_span(place)

    def new_statistics(block):
        grad = grad_full[block].reshape(order, order)
        own = grad_full[block, place, side]
        left_new_ref[block] = decay_rate * left_stat[local(block)] + dot(own, grad, (1, 1)) / order
        turned_rows = grad_full[block, :, :, :, tile].reshape(order, group).T
        own_turned = jnp.where(side == 0, turned_rows[:rows], turned_rows[rows:])
        right_new_ref[block] = decay_rate * right_stat[local(block)] + dot(own_turned, grad) / order

    def renew_begin(which):
        identity = (
            lax.broadcasted_iota(jnp.int32, (order, order), 0)
            == lax.broadcasted_iota(jnp.int32, (order, order), 1)
        ).astype(jnp.float32)
        grad = grad_full[0].reshape(order, order)
        if which == 0:
            turned[...] = grad.T
            product = dot(grad, turned[...])
        else:
            product = dot(turned[...], grad)
        old = stat_full[which].reshape(order, order).astype(jnp.float32)
        shifted = decay_rate * old + product / order + epsilon_shift * identity
        scale = 2.5 / jnp.sqrt(jnp.sum(shifted * shifted))
        start = scale * shifted
        moment[which] = start.astype(jnp.bfloat16)
        step = (5.0 * identity - start) * 0.25
        factor[which] = step.astype(jnp.bfloat16)
        current[which] = (jnp.sqrt(jnp.sqrt(scale)) * step).astype(jnp.bfloat16)

    def renew_square():
        for which in range(2):
            square[which] = dot(factor[which], factor[which]).astype(jnp.bfloat16)

    def renew_fourth():
        for which in range(2):
            factor[which] = dot(square[which], square[which]).astype(jnp.bfloat16)

    def renew_factor():
        identity = (
            lax.broadcasted_iota(jnp.int32, (order, order), 0)
            == lax.broadcasted_iota(jnp.int32, (order, order), 1)
        ).astype(jnp.float32)
        for which in range(2):
            value = dot(factor[which], moment[which])
            square[which] = ((5.0 * identity - value) * 0.25).astype(jnp.bfloat16)

    def renew_end():
        moment[0] = dot(current[0], square[0]).astype(jnp.bfloat16)
        fresh_right_ref[...] = dot(current[1], square[1]).astype(jnp.bfloat16)
        fresh_rows_ref[...] = moment[0, span(me), :]

    def direct(block):
        root = left_full[local(block)]
        other = right_full[local(block)]
        if block == 0:
            root = jnp.where(owns, moment[0], root)
            other = jnp.where(owns, fresh_right_ref[...], other)
        half = dot(root, grad_full[block].reshape(order, order)).astype(jnp.bfloat16)
        direction_ref[block] = dot(half, other).astype(jnp.bfloat16)

    @pl.when(edge)
    def _():
        send_across("edge", 0, (3, 2, 1, 0))
        send_across("edge", 1, (3, 2, 1, 0))

    @pl.when(middle)
    def _():
        send_across("middle", 1, (3, 2, 0, 1))
        send_across("middle", 0, (3, 2, 0, 1))
    for block in range(1, blocks):
        mine[block] = arrived[local(block)]
    loads[0].wait()
    loads[1].wait()
    part = rows // shards
    for index in range(shards):
        part_rows = pl.ds(index * part, part)
        stat_ref[index, 0] = left_stat[slot, part_rows, :].astype(jnp.bfloat16)
        stat_ref[index, 1] = right_stat[slot, part_rows, :].astype(jnp.bfloat16)
    for step in range(1, shards):
        send("all", lambda step=step: to_shards(step))
    quarter_in[shard] = stat_ref[shard]
    loads[3].wait()
    loads[4].start()

    @pl.when(edge)
    def _():
        edge_roots()
        edge_far(0, 3)
        send_across("edge", 2, (3, 2, 1, 0))
        edge_far(0, 2)
        send_across("edge", 3, (3, 2, 1, 0))
        edge_far(1, 3)
        edge_far(1, 2)
        send_quarters("edge")
        edge_far(2, 3)
        send_across("edge", 4, (3, 2, 1, 0))
        edge_far(2, 2)
        edge_far(3, 3)
        send_across("edge", 5, (3, 2, 1, 0))
        edge_far(1, 1)
        edge_far(3, 2)
        stat_begin("edge")
        edge_far(4, 3)
        edge_own(0)
        edge_roots_next()
        edge_far(3, 1)
        send("edge", root_side("edge", 0))
        edge_far(5, 2)
        edge_far(5, 3)
        edge_own(1)
        send("edge", root_side("edge", 2))
        take("edge", 0)
        edge_own(2)
        take("edge", 1)
        send("edge", root_side("edge", 1))
        edge_own(3)
        send("edge", root_side("edge", 3))
        edge_far(5, 1)
        edge_far(4, 2)
        spread_quarters("edge")
        line_next("edge", 1, 1)
        take("edge", 2)
        take("edge", 3)
        line_next("edge", 3, 1)
        edge_far(4, 1)
        line_next("edge", 1, 2)
        edge_own(5)
        edge_own(4)
        wait_root_side("edge")
        line_next("edge", 0, 3)
        line_next("edge", 1, 3)
        line_next("edge", 3, 2)
        spread_next("edge")
        mirror("edge")
        take("edge", 5)
        line_next("edge", 5, 1)
        spread_end()
        take("edge", 4)
        gathered("edge", 0)

    @pl.when(middle)
    def _():
        middle_roots()
        middle_root(0)
        send_quarters("middle")
        middle_root(2)
        middle_root(1)
        middle_far(0, 3)
        send_across("middle", 2, (3, 2, 0, 1))
        middle_far(0, 2)
        middle_root(4)
        stat_begin("middle")
        send_across("middle", 3, (3, 2, 0, 1))
        middle_far(1, 3)
        middle_far(0, 0)
        middle_far(1, 2)
        middle_far(0, 1)
        middle_far(2, 3)
        send_across("middle", 4, (3, 2, 0, 1))
        stat_next(2)
        send_across("middle", 5, (3, 2, 0, 1))
        middle_far(2, 2)
        send("middle", root_side("middle", 5))
        middle_far(3, 3)
        middle_far(1, 0)
        middle_own(1)
        middle_far(2, 0)
        send("middle", root_side("middle", 1))
        middle_far(3, 2)
        middle_far(2, 1)
        stat_next(0)
        middle_far(3, 0)
        take("middle", 1)
        middle_far(4, 3)
        send("middle", root_side("middle", 0))
        middle_own(3)
        stat_next(3)
        middle_far(5, 2)
        spread_quarters("middle")
        middle_far(5, 3)
        line_next("middle", 1, 2)
        middle_far(4, 0)
        line_next("middle", 0, 0)
        line_next("middle", 1, 0)
        take("middle", 3)
        send("middle", root_side("middle", 3))
        middle_far(5, 0)
        middle_own(5)
        line_next("middle", 0, 3)
        middle_far(4, 2)
        line_next("middle", 1, 3)
        send("middle", root_side("middle", 4))
        line_next("middle", 3, 2)
        line_next("middle", 2, 0)
        line_next("middle", 3, 0)
        take("middle", 5)
        spread_next("middle")
        middle_own(4)
        send("middle", root_side("middle", 2))
        line_next("middle", 2, 3)
        spread_end()
        gathered("middle", 0)
        line_next("middle", 3, 3)

    renew_begin(0)
    @pl.when(edge)
    def _():
        line_next("edge", 2, 3)

    renew_begin(1)
    @pl.when(edge)
    def _():
        line_next("edge", 5, 2)

    renew_square()
    @pl.when(edge)
    def _():
        line_next("edge", 3, 3)
        line_next("edge", 5, 3)

    @pl.when(middle)
    def _():
        take("middle", 4)
        line_next("middle", 5, 0)

    renew_fourth()
    @pl.when(middle)
    def _():
        line_next("middle", 5, 3)

    renew_factor()
    @pl.when(edge)
    def _():
        line_next("edge", 4, 1)
        line_next("edge", 4, 3)

    @pl.when(middle)
    def _():
        wait_root_side("middle")
        line_next("middle", 4, 0)
        mirror("middle")
        gathered("middle", 1)

    renew_end()
    @pl.when(edge)
    def _():
        line_next("edge", 4, 2)

    @pl.when(middle)
    def _():
        line_next("middle", 4, 2)
        line_next("middle", 5, 2)

    loads[4].wait()
    direct(0)
    @pl.when(edge)
    def _():
        gathered("edge", 1)

    @pl.when(middle)
    def _():
        line_next("middle", 4, 3)

    new_statistics(1)
    new_statistics(0)
    direct(1)
    @pl.when(edge)
    def _():
        gathered("edge", 2)

    @pl.when(middle)
    def _():
        gathered("middle", 2)

    new_statistics(2)
    direct(2)
    both(lambda: drain("edge"), lambda: drain("middle"))


def exchange(owner_slot, refresh, grads, left_root, left_stat, right_stat, right_root, shards):
    blocks, order = grads.shape[1], grads.shape[2]
    reps = 2 * LINE
    rows = order // reps
    part = rows // shards
    chunks = len(CHUNKS)
    low = jnp.bfloat16
    wide = jnp.float32
    smem = pl.BlockSpec(memory_space=pltpu.SMEM)
    hbm = pl.BlockSpec(memory_space=pltpu.HBM)
    dma = pltpu.SemaphoreType.DMA
    return pl.pallas_call(
        exchange_kernel,
        out_shape=(
            jax.ShapeDtypeStruct((blocks, rows, order), wide),
            jax.ShapeDtypeStruct((blocks, rows, order), wide),
            jax.ShapeDtypeStruct((blocks, order, order), low),
            jax.ShapeDtypeStruct((rows, order), low),
            jax.ShapeDtypeStruct((order, order), low),
        ),
        in_specs=[hbm, smem] + [hbm] * 5,
        out_specs=(pl.BlockSpec(memory_space=pltpu.VMEM),) * 5,
        scratch_shapes=[
            pltpu.SMEM(owner_slot.shape, owner_slot.dtype),
            pltpu.VMEM((blocks, order, order), low),
            pltpu.VMEM((blocks, order, order), low),
            pltpu.VMEM((blocks, rows, order), wide),
            pltpu.VMEM((blocks, rows, order), wide),
            pltpu.VMEM((blocks, order, order), low),
            pltpu.VMEM((blocks, order, order), low),
            pltpu.VMEM((blocks, LINE, 2, rows, order), low),
            pltpu.VMEM((shards, 2, part, order), low),
            pltpu.VMEM((shards, 2, part, order), low),
            pltpu.VMEM((2, reps, shards, part, order), low),
            pltpu.VMEM((blocks, LINE, rows, order), low),
            pltpu.VMEM((blocks, LINE, rows, order), wide),
            pltpu.VMEM((blocks, 3, rows, order), wide),
            pltpu.VMEM((blocks, 2, rows, order), wide),
            pltpu.VMEM((blocks, 2, rows, order), low),
            pltpu.VMEM((blocks, shards, 2, rows, order), low),
            pltpu.VMEM((order, order), low),
            pltpu.VMEM((2, order, order), low),
            pltpu.VMEM((2, order, order), low),
            pltpu.VMEM((2, order, order), low),
            pltpu.VMEM((2, order, order), low),
            dma((6,)),
            dma((chunks, LINE)),
            dma((chunks, LINE)),
            dma((chunks, LINE)),
            dma((chunks, 3)),
            dma((chunks, 2)),
            dma((chunks, 3)),
            dma((chunks, 3)),
            dma((shards,)),
            dma((shards,)),
            dma((LINE, 2)),
            dma((LINE,)),
            dma((1,)),
            dma((1,)),
            dma((3,)),
            dma((3,)),
            dma((6,)),
            dma((5,)),
            dma((6,)),
            dma((6,)),
            dma((chunks, LINE, 3)),
            dma((chunks, LINE)),
            dma((chunks, LINE)),
            dma((chunks, LINE)),
        ],
        compiler_params=pltpu.CompilerParams(
            collective_id=0, has_side_effects=True, vmem_limit_bytes=48 * 2**20
        ),
    )(
        fixed(owner_slot),
        refresh,
        *map(fixed, (grads, left_root, left_stat, right_stat, right_root)),
    )


def fixed(array):
    return pltpu.with_memory_space_constraint(array, pltpu.HBM)


def arrange_kernel(
    slots_ref,
    refresh_ref,
    left_in,
    right_in,
    direction_in,
    fresh_rows,
    fresh_right,
    left_root,
    right_root,
    left_new,
    right_new,
    left_root_new,
    right_root_new,
    direction,
    sems,
):
    blocks = left_in.shape[0]
    fresh_slot = slots_ref[refresh_ref[0]]
    slot = fresh_slot % blocks
    owns = fresh_slot // blocks == lax.axis_index("shard")
    copies = []

    def copy(source, target):
        copies.append(pltpu.make_async_copy(source, target, sems.at[len(copies)]))
        copies[-1].start()

    for block in range(blocks):
        where = (slot + block) % blocks
        copy(direction_in.at[block], direction.at[where])
        copy(left_in.at[block], left_new.at[where])
        copy(right_in.at[block], right_new.at[where])
        if block > 0:
            copy(right_root.at[where], right_root_new.at[where])
            copy(left_root.at[where], left_root_new.at[where])
    last = len(copies)

    @pl.when(owns)
    def _():
        pltpu.make_async_copy(fresh_right, right_root_new.at[slot], sems.at[last]).start()
        pltpu.make_async_copy(fresh_rows, left_root_new.at[slot], sems.at[last + 1]).start()

    @pl.when(jnp.logical_not(owns))
    def _():
        pltpu.make_async_copy(
            right_root.at[slot], right_root_new.at[slot], sems.at[last]
        ).start()
        pltpu.make_async_copy(
            left_root.at[slot], left_root_new.at[slot], sems.at[last + 1]
        ).start()

    pltpu.make_async_copy(fresh_right, right_root_new.at[slot], sems.at[last]).wait()
    pltpu.make_async_copy(fresh_rows, left_root_new.at[slot], sems.at[last + 1]).wait()
    for item in copies:
        item.wait()


def arrange(*operands):
    stat, root, right = operands[2], operands[7], operands[8]
    smem = pl.BlockSpec(memory_space=pltpu.SMEM)
    hbm = pl.BlockSpec(memory_space=pl.ANY)
    return pl.pallas_call(
        arrange_kernel,
        out_shape=(
            jax.ShapeDtypeStruct(stat.shape, stat.dtype),
            jax.ShapeDtypeStruct(stat.shape, stat.dtype),
            jax.ShapeDtypeStruct(root.shape, root.dtype),
            jax.ShapeDtypeStruct(right.shape, right.dtype),
            jax.ShapeDtypeStruct(right.shape, right.dtype),
        ),
        in_specs=[smem, smem] + [hbm] * 7,
        out_specs=(hbm,) * 5,
        scratch_shapes=[pltpu.SemaphoreType.DMA((5 * stat.shape[0],))],
        compiler_params=pltpu.CompilerParams(vmem_limit_bytes=2**20),
    )(*operands)


def direct_body(grads, owner_slot, refresh, left_stat, right_stat, left_root, right_root):
    results = exchange(
        owner_slot,
        refresh,
        grads,
        left_root,
        left_stat,
        right_stat,
        right_root,
        lax.axis_size("shard"),
    )
    return arrange(owner_slot, refresh, *results, left_root, right_root)


def choose(mesh, *arrays):
    reps, shards = mesh.shape["rep"], mesh.shape["shard"]
    rows = arrays[0].shape[2] // reps
    blocks = arrays[0].shape[1] // shards
    finest = 16 * max(shards, *(entry[2] for entry in CHUNKS))
    direct = (reps, shards, blocks) == (2 * LINE, 4, 3) and rows % finest == 0
    return direct_body if direct else body


def solution(mesh):
    def run(*arrays):
        return mapped(mesh, choose(mesh, *arrays))(*arrays)

    return run


def mapped(mesh, body):
    return jax.shard_map(
        body,
        mesh=mesh,
        in_specs=(
            P("rep", "shard", None, None),
            P(),
            P(),
            P("shard", "rep", None),
            P("shard", "rep", None),
            P("shard", "rep", None),
            P("shard", None, None),
        ),
        out_specs=(
            P("shard", "rep", None),
            P("shard", "rep", None),
            P("shard", "rep", None),
            P("shard", None, None),
            P("shard", None, None),
        ),
        check_vma=False,
    )
```

```python
import functools

import jax
import jax.numpy as jnp
from jax import lax
from jax.experimental import pallas as pl
from jax.experimental.pallas import tpu as pltpu
from jax.sharding import PartitionSpec as P

ITERS = 2


decay_rate = 0.95
epsilon_shift = 1e-06


def inverse_root(statistic):
    order = statistic.shape[0]
    identity = (
        lax.broadcasted_iota(jnp.int32, (order, order), 0)
        == lax.broadcasted_iota(jnp.int32, (order, order), 1)
    ).astype(jnp.float32)
    shifted = statistic + epsilon_shift * identity
    norm_scale = 2.5 / jnp.sqrt(jnp.sum(shifted * shifted))
    moment = norm_scale * shifted
    current = identity
    for number in range(ITERS):
        factor = (5.0 * identity - moment) * 0.25
        factor_low = factor.astype(jnp.bfloat16)
        if number == 0:
            current = jnp.sqrt(jnp.sqrt(norm_scale)) * factor
        else:
            current = jnp.dot(
                current.astype(jnp.bfloat16), factor_low, preferred_element_type=jnp.float32
            )
        if number + 1 < ITERS:
            square = jnp.dot(factor_low, factor_low, preferred_element_type=jnp.float32).astype(
                jnp.bfloat16
            )
            fourth = jnp.dot(square, square, preferred_element_type=jnp.float32).astype(
                jnp.bfloat16
            )
            moment = jnp.dot(
                fourth, moment.astype(jnp.bfloat16), preferred_element_type=jnp.float32
            )
    return current.astype(jnp.bfloat16)


def both_roots(fresh_whole):
    return (inverse_root(fresh_whole[0]), inverse_root(fresh_whole[1]))


def empty_roots(fresh_whole):
    blank = jnp.zeros(fresh_whole.shape[1:], jnp.bfloat16)
    return (blank, blank)


def body(grads, owner_slot, refresh, left_stat, right_stat, left_root, right_root):
    blocks = grads.shape[1]
    block_order = grads.shape[2]
    rep_count = lax.axis_size("rep")
    shards = lax.axis_size("shard")
    row_count = block_order // rep_count
    rep_index = lax.axis_index("rep")
    shard_index = lax.axis_index("shard")
    partial_value = grads[0].astype(jnp.float32)
    row_share = lax.psum_scatter(partial_value, "rep", scatter_dimension=1, tiled=True)
    row_share = row_share.astype(jnp.bfloat16)
    slot_table = owner_slot.reshape(shards, blocks)
    own_slots = lax.dynamic_index_in_dim(slot_table, shard_index, 0, keepdims=False)
    targets = own_slots // blocks
    selector = (targets[None, :] == jnp.arange(shards, dtype=jnp.int32)[:, None]).astype(
        jnp.bfloat16
    )
    outgoing = jnp.einsum(
        "ok,krc->orc", selector, row_share, preferred_element_type=jnp.float32
    ).astype(jnp.bfloat16)
    incoming = lax.all_to_all(outgoing, "shard", split_axis=0, concat_axis=0, tiled=True)
    wanted = shard_index * blocks + jnp.arange(blocks, dtype=jnp.int32)
    receiver = (jnp.transpose(slot_table) == wanted[:, None]).astype(jnp.bfloat16)
    owned_rows = jnp.einsum(
        "ks,src->krc", receiver, incoming, preferred_element_type=jnp.float32
    ).astype(jnp.bfloat16)
    gathered = lax.all_gather(owned_rows, "rep", axis=1, tiled=True)
    left_new = (
        decay_rate * left_stat
        + jnp.einsum("krc,kjc->krj", owned_rows, gathered, preferred_element_type=jnp.float32)
        / block_order
    )
    column_share = lax.dynamic_slice_in_dim(gathered, rep_index * row_count, row_count, 2)
    right_new = (
        decay_rate * right_stat
        + jnp.einsum("kic,kij->kcj", column_share, gathered, preferred_element_type=jnp.float32)
        / block_order
    )
    fresh_slot = owner_slot[refresh[0]]
    holder = fresh_slot // blocks
    slot_index = fresh_slot % blocks
    owns_fresh = holder == shard_index
    fresh_pair = jnp.stack(
        [
            lax.dynamic_index_in_dim(left_new, slot_index, 0, keepdims=False),
            lax.dynamic_index_in_dim(right_new, slot_index, 0, keepdims=False),
        ]
    )
    fresh_whole = lax.all_gather(fresh_pair, "rep", axis=1, tiled=True)
    fresh_left, fresh_right = lax.cond(owns_fresh, both_roots, empty_roots, fresh_whole)
    fresh_rows = lax.dynamic_slice_in_dim(fresh_left, rep_index * row_count, row_count, 0)
    left_updated = lax.dynamic_update_index_in_dim(left_root, fresh_rows, slot_index, 0)
    left_root_new = jnp.where(owns_fresh, left_updated, left_root)
    right_updated = lax.dynamic_update_index_in_dim(right_root, fresh_right, slot_index, 0)
    right_root_new = jnp.where(owns_fresh, right_updated, right_root)
    half_step = jnp.einsum(
        "kri,kic->krc", left_root_new, gathered, preferred_element_type=jnp.float32
    ).astype(jnp.bfloat16)
    preconditioned = jnp.einsum(
        "kri,kic->krc", half_step, right_root_new, preferred_element_type=jnp.float32
    ).astype(jnp.bfloat16)
    direction = lax.all_gather(preconditioned, "rep", axis=1, tiled=True)
    return (left_new, right_new, left_root_new, right_root_new, direction)


MESH = pl.DeviceIdType.MESH
LINE = 4
CHUNKS = ((0, 0, 2, True), (0, 1, 2, False), (1, 0, 2, True), (1, 1, 2, False), (2, 0, 2, False), (2, 1, 2, False))
DIRECT = (2,)
PAIRED = ()


def dot(left, right, dims=(1, 0)):
    return lax.dot_general(
        left, right, (((dims[0],), (dims[1],)), ((), ())), preferred_element_type=jnp.float32
    )


def exchange_kernel(
    slots_in,
    refresh_ref,
    grads_ref,
    left_ref,
    left_stat_ref,
    right_stat_ref,
    right_ref,
    left_new_ref,
    right_new_ref,
    direction_ref,
    fresh_rows_ref,
    fresh_right_ref,
    slots_ref,
    arrived,
    mine,
    left_stat,
    right_stat,
    right_full,
    left_full,
    grad_full,
    stat_ref,
    quarter_in,
    stat_full,
    across,
    partial_out,
    from_outer,
    from_inner,
    share,
    incoming,
    turned,
    moment,
    factor,
    current,
    square,
    load_sem,
    across_send,
    across_recv,
    partial_send,
    outer_recv,
    inner_recv,
    swap_send,
    swap_recv,
    part_send,
    part_recv,
    stat_send,
    stat_recv,
    stat_side_send,
    stat_side_recv,
    spread_send,
    spread_recv,
    root_send,
    root_recv,
    root_side_send,
    root_side_recv,
    line_send,
    line_recv,
    side_send,
    side_recv,
):
    blocks, order = arrived.shape[0], arrived.shape[1]
    rows = order // (2 * LINE)
    group = 2 * rows
    shards = stat_ref.shape[0]
    me = lax.axis_index("rep")
    shard = lax.axis_index("shard")
    place = me // 2
    side = me % 2
    other_row = (shard + 2) % shards
    other_core = shard + 1 - 2 * (shard % 2)
    partner = (place * 2 + (1 - side), shard)
    flip = place // (LINE // 2)
    middle = (place == 1) | (place == 2)
    edge = jnp.logical_not(middle)

    def real(position):
        return position + flip * (LINE - 1 - 2 * position)

    def at(position):
        return (real(position) * 2 + side, shard)

    def span(index):
        return pl.ds(pl.multiple_of(index * rows, rows), rows)

    def pair_span(index):
        return pl.ds(pl.multiple_of(index * group, group), group)

    loads = [
        pltpu.make_async_copy(left_stat_ref, left_stat, load_sem.at[0]),
        pltpu.make_async_copy(right_stat_ref, right_stat, load_sem.at[1]),
        pltpu.make_async_copy(grads_ref.at[0], arrived, load_sem.at[2]),
        pltpu.make_async_copy(left_ref, left_full.at[:, span(me), :], load_sem.at[3]),
        pltpu.make_async_copy(right_ref, right_full, load_sem.at[4]),
        pltpu.make_async_copy(slots_in, slots_ref, load_sem.at[5]),
    ]
    barrier = pltpu.get_barrier_semaphore()
    for step in range(1, LINE):
        pl.semaphore_signal(
            barrier,
            inc=1,
            device_id=((place + step) % LINE * 2 + side, shard),
            device_id_type=MESH,
        )
    pl.semaphore_signal(barrier, inc=1, device_id=partner, device_id_type=MESH)
    for step in range(1, shards):
        pl.semaphore_signal(
            barrier, inc=1, device_id=(me, (shard + step) % shards), device_id_type=MESH
        )
    loads[5].start()
    loads[2].start()
    loads[5].wait()
    slot = slots_ref[refresh_ref[0]] % blocks
    keeper = slots_ref[refresh_ref[0]] // blocks
    owns = keeper == shard

    def local(block):
        return (slot + block) % blocks

    loads[2].wait()
    for index in (0, 1, 3):
        loads[index].start()
    mine[0] = arrived[local(0)].reshape(mine.shape[1:])
    pl.semaphore_wait(barrier, LINE - 1 + 1 + shards - 1)

    pending = {"all": [], "edge": [], "middle": []}

    def remote(src, dst, send_sem, recv_sem, device):
        return pltpu.make_async_remote_copy(
            src_ref=src,
            dst_ref=dst,
            send_sem=send_sem,
            recv_sem=recv_sem,
            device_id=device,
            device_id_type=MESH,
        )

    def send(kind, make):
        make().start()
        pending[kind].append(make)

    def drain(kind):
        for make in pending[kind]:
            make().wait_send()
        pending[kind] = []

    def arrive(dst, recv_sem):
        remote(dst, dst, recv_sem, recv_sem, partner).wait_recv()

    def both(on_edge, on_middle):
        pl.when(edge)(on_edge)
        pl.when(middle)(on_middle)

    def cells(chunk):
        block, number, count, _ = CHUNKS[chunk]
        size = rows // count
        return block, pl.ds(number * size, size)

    def span_of(chunk, index):
        block, number, count, _ = CHUNKS[chunk]
        size = rows // count
        first = index * rows + number * size
        return block, pl.ds(pl.multiple_of(first, size), size)

    def across_copy(chunk, target):
        block, here = cells(chunk)
        return remote(
            mine.at[block, target, 1 - side, here],
            across.at[block, target, here],
            across_send.at[chunk, target],
            across_recv.at[chunk, target],
            partner,
        )

    def send_across(kind, chunk, positions):
        if CHUNKS[chunk][0] == blocks - 1:
            send(kind, lambda: across_whole(chunk))
            return
        for position in positions:
            send(kind, lambda p=position: across_copy(chunk, real(p)))

    def across_whole(chunk):
        block, here = cells(chunk)
        return remote(
            mine.at[block, :, 1 - side, here],
            across.at[block, :, here],
            across_send.at[chunk, 0],
            across_recv.at[chunk, 0],
            partner,
        )

    arrived_whole = set()

    def pair_sum(kind, chunk, position):
        target = real(position)
        block, here = cells(chunk)
        if block < blocks - 1:
            arrive(across.at[block, target, here], across_recv.at[chunk, target])
        elif (kind, chunk) not in arrived_whole:
            arrive(across.at[block, :, here], across_recv.at[chunk, 0])
            arrived_whole.add((kind, chunk))
        own = mine[block, target, side, here].astype(jnp.float32)
        return own + across[block, target, here].astype(jnp.float32)

    def wait_outer(chunk, number):
        block, here = cells(chunk)
        arrive(from_outer.at[block, number, here], outer_recv.at[chunk, number])
        return from_outer[block, number, here]

    def wait_inner(chunk, number):
        block, here = cells(chunk)
        arrive(from_inner.at[block, number, here], inner_recv.at[chunk, number])
        return from_inner[block, number, here]

    def edge_far(chunk, position):
        number = position - 1
        block, here = cells(chunk)
        partial_out[block, number, here] = pair_sum("edge", chunk, position)
        send(
            "edge",
            lambda: remote(
                partial_out.at[block, number, here],
                from_outer.at[block, number, here],
                partial_send.at[chunk, number],
                outer_recv.at[chunk, number],
                at(1),
            ),
        )

    def middle_far(chunk, position):
        number = {3: 0, 2: 1, 0: 2, 1: 3}[position]
        block, here = cells(chunk)
        if position < 2:
            earlier = wait_inner(chunk, position)
            goal, landing = 0, position
        else:
            earlier = wait_outer(chunk, position - 1)
            goal, landing = 2, number
        partial_out[block, number, here] = pair_sum("middle", chunk, position) + earlier
        send(
            "middle",
            lambda: remote(
                partial_out.at[block, number, here],
                from_inner.at[block, landing, here],
                partial_send.at[chunk, number],
                inner_recv.at[chunk, landing],
                at(goal),
            ),
        )

    def swap_rows(chunk, owner):
        block, here = cells(chunk)
        return incoming.at[block, owner, groups(chunk), here]

    def at_ends(chunk):
        return CHUNKS[chunk][3]

    def groups(chunk):
        return slice(None) if at_ends(chunk) else 0

    others = ((other_core + 2) % shards, other_row, other_core)

    def swap(kind, chunk, *totals):
        block, here = cells(chunk)
        for number, total in enumerate(totals):
            value = total.astype(jnp.bfloat16)
            share[block, number, here] = value
            incoming[block, shard, number, here] = value
        for number, goal in enumerate(others):
            send(
                kind,
                lambda n=number, g=goal: remote(
                    share.at[block, groups(chunk), here],
                    swap_rows(chunk, shard),
                    swap_send.at[chunk, n],
                    swap_recv.at[chunk, n],
                    (me, g),
                ),
            )

    def edge_own(chunk):
        positions = (0, 1) if at_ends(chunk) else (0,)
        swap("edge", chunk, *(pair_sum("edge", chunk, p) + wait_inner(chunk, p) for p in positions))

    def middle_own(chunk):
        total = pair_sum("middle", chunk, 1) + wait_inner(chunk, 1)
        swap("middle", chunk, total + wait_outer(chunk, 0))

    def share_rows(chunk, source, which):
        block, here = cells(chunk)
        if at_ends(chunk):
            half = LINE // 2
            return grad_full.at[block, pl.ds(source // half * half, half), which, here]
        return grad_full.at[block, source, which, here]

    def side_copy(chunk, source):
        where = share_rows(chunk, source, side)
        return remote(
            where, where, side_send.at[chunk, source], side_recv.at[chunk, source], partner
        )

    def wait_side(chunk, source):
        arrive(share_rows(chunk, source, 1 - side), side_recv.at[chunk, source])

    def line_rows(chunk, position):
        if CHUNKS[chunk][0] in PAIRED and position in (1, 2):
            return share_rows(chunk, real(position), slice(None))
        return share_rows(chunk, real(position), side)

    def line_copy(chunk, position, way, goal):
        where = line_rows(chunk, position)
        return remote(
            where,
            where,
            line_send.at[chunk, real(position), way],
            line_recv.at[chunk, real(position)],
            at(goal),
        )

    def take(kind, chunk):
        for number, origin in enumerate(others):
            arrive(swap_rows(chunk, origin), swap_recv.at[chunk, number])
        block, here = cells(chunk)
        wanted = shard * blocks + local(block)
        for number in range(2 if at_ends(chunk) else 1):
            value = incoming[block, 0, number, here]
            for origin in range(1, shards):
                held = slots_ref[origin * blocks + local(block)] == wanted
                value = jnp.where(held, incoming[block, origin, number, here], value)
            group_place = real(number) if at_ends(chunk) else place
            grad_full[block, group_place, side, here] = value
        paired = block in PAIRED and kind == "middle"
        if not paired:
            line_begin(kind, chunk)
        send(kind, lambda: side_copy(chunk, place))
        if block in DIRECT:
            own, near, far = (0, 1, (2, 3)) if kind == "edge" else (1, 2, (3,))
            for way, goal in enumerate(far):
                send(kind, lambda w=way, g=goal: line_copy(chunk, own, near + w, g))

    def line_begin(kind, chunk):
        if CHUNKS[chunk][0] in PAIRED and kind == "middle":
            wait_side(chunk, place)
        if kind == "edge":
            send(kind, lambda: line_copy(chunk, 0, 0, 1))
        else:
            send(kind, lambda: line_copy(chunk, 1, 0, 0))
            send(kind, lambda: line_copy(chunk, 1, 1, 2))

    def wait_line(chunk, position):
        arrive(line_rows(chunk, position), line_recv.at[chunk, real(position)])

    def line_next(kind, chunk, position):
        block = CHUNKS[chunk][0]
        wait_line(chunk, position)
        if kind == "middle" and block not in DIRECT:
            goal = 2 if position == 0 else 0
            send(kind, lambda: line_copy(chunk, position, 0, goal))
        if block not in PAIRED or position in (0, 3):
            send(kind, lambda: side_copy(chunk, real(position)))

    def gathered(kind, block):
        if block == blocks - 1:
            for make in pending["all"]:
                make().wait_send()
            drain(kind)
        for chunk, entry in enumerate(CHUNKS):
            if entry[0] != block:
                continue
            paired = block in PAIRED
            if paired and kind == "edge":
                wait_line(chunk, 1)
                wait_line(chunk, 2)
            for position in (0, 3) if paired or entry[3] else range(LINE):
                wait_side(chunk, real(position))

    pieces = {
        "edge": ((1, 1, 3), (2, 2, 2), (3, 3, 1)),
        "middle": ((0, 0, 1), (0, 3, 1), (2, 2, 2), (2, 0, 1), (3, 3, 1)),
    }

    def columns(first, count):
        return pl.ds(
            pl.multiple_of((first + flip * (LINE - 2 * first - count)) * group, group),
            count * group,
        )

    def root_piece(piece, which):
        position, first, count = piece
        return left_full.at[:, span(real(position) * 2 + which), columns(first, count)]

    def send_root(kind, number, piece, goal, landing):
        send(
            kind,
            lambda: remote(
                root_piece(piece, side),
                root_piece(piece, side),
                root_send.at[number],
                root_recv.at[landing],
                at(goal),
            ),
        )

    def wait_root(kind, number):
        arrive(root_piece(pieces[kind][number], side), root_recv.at[number])

    def edge_roots():
        send_root("edge", 0, (0, 0, 1), 1, 0)
        send_root("edge", 1, (0, 3, 1), 1, 1)

    def middle_roots():
        send_root("middle", 0, (1, 0, 2), 2, 2)
        send_root("middle", 1, (1, 1, 3), 0, 0)
        send_root("middle", 2, (1, 3, 1), 2, 3)

    def middle_root(number):
        wait_root("middle", number)
        if number == 0:
            send_root("middle", 3, (0, 0, 1), 2, 4)
        if number == 2:
            send_root("middle", 4, (2, 2, 2), 0, 1)
        if number == 4:
            send_root("middle", 5, (3, 3, 1), 0, 2)
        if number == 1:
            wait_root("middle", 3)

    def edge_roots_next():
        for number in range(3):
            wait_root("edge", number)

    def root_side(kind, number):
        def make():
            if number == 0:
                where = left_full.at[:, span(me), :]
            else:
                where = root_piece(pieces[kind][number - 1], side)
            return remote(
                where, where, root_side_send.at[number], root_side_recv.at[number], partner
            )

        return make

    def wait_root_side(kind):
        arrive(left_full.at[:, span(place * 2 + 1 - side), :], root_side_recv.at[0])
        for number, piece in enumerate(pieces[kind]):
            arrive(root_piece(piece, 1 - side), root_side_recv.at[number + 1])

    def mirror(kind):
        tiles = [(1, 2), (1, 3), (2, 3)]
        if kind == "edge":
            tiles += [(0, 1), (0, 2), (0, 3)]
        else:
            tiles += [(1, 0), (2, 0), (0, 3)]
        for block in range(blocks):
            for row, column in tiles:
                value = left_full[block, pair_span(real(row)), columns(column, 1)]
                left_full[block, pair_span(real(column)), columns(row, 1)] = value.T

    def to_shards(step):
        peer = (shard + step) % shards
        return remote(
            stat_ref.at[peer],
            quarter_in.at[shard],
            part_send.at[step],
            part_recv.at[step],
            (me, peer),
        )

    def stat_side():
        where = stat_full.at[:, me, shard]
        return remote(where, where, stat_side_send.at[0], stat_side_recv.at[0], partner)

    def stat_rows(position):
        return stat_full.at[:, pl.ds(real(position) * 2, 2), shard]

    def stat_copy(position, way, goal):
        where = stat_rows(position)
        return remote(
            where,
            where,
            stat_send.at[real(position), way],
            stat_recv.at[real(position)],
            at(goal),
        )

    def wait_stat(position):
        arrive(stat_rows(position), stat_recv.at[real(position)])

    def send_quarters(kind):
        for step in range(1, shards):
            origin = (shard + shards - step) % shards
            arrive(quarter_in.at[origin], part_recv.at[step])
        stat_full[:, me, shard] = quarter_in[keeper]
        send(kind, stat_side)

    def stat_begin(kind):
        arrive(stat_full.at[:, place * 2 + (1 - side), shard], stat_side_recv.at[0])
        if kind == "edge":
            send(kind, lambda: stat_copy(0, 0, 1))
        else:
            send(kind, lambda: stat_copy(1, 0, 0))
            send(kind, lambda: stat_copy(1, 1, 2))

    def stat_next(position):
        wait_stat(position)
        goal = 2 if position == 0 else 0
        send("middle", lambda: stat_copy(position, 0, goal))

    def spread(number, owner, goal):
        where = stat_full.at[:, :, owner]
        return remote(
            where, where, spread_send.at[number], spread_recv.at[number], (me, goal)
        )

    def spread_quarters(kind):
        if kind == "edge":
            for position in (1, 2, 3):
                wait_stat(position)
        send(kind, lambda: spread(0, shard, other_row))
        send(kind, lambda: spread(1, shard, other_core))

    def spread_next(kind):
        arrive(stat_full.at[:, :, other_row], spread_recv.at[0])
        send(kind, lambda: spread(2, other_row, other_core))

    def spread_end():
        arrive(stat_full.at[:, :, other_core], spread_recv.at[1])
        arrive(
            stat_full.at[:, :, (other_core + 2) % shards], spread_recv.at[2]
        )

    tile = pair_span(place)

    def new_statistics(block):
        grad = grad_full[block].reshape(order, order)
        own = grad_full[block, place, side]
        left_new_ref[block] = decay_rate * left_stat[local(block)] + dot(own, grad, (1, 1)) / order
        turned_rows = grad_full[block, :, :, :, tile].reshape(order, group).T
        own_turned = jnp.where(side == 0, turned_rows[:rows], turned_rows[rows:])
        right_new_ref[block] = decay_rate * right_stat[local(block)] + dot(own_turned, grad) / order

    def renew_begin(which):
        identity = (
            lax.broadcasted_iota(jnp.int32, (order, order), 0)
            == lax.broadcasted_iota(jnp.int32, (order, order), 1)
        ).astype(jnp.float32)
        grad = grad_full[0].reshape(order, order)
        if which == 0:
            turned[...] = grad.T
            product = dot(grad, turned[...])
        else:
            product = dot(turned[...], grad)
        old = stat_full[which].reshape(order, order).astype(jnp.float32)
        shifted = decay_rate * old + product / order + epsilon_shift * identity
        scale = 2.5 / jnp.sqrt(jnp.sum(shifted * shifted))
        start = scale * shifted
        moment[which] = start.astype(jnp.bfloat16)
        step = (5.0 * identity - start) * 0.25
        factor[which] = step.astype(jnp.bfloat16)
        current[which] = (jnp.sqrt(jnp.sqrt(scale)) * step).astype(jnp.bfloat16)

    def renew_square():
        for which in range(2):
            square[which] = dot(factor[which], factor[which]).astype(jnp.bfloat16)

    def renew_fourth():
        for which in range(2):
            factor[which] = dot(square[which], square[which]).astype(jnp.bfloat16)

    def renew_factor():
        identity = (
            lax.broadcasted_iota(jnp.int32, (order, order), 0)
            == lax.broadcasted_iota(jnp.int32, (order, order), 1)
        ).astype(jnp.float32)
        for which in range(2):
            value = dot(factor[which], moment[which])
            square[which] = ((5.0 * identity - value) * 0.25).astype(jnp.bfloat16)

    def renew_end():
        moment[0] = dot(current[0], square[0]).astype(jnp.bfloat16)
        fresh_right_ref[...] = dot(current[1], square[1]).astype(jnp.bfloat16)
        fresh_rows_ref[...] = moment[0, span(me), :]

    def direct(block):
        root = left_full[local(block)]
        other = right_full[local(block)]
        if block == 0:
            root = jnp.where(owns, moment[0], root)
            other = jnp.where(owns, fresh_right_ref[...], other)
        half = dot(root, grad_full[block].reshape(order, order)).astype(jnp.bfloat16)
        direction_ref[block] = dot(half, other).astype(jnp.bfloat16)

    @pl.when(edge)
    def _():
        send_across("edge", 0, (3, 2, 1, 0))
        send_across("edge", 1, (3, 2, 1, 0))

    @pl.when(middle)
    def _():
        send_across("middle", 1, (3, 2, 0, 1))
        send_across("middle", 0, (3, 2, 0, 1))
    for block in range(1, blocks):
        mine[block] = arrived[local(block)].reshape(mine.shape[1:])
    loads[0].wait()
    loads[1].wait()
    part = rows // shards
    for index in range(shards):
        part_rows = pl.ds(index * part, part)
        stat_ref[index, 0] = left_stat[slot, part_rows, :].astype(jnp.bfloat16)
        stat_ref[index, 1] = right_stat[slot, part_rows, :].astype(jnp.bfloat16)
    for step in range(1, shards):
        send("all", lambda step=step: to_shards(step))
    quarter_in[shard] = stat_ref[shard]
    loads[3].wait()
    loads[4].start()

    @pl.when(edge)
    def _():
        edge_roots()
        edge_far(0, 3)
        send_across("edge", 2, (3, 2, 1, 0))
        edge_far(0, 2)
        send_across("edge", 3, (3, 2, 1, 0))
        edge_far(1, 3)
        edge_far(1, 2)
        send_quarters("edge")
        edge_far(2, 3)
        send_across("edge", 4, (3, 2, 1, 0))
        edge_far(2, 2)
        edge_far(3, 3)
        send_across("edge", 5, (3, 2, 1, 0))
        edge_far(1, 1)
        edge_far(3, 2)
        stat_begin("edge")
        edge_far(4, 3)
        edge_own(0)
        edge_roots_next()
        edge_far(3, 1)
        send("edge", root_side("edge", 0))
        edge_far(5, 2)
        edge_far(5, 3)
        edge_own(1)
        send("edge", root_side("edge", 2))
        take("edge", 0)
        edge_own(2)
        take("edge", 1)
        send("edge", root_side("edge", 1))
        edge_own(3)
        send("edge", root_side("edge", 3))
        edge_far(5, 1)
        edge_far(4, 2)
        spread_quarters("edge")
        line_next("edge", 1, 1)
        take("edge", 2)
        take("edge", 3)
        line_next("edge", 3, 1)
        edge_far(4, 1)
        line_next("edge", 1, 2)
        edge_own(5)
        edge_own(4)
        wait_root_side("edge")
        line_next("edge", 0, 3)
        line_next("edge", 1, 3)
        line_next("edge", 3, 2)
        spread_next("edge")
        mirror("edge")
        take("edge", 5)
        line_next("edge", 5, 1)
        spread_end()
        take("edge", 4)
        gathered("edge", 0)

    @pl.when(middle)
    def _():
        middle_roots()
        middle_root(0)
        send_quarters("middle")
        middle_root(2)
        middle_root(1)
        middle_far(0, 3)
        send_across("middle", 2, (3, 2, 0, 1))
        middle_far(0, 2)
        middle_root(4)
        stat_begin("middle")
        send_across("middle", 3, (3, 2, 0, 1))
        middle_far(1, 3)
        middle_far(0, 0)
        middle_far(1, 2)
        middle_far(0, 1)
        middle_far(2, 3)
        send_across("middle", 4, (3, 2, 0, 1))
        stat_next(2)
        send_across("middle", 5, (3, 2, 0, 1))
        middle_far(2, 2)
        send("middle", root_side("middle", 5))
        middle_far(3, 3)
        middle_far(1, 0)
        middle_own(1)
        middle_far(2, 0)
        send("middle", root_side("middle", 1))
        middle_far(3, 2)
        middle_far(2, 1)
        stat_next(0)
        middle_far(3, 0)
        take("middle", 1)
        middle_far(4, 3)
        send("middle", root_side("middle", 0))
        middle_own(3)
        stat_next(3)
        middle_far(5, 2)
        spread_quarters("middle")
        middle_far(5, 3)
        line_next("middle", 1, 2)
        middle_far(4, 0)
        line_next("middle", 0, 0)
        line_next("middle", 1, 0)
        take("middle", 3)
        send("middle", root_side("middle", 3))
        middle_far(5, 0)
        middle_own(5)
        line_next("middle", 0, 3)
        middle_far(4, 2)
        line_next("middle", 1, 3)
        send("middle", root_side("middle", 4))
        line_next("middle", 3, 2)
        line_next("middle", 2, 0)
        line_next("middle", 3, 0)
        take("middle", 5)
        spread_next("middle")
        middle_own(4)
        send("middle", root_side("middle", 2))
        line_next("middle", 2, 3)
        spread_end()
        gathered("middle", 0)
        line_next("middle", 3, 3)

    renew_begin(0)
    @pl.when(edge)
    def _():
        line_next("edge", 2, 3)

    renew_begin(1)
    @pl.when(edge)
    def _():
        line_next("edge", 5, 2)

    renew_square()
    @pl.when(edge)
    def _():
        line_next("edge", 3, 3)
        line_next("edge", 5, 3)

    @pl.when(middle)
    def _():
        take("middle", 4)
        line_next("middle", 5, 0)

    renew_fourth()
    @pl.when(middle)
    def _():
        line_next("middle", 5, 3)

    renew_factor()
    @pl.when(edge)
    def _():
        line_next("edge", 4, 1)
        line_next("edge", 4, 3)

    @pl.when(middle)
    def _():
        wait_root_side("middle")
        line_next("middle", 4, 0)
        mirror("middle")
        gathered("middle", 1)

    renew_end()
    @pl.when(edge)
    def _():
        line_next("edge", 4, 2)

    @pl.when(middle)
    def _():
        line_next("middle", 4, 2)
        line_next("middle", 5, 2)

    loads[4].wait()
    direct(0)
    @pl.when(edge)
    def _():
        gathered("edge", 1)

    @pl.when(middle)
    def _():
        line_next("middle", 4, 3)

    new_statistics(1)
    new_statistics(0)
    direct(1)
    @pl.when(edge)
    def _():
        gathered("edge", 2)

    @pl.when(middle)
    def _():
        gathered("middle", 2)

    new_statistics(2)
    direct(2)
    both(lambda: drain("edge"), lambda: drain("middle"))


def exchange(owner_slot, refresh, grads, left_root, left_stat, right_stat, right_root, shards):
    blocks, order = grads.shape[1], grads.shape[2]
    reps = 2 * LINE
    rows = order // reps
    part = rows // shards
    chunks = len(CHUNKS)
    low = jnp.bfloat16
    wide = jnp.float32
    smem = pl.BlockSpec(memory_space=pltpu.SMEM)
    hbm = pl.BlockSpec(memory_space=pltpu.HBM)
    dma = pltpu.SemaphoreType.DMA
    return pl.pallas_call(
        exchange_kernel,
        out_shape=(
            jax.ShapeDtypeStruct((blocks, rows, order), wide),
            jax.ShapeDtypeStruct((blocks, rows, order), wide),
            jax.ShapeDtypeStruct((blocks, order, order), low),
            jax.ShapeDtypeStruct((rows, order), low),
            jax.ShapeDtypeStruct((order, order), low),
        ),
        in_specs=[hbm, smem] + [hbm] * 5,
        out_specs=(pl.BlockSpec(memory_space=pltpu.VMEM),) * 5,
        scratch_shapes=[
            pltpu.SMEM(owner_slot.shape, owner_slot.dtype),
            pltpu.VMEM((blocks, order, order), low),
            pltpu.VMEM((blocks, LINE, 2, rows, order), low),
            pltpu.VMEM((blocks, rows, order), wide),
            pltpu.VMEM((blocks, rows, order), wide),
            pltpu.VMEM((blocks, order, order), low),
            pltpu.VMEM((blocks, order, order), low),
            pltpu.VMEM((blocks, LINE, 2, rows, order), low),
            pltpu.VMEM((shards, 2, part, order), low),
            pltpu.VMEM((shards, 2, part, order), low),
            pltpu.VMEM((2, reps, shards, part, order), low),
            pltpu.VMEM((blocks, LINE, rows, order), low),
            pltpu.VMEM((blocks, LINE, rows, order), wide),
            pltpu.VMEM((blocks, 3, rows, order), wide),
            pltpu.VMEM((blocks, 2, rows, order), wide),
            pltpu.VMEM((blocks, 2, rows, order), low),
            pltpu.VMEM((blocks, shards, 2, rows, order), low),
            pltpu.VMEM((order, order), low),
            pltpu.VMEM((2, order, order), low),
            pltpu.VMEM((2, order, order), low),
            pltpu.VMEM((2, order, order), low),
            pltpu.VMEM((2, order, order), low),
            dma((6,)),
            dma((chunks, LINE)),
            dma((chunks, LINE)),
            dma((chunks, LINE)),
            dma((chunks, 3)),
            dma((chunks, 2)),
            dma((chunks, 3)),
            dma((chunks, 3)),
            dma((shards,)),
            dma((shards,)),
            dma((LINE, 2)),
            dma((LINE,)),
            dma((1,)),
            dma((1,)),
            dma((3,)),
            dma((3,)),
            dma((6,)),
            dma((5,)),
            dma((6,)),
            dma((6,)),
            dma((chunks, LINE, 3)),
            dma((chunks, LINE)),
            dma((chunks, LINE)),
            dma((chunks, LINE)),
        ],
        compiler_params=pltpu.CompilerParams(
            collective_id=0, has_side_effects=True, vmem_limit_bytes=48 * 2**20
        ),
    )(
        fixed(owner_slot),
        refresh,
        *map(fixed, (grads, left_root, left_stat, right_stat, right_root)),
    )


def fixed(array):
    return pltpu.with_memory_space_constraint(array, pltpu.HBM)


def arrange_kernel(
    slots_ref,
    refresh_ref,
    left_in,
    right_in,
    direction_in,
    fresh_rows,
    fresh_right,
    left_root,
    right_root,
    left_new,
    right_new,
    left_root_new,
    right_root_new,
    direction,
    sems,
):
    blocks = left_in.shape[0]
    fresh_slot = slots_ref[refresh_ref[0]]
    slot = fresh_slot % blocks
    owns = fresh_slot // blocks == lax.axis_index("shard")
    copies = []

    def copy(source, target):
        copies.append(pltpu.make_async_copy(source, target, sems.at[len(copies)]))
        copies[-1].start()

    for block in range(blocks):
        where = (slot + block) % blocks
        copy(direction_in.at[block], direction.at[where])
        copy(left_in.at[block], left_new.at[where])
        copy(right_in.at[block], right_new.at[where])
        if block > 0:
            copy(right_root.at[where], right_root_new.at[where])
            copy(left_root.at[where], left_root_new.at[where])
    last = len(copies)

    @pl.when(owns)
    def _():
        pltpu.make_async_copy(fresh_right, right_root_new.at[slot], sems.at[last]).start()
        pltpu.make_async_copy(fresh_rows, left_root_new.at[slot], sems.at[last + 1]).start()

    @pl.when(jnp.logical_not(owns))
    def _():
        pltpu.make_async_copy(
            right_root.at[slot], right_root_new.at[slot], sems.at[last]
        ).start()
        pltpu.make_async_copy(
            left_root.at[slot], left_root_new.at[slot], sems.at[last + 1]
        ).start()

    pltpu.make_async_copy(fresh_right, right_root_new.at[slot], sems.at[last]).wait()
    pltpu.make_async_copy(fresh_rows, left_root_new.at[slot], sems.at[last + 1]).wait()
    for item in copies:
        item.wait()


def arrange(*operands):
    stat, root, right = operands[2], operands[7], operands[8]
    smem = pl.BlockSpec(memory_space=pltpu.SMEM)
    hbm = pl.BlockSpec(memory_space=pl.ANY)
    return pl.pallas_call(
        arrange_kernel,
        out_shape=(
            jax.ShapeDtypeStruct(stat.shape, stat.dtype),
            jax.ShapeDtypeStruct(stat.shape, stat.dtype),
            jax.ShapeDtypeStruct(root.shape, root.dtype),
            jax.ShapeDtypeStruct(right.shape, right.dtype),
            jax.ShapeDtypeStruct(right.shape, right.dtype),
        ),
        in_specs=[smem, smem] + [hbm] * 7,
        out_specs=(hbm,) * 5,
        scratch_shapes=[pltpu.SemaphoreType.DMA((5 * stat.shape[0],))],
        compiler_params=pltpu.CompilerParams(vmem_limit_bytes=2**20),
    )(*operands)


def direct_body(grads, owner_slot, refresh, left_stat, right_stat, left_root, right_root):
    results = exchange(
        owner_slot,
        refresh,
        grads,
        left_root,
        left_stat,
        right_stat,
        right_root,
        lax.axis_size("shard"),
    )
    return arrange(owner_slot, refresh, *results, left_root, right_root)


def choose(mesh, *arrays):
    reps, shards = mesh.shape["rep"], mesh.shape["shard"]
    rows = arrays[0].shape[2] // reps
    blocks = arrays[0].shape[1] // shards
    finest = 16 * max(shards, *(entry[2] for entry in CHUNKS))
    direct = (reps, shards, blocks) == (2 * LINE, 4, 3) and rows % finest == 0
    return direct_body if direct else body


def solution(mesh):
    def run(*arrays):
        return mapped(mesh, choose(mesh, *arrays))(*arrays)

    return run


def mapped(mesh, body):
    return jax.shard_map(
        body,
        mesh=mesh,
        in_specs=(
            P("rep", "shard", None, None),
            P(),
            P(),
            P("shard", "rep", None),
            P("shard", "rep", None),
            P("shard", "rep", None),
            P("shard", None, None),
        ),
        out_specs=(
            P("shard", "rep", None),
            P("shard", "rep", None),
            P("shard", "rep", None),
            P("shard", None, None),
            P("shard", None, None),
        ),
        check_vma=False,
    )
```
